32 devices in a mesh: frame: 16 (over z, y, core), row: 2 (over x).
Axes of the slice: x: 2, y: 2, z: 4, core: 2. Of those that a mesh axis runs over, the one named last changes fastest.
Arguments:
- spatial_q: bfloat16 [16, 256, 3072], P('frame', 'row'), may hold values from -6 to 6
- spatial_k: bfloat16 [16, 256, 3072], P('frame', 'row'), may hold values from -6 to 6
- spatial_v: bfloat16 [16, 256, 3072], P('frame', 'row'), may hold values from -6 to 6
- norm_gain: float32 [3072], replicated, may hold values from 0.5 to 1.5
- temporal_weight: bfloat16 [3072, 3, 3072], P(None, None, 'row'), may hold values from -0.625 to 0.625
Outputs:
- temporal_out: bfloat16 [16, 256, 3072], P('frame', 'row')
The draws below stay inside these ranges and needn't reach their ends.
All inputs are finite; a program needn't handle non-finite values.
Results may differ from the reference program's by a relative error of at most 0.0083.
Values may be sent and summed in bfloat16 or wider, within the bound.
No kernel may reach another device: no remote copies, remote signals or barrier semaphores. Data moves between devices by JAX's collectives and lax.ppermute only.
A program may use at most 64 MiB of HBM per device.

```python
from functools import partial
import jax
import jax.numpy as jnp
from jax import lax

D = 3072
HEADS = 24
AGENTS = 128
TOK_DEV = 128
FRAMES = 16
TOK_FRAME = 256


def spatial_pair(key):
    shape = (FRAMES, TOK_FRAME, D)
    subkeys = jax.random.split(jax.random.fold_in(key, 71), 2)
    queries = jnp.clip(jax.random.normal(subkeys[0], shape, jnp.float32), -5.9, 5.9)
    keys_out = jnp.clip(jax.random.normal(subkeys[1], shape, jnp.float32), -5.9, 5.9)
    return (queries.astype(jnp.bfloat16), keys_out.astype(jnp.bfloat16))


def draw_spatial_q(key, part):
    return spatial_pair(key)[0]


def draw_spatial_k(key, part):
    return spatial_pair(key)[1]


def draw_temporal_weight(key, part):
    subkeys = jax.random.split(jax.random.fold_in(key, 53), 1)
    base = jax.random.normal(subkeys[0], (D, 3, D), jnp.float32) / jnp.sqrt(jnp.float32(D))
    return jnp.clip(base, -0.625, 0.625).astype(jnp.bfloat16)


def block_scale(own_key, extent, pieces, smallest, top_value):
    def one(axis_at, shards_of):
        heights = jax.random.uniform(jax.random.fold_in(jax.random.fold_in(own_key, 6), axis_at), (shards_of,), jnp.float32, smallest / len(pieces), top_value / len(pieces))
        return jnp.repeat(jnp.exp(heights), extent[axis_at] // shards_of).reshape((-1,) + (1,) * (len(extent) - axis_at - 1))

    loudness = one(*pieces[0])
    for cut in pieces[1:]:
        loudness = loudness * one(*cut)
    return loudness


def noise(rng, extent, deviation, limit, cuts=(), held_as=jnp.bfloat16):
    drawn = deviation * jax.random.normal(rng, extent, jnp.float32)
    if cuts:
        drawn = drawn * block_scale(rng, extent, cuts, -0.22, 0.18)
    return jnp.clip(drawn, -limit, limit).astype(held_as)


def setup_inputs(seed: int = 0) -> dict:
    arg_keys = jax.random.split(jax.random.key(seed), 6)
    spatial_q = draw_spatial_q(jax.random.fold_in(arg_keys[5], 71), 0)
    spatial_k = draw_spatial_k(jax.random.fold_in(arg_keys[5], 71), 0)
    spatial_v = noise(arg_keys[2], (FRAMES, TOK_FRAME, D), 1.0, 6.0, ((0, 16), (1, 2)))
    norm_gain = jnp.clip(1.0 + 0.1 * jax.random.normal(arg_keys[3], (D,), jnp.float32), 0.5, 1.5)
    temporal_weight = draw_temporal_weight(jax.random.fold_in(arg_keys[5], 71), 0)
    return {"spatial_q": spatial_q, "spatial_k": spatial_k, "spatial_v": spatial_v, "norm_gain": norm_gain, "temporal_weight": temporal_weight}


epsilon = 1e-06

def rounded(values):
    return lax.optimization_barrier(values.astype(jnp.bfloat16)).astype(jnp.float32)

def spatial_frame(gain, operands):
    queries, keys_in, values_in = operands
    head_size = D // HEADS
    scale = head_size ** (-0.5)
    pool_size = TOK_FRAME // AGENTS
    agents = lax.optimization_barrier(jnp.mean(queries.reshape(AGENTS, pool_size, D), axis=1, dtype=jnp.float32)).astype(jnp.bfloat16)
    query_heads = queries.astype(jnp.float32).reshape(TOK_FRAME, HEADS, head_size)
    key_heads = keys_in.astype(jnp.float32).reshape(TOK_FRAME, HEADS, head_size)
    value_heads = values_in.astype(jnp.float32).reshape(TOK_FRAME, HEADS, head_size)
    agent_heads = agents.astype(jnp.float32).reshape(AGENTS, HEADS, head_size)
    agent_scores = jnp.einsum('ahd,thd->hat', agent_heads, key_heads) * scale
    peak = lax.optimization_barrier(jnp.max(agent_scores, axis=-1, keepdims=True))
    agent_weights = jnp.exp(agent_scores - peak)
    agent_totals = lax.optimization_barrier(jnp.sum(agent_weights, axis=-1))
    agent_numer = jnp.einsum('hat,thd->had', rounded(agent_weights), value_heads)
    agent_values = rounded(agent_numer / agent_totals[:, :, None])
    token_scores = jnp.einsum('thd,ahd->hta', query_heads, agent_heads) * scale
    token_weights = rounded(jax.nn.softmax(token_scores, axis=-1))
    spatial_out = jnp.einsum('hta,had->thd', token_weights, agent_values).reshape(TOK_FRAME, D)
    mean_square = lax.optimization_barrier(jnp.mean(spatial_out * spatial_out, axis=-1, keepdims=True))
    return (spatial_out * lax.rsqrt(mean_square + epsilon) * gain).astype(jnp.bfloat16)

def temporal_block(weight_matrix, block):
    head_size = D // HEADS
    scale = head_size ** (-0.5)
    locations = block.shape[1]
    projected = jnp.dot(block.reshape(-1, D), weight_matrix, preferred_element_type=jnp.float32)
    qkv = rounded(projected).reshape(FRAMES, locations, 3, HEADS, head_size)
    scores = jnp.einsum('flhd,glhd->lhfg', qkv[:, :, 0], qkv[:, :, 1]) * scale
    weights = rounded(jax.nn.softmax(scores, axis=-1))
    result = jnp.einsum('lhfg,glhd->flhd', weights, qkv[:, :, 2])
    return result.reshape(FRAMES, locations, D).astype(jnp.bfloat16)

def reference(spatial_q, spatial_k, spatial_v, norm_gain, temporal_weight):
    normed = lax.map(partial(spatial_frame, norm_gain), (spatial_q, spatial_k, spatial_v))
    block_count = TOK_FRAME // TOK_DEV
    blocks = normed.reshape(FRAMES, block_count, TOK_DEV, D).transpose(1, 0, 2, 3)
    outputs = lax.map(partial(temporal_block, temporal_weight.reshape(D, 3 * D)), blocks)
    return outputs.transpose(1, 0, 2, 3).reshape(FRAMES, TOK_FRAME, D)
```

```python
import math
from functools import partial

import jax
import jax.numpy as jnp
from jax import lax
from jax.experimental import pallas as pl
from jax.experimental.pallas import tpu as pltpu
from jax.sharding import PartitionSpec as P

D = 3072
HEADS = 24
AGENTS = 128
HEAD = D // HEADS
SCALE = HEAD ** (-0.5)

epsilon = 1e-06


def dot(left, right):
    return jnp.dot(left, right, preferred_element_type=jnp.float32)


def dot_nt(left, right):
    return lax.dot_general(
        left, right, (((1,), (1,)), ((), ())), preferred_element_type=jnp.float32
    )


def spatial_kernel(base, q, k, v, *rest, heads, pool, tiled):
    received, gain, out = rest[:-2], rest[-2], rest[-1]
    ways = len(received) + 1
    tokens = q.shape[1]
    agent = lax.broadcasted_iota(jnp.int32, (tokens // pool, tokens), 0)
    token = lax.broadcasted_iota(jnp.int32, (tokens // pool, tokens), 1)
    member = ((token >= agent * pool) & (token < (agent + 1) * pool)).astype(jnp.bfloat16)
    for h in range(heads):
        cols = slice(h * HEAD, (h + 1) * HEAD)
        blocks = [q[0, :, cols]] + [ref[0, :, cols] for ref in received]
        agents = jnp.concatenate([dot(member, block) for block in blocks]) * (1.0 / pool)
        agents = agents.astype(jnp.bfloat16)
        queries = jnp.concatenate(blocks)
        keys = jnp.concatenate([k[0, :, cols]] + [ref[1, :, cols] for ref in received])
        values = jnp.concatenate([v[0, :, cols]] + [ref[2, :, cols] for ref in received])
        scores = dot_nt(agents, keys) * SCALE
        weights = jnp.exp(scores - jnp.max(scores, axis=1, keepdims=True))
        totals = jnp.sum(weights, axis=1, keepdims=True)
        agent_values = (dot(weights.astype(jnp.bfloat16), values) / totals).astype(jnp.bfloat16)
        scores = dot_nt(queries, agents) * SCALE
        weights = jnp.exp(scores - jnp.max(scores, axis=1, keepdims=True))
        weights = weights / jnp.sum(weights, axis=1, keepdims=True)
        result = dot(weights.astype(jnp.bfloat16), agent_values)
        result = (result * gain[:, cols]).astype(jnp.bfloat16)
        for j in range(ways):
            block = result[j * tokens : (j + 1) * tokens]
            if tiled:
                out[:, j, :, cols] = block.reshape(out.shape[0], out.shape[2], HEAD)
            else:
                out[j, :, cols] = block


def spatial(q, k, v, received, gain, base, frames, width, heads):
    tokens = q.shape[1]
    ways = len(received) + 1
    slot = tokens // frames
    pool = tokens * ways // AGENTS
    step = heads * HEAD
    tiled = slot % 8 == 0
    own = pl.BlockSpec((1, tokens, step), lambda i, base: (0, 0, base[0] // heads + i))
    other = pl.BlockSpec((3, tokens, step), lambda i, base: (0, 0, i))
    if tiled:
        shape = (frames, ways, slot, width)
        out_spec = pl.BlockSpec((frames, ways, slot, step), lambda i, base: (0, 0, 0, i))
    else:
        shape = (ways, tokens, width)
        out_spec = pl.BlockSpec((ways, tokens, step), lambda i, base: (0, 0, i))
    out = pl.pallas_call(
        partial(spatial_kernel, heads=heads, pool=pool, tiled=tiled),
        out_shape=jax.ShapeDtypeStruct(shape, jnp.bfloat16),
        grid_spec=pltpu.PrefetchScalarGridSpec(
            num_scalar_prefetch=1,
            grid=(width // step,),
            in_specs=[own] * 3
            + [other] * len(received)
            + [pl.BlockSpec((1, step), lambda i, base: (0, base[0] // heads + i))],
            out_specs=out_spec,
        ),
        cost_estimate=pl.CostEstimate(
            flops=10 * tokens * ways * AGENTS * width,
            bytes_accessed=10 * tokens * ways * width,
            transcendentals=2 * tokens * ways * width,
        ),
        name="spatial",
    )(base, q, k, v, *received, gain)
    if not tiled:
        out = out.reshape(ways, frames, slot, width).transpose(1, 0, 2, 3)
    return out


def rows_of(ref, block, cols, tokens, tiled):
    if tiled:
        return ref[:, block, :, cols].reshape(tokens, -1)
    return ref[block, :, cols]


def squares(x, inverse):
    y = x.astype(jnp.float32) * inverse
    y = y * y
    total = y[:, :HEAD]
    for at in range(HEAD, y.shape[1], HEAD):
        total = total + y[:, at : at + HEAD]
    return total


def project_kernel(at, *refs, pieces, arrays, first, tokens, ways, tiled):
    xs = refs[:arrays]
    if first:
        w, inverse, acc, ss, held = refs[arrays:]
    else:
        w, inverse, acc_in, ss_in, acc, ss, held = refs[arrays:]
    depth = held.shape[1]
    step = pl.program_id(0)
    for i, (which, col, shift) in enumerate(pieces):

        @pl.when(step == i)
        def _():
            for j in range(ways):
                held[j * tokens : (j + 1) * tokens, :] = rows_of(
                    xs[which], (j - shift) % ways, slice(col, col + depth), tokens, tiled
                )

    part = squares(held[...], inverse[...])

    @pl.when(step == 0)
    def _():
        if first:
            ss[...] = part
        else:
            ss[...] = ss_in[...] + part

    @pl.when(step > 0)
    def _():
        ss[...] += part

    width = w.shape[2]
    tile = width // 3 if width % 3 == 0 else width
    for c in range(3):
        for n in range(0, width, tile):
            cols = slice(n, n + tile)
            value = dot(held[...], w[c, :, cols])

            @pl.when(step == 0)
            def _():
                if first:
                    acc[c, :, cols] = value
                else:
                    acc[c, :, cols] = acc_in[c, :, cols] + value

            @pl.when(step > 0)
            def _():
                acc[c, :, cols] += value


def project(pieces, arrays, at, weight, inverse, depth, carried, tokens, ways, tiled):
    rows = tokens * ways
    width = weight.shape[2]
    whole = lambda shape: pl.BlockSpec(shape, lambda i, at: (0,) * len(shape))
    acc_shape, ss_shape = (3, rows, width), (rows, HEAD)
    in_specs = [whole(x.shape) for x in arrays] + [
        pl.BlockSpec((3, depth, width), lambda i, at: (0, at[i], 0)),
        pl.BlockSpec((1, depth), lambda i, at: (0, at[i])),
    ]
    operands = list(arrays) + [weight, inverse]
    if carried is not None:
        in_specs += [whole(acc_shape), whole(ss_shape)]
        operands += list(carried)
    return pl.pallas_call(
        partial(
            project_kernel,
            pieces=pieces,
            arrays=len(arrays),
            first=carried is None,
            tokens=tokens,
            ways=ways,
            tiled=tiled,
        ),
        out_shape=(
            jax.ShapeDtypeStruct(acc_shape, jnp.float32),
            jax.ShapeDtypeStruct(ss_shape, jnp.float32),
        ),
        grid_spec=pltpu.PrefetchScalarGridSpec(
            num_scalar_prefetch=1,
            grid=(len(pieces),),
            in_specs=in_specs,
            out_specs=(whole(acc_shape), whole(ss_shape)),
            scratch_shapes=[pltpu.VMEM((rows, depth), jnp.bfloat16)],
        ),
        cost_estimate=pl.CostEstimate(
            flops=6 * rows * depth * len(pieces) * width,
            bytes_accessed=6 * depth * len(pieces) * width + 8 * 3 * rows * width,
            transcendentals=0,
        ),
        name="project",
    )(at, *operands)


def temporal_kernel(at, *refs, count, heads, tokens, ways, slot, tiled, pieces, columns):
    xs = refs[: len(columns)]
    ws = refs[len(columns) : len(columns) + count]
    inverses = refs[len(columns) + count : len(columns) + 2 * count]
    acc, ss = refs[len(columns) + 2 * count : len(columns) + 2 * count + 2]
    outs = refs[len(columns) + 2 * count + 2 : -2]
    held, rstd = refs[-2:]
    depth = held.shape[2]

    @pl.when(pl.program_id(0) == 0)
    def _():
        total = ss[...]
        for i, (which, col, shift) in enumerate(pieces):
            for j in range(ways):
                held[i, j * tokens : (j + 1) * tokens, :] = rows_of(
                    xs[which], (j - shift) % ways, slice(col, col + depth), tokens, tiled
                )
            total = total + squares(held[i], inverses[i][...])
        mean = jnp.sum(total, axis=1, keepdims=True) * (1.0 / D)
        rstd[...] = jnp.broadcast_to(lax.rsqrt(mean + epsilon), rstd.shape)

    row = lax.broadcasted_iota(jnp.int32, (tokens, tokens), 0)
    col = lax.broadcasted_iota(jnp.int32, (tokens, tokens), 1)
    same = lax.rem(row, slot) == lax.rem(col, slot)
    qkv = []
    for c in range(3):
        value = acc[c]
        for i in range(count):
            value = value + dot(held[i], ws[i][c])
        qkv.append(value)
    for h in range(heads):
        cols = slice(h * HEAD, (h + 1) * HEAD)
        for j in range(ways):
            rows = slice(j * tokens, (j + 1) * tokens)
            q, k, v = ((x[rows, cols] * rstd[rows]).astype(jnp.bfloat16) for x in qkv)
            scores = jnp.where(same, dot_nt(q, k) * SCALE, -1e30)
            weights = jnp.exp(scores - jnp.max(scores, axis=1, keepdims=True))
            weights = weights / jnp.sum(weights, axis=1, keepdims=True)
            outs[j][:, cols] = dot(weights.astype(jnp.bfloat16), v).astype(jnp.bfloat16)


def temporal(pieces, arrays, at, weight, inverse, depth, carried, tokens, ways, slot, tiled):
    rows = tokens * ways
    width = weight.shape[2]
    count = len(pieces)
    heads = 2 if width % (2 * HEAD) == 0 else 1
    step = heads * HEAD
    whole = lambda shape: pl.BlockSpec(shape, lambda n, at: (0,) * len(shape))
    at_piece = lambda i: pl.BlockSpec((3, depth, step), lambda n, at: (0, at[i], n))
    gain_piece = lambda i: pl.BlockSpec((1, depth), lambda n, at: (0, at[i]))
    return pl.pallas_call(
        partial(
            temporal_kernel,
            count=count,
            heads=heads,
            tokens=tokens,
            ways=ways,
            slot=slot,
            tiled=tiled,
            pieces=pieces,
            columns=tuple(range(len(arrays))),
        ),
        out_shape=tuple(jax.ShapeDtypeStruct((tokens, width), jnp.bfloat16) for _ in range(ways)),
        grid_spec=pltpu.PrefetchScalarGridSpec(
            num_scalar_prefetch=1,
            grid=(width // step,),
            in_specs=[whole(x.shape) for x in arrays]
            + [at_piece(i) for i in range(count)]
            + [gain_piece(i) for i in range(count)]
            + [
                pl.BlockSpec((3, rows, step), lambda n, at: (0, 0, n)),
                whole((rows, HEAD)),
            ],
            out_specs=tuple(
                pl.BlockSpec((tokens, step), lambda n, at: (0, n)) for _ in range(ways)
            ),
            scratch_shapes=[
                pltpu.VMEM((count, rows, depth), jnp.bfloat16),
                pltpu.VMEM((rows, HEAD), jnp.float32),
            ],
        ),
        cost_estimate=pl.CostEstimate(
            flops=6 * rows * depth * count * width,
            bytes_accessed=6 * depth * count * width + 4 * 3 * rows * width,
            transcendentals=rows * width,
        ),
        name="temporal",
    )(at, *arrays, *[weight] * count, *[inverse] * count, *carried)


def chunk_heads(group):
    return (group // 4, group // 2, group // 4) if group % 4 == 0 else (1,) * group


def local(spatial_q, spatial_k, spatial_v, norm_gain, temporal_weight):
    frames = lax.axis_size("frame")
    ways = lax.axis_size("row")
    me = lax.axis_index("row")
    tokens = spatial_q.shape[1]
    slot = tokens // frames
    tiled = slot % 8 == 0
    width = temporal_weight.shape[2]
    group = width // HEAD
    chunks = chunk_heads(group)
    depth = min(chunks) * HEAD
    starts = [sum(chunks[:i]) for i in range(len(chunks))]
    weight = jnp.transpose(temporal_weight, (1, 0, 2))
    gain = norm_gain.reshape(1, -1)
    inverse = 1.0 / gain

    def shift(x, k):
        return lax.ppermute(x, "row", [(i, (i + k) % ways) for i in range(ways)])

    received = []
    for start, size in zip(starts, chunks):
        parts = []
        for k in range(1, ways):
            column = lax.rem(me + k, ways) * width + start * HEAD
            stack = [
                lax.dynamic_slice_in_dim(x[0], column, size * HEAD, axis=1)
                for x in (spatial_q, spatial_k, spatial_v)
            ]
            parts.append(shift(jnp.stack(stack), k))
        received.append(parts)

    own = []
    others = []
    for start, size, parts in zip(starts, chunks, received):
        base = (me * group + start).astype(jnp.int32).reshape(1)
        out = spatial(
            spatial_q,
            spatial_k,
            spatial_v,
            parts,
            gain,
            base,
            frames,
            size * HEAD,
            math.gcd(group, start, size),
        )
        moved = lax.all_to_all(out, "frame", split_axis=0, concat_axis=0, tiled=True)
        own.append(moved)
        others.append([shift(moved, k) for k in range(1, ways)])
    if not tiled:
        flat = lambda x: x.transpose(1, 0, 2, 3).reshape(ways, tokens, x.shape[3])
        own = [flat(x) for x in own]
        others = [[flat(x) for x in parts] for parts in others]

    blocks = width // depth

    def gather(wanted):
        pieces, arrays, at = [], [], []
        for i, k in wanted:
            arrays.append(own[i] if k == 0 else others[i][k - 1])
            owner = lax.rem(me + ways - k, ways)
            for sub in range(chunks[i] * HEAD // depth):
                pieces.append((len(arrays) - 1, sub * depth, k))
                at.append(owner * blocks + starts[i] * HEAD // depth + sub)
        return tuple(pieces), arrays, jnp.stack(at).astype(jnp.int32)

    last = len(chunks) - 1
    sizes = dict(tokens=tokens, ways=ways, tiled=tiled)
    before = [(i, k) for i in range(last - 1) for k in range(ways)] + [(last - 1, 0)]
    between = [(last - 1, k) for k in range(1, ways)] + [(last, 0)]
    carried = project(*gather(before), weight, inverse, depth, None, **sizes)
    carried = project(*gather(between), weight, inverse, depth, carried, **sizes)
    final = [(last, k) for k in range(1, ways)]
    attended = temporal(*gather(final), weight, inverse, depth, carried, slot=slot, **sizes)

    def home(x):
        x = x.reshape(frames, slot, width)
        x = lax.all_to_all(x, "frame", split_axis=0, concat_axis=0, tiled=True)
        return x.reshape(tokens, width)

    out = jnp.zeros((tokens, ways * width), jnp.bfloat16)
    for k in range(ways):
        part = attended[0] if k == 0 else shift(attended[k], -k)
        out = lax.dynamic_update_slice_in_dim(
            out, home(part), lax.rem(me + k, ways) * width, axis=1
        )
    return out[None]


def solution(mesh):
    return jax.shard_map(
        local,
        mesh=mesh,
        in_specs=(
            P("frame", "row", None),
            P("frame", "row", None),
            P("frame", "row", None),
            P(),
            P(None, None, "row"),
        ),
        out_specs=P("frame", "row", None),
        check_vma=False,
    )
```

```python
import math
from functools import partial

import jax
import jax.numpy as jnp
from jax import lax
from jax.experimental import pallas as pl
from jax.experimental.pallas import tpu as pltpu
from jax.sharding import PartitionSpec as P

D = 3072
HEADS = 24
AGENTS = 128
HEAD = D // HEADS
SCALE = HEAD ** (-0.5)
EXPONENT = SCALE * math.log2(math.e)

epsilon = 1e-06


def dot(left, right):
    return jnp.dot(left, right, preferred_element_type=jnp.float32)


def dot_nt(left, right):
    return lax.dot_general(
        left, right, (((1,), (1,)), ((), ())), preferred_element_type=jnp.float32
    )


def weighted(scores):
    weights = jnp.exp2((scores - jnp.max(scores, axis=1, keepdims=True)) * EXPONENT)
    return weights, 1.0 / jnp.sum(weights, axis=1, keepdims=True)


def spatial_kernel(base, q, k, v, *rest, heads, pool, tiled):
    received, gain, out = rest[:-2], rest[-2], rest[-1]
    ways = len(received) + 1
    tokens = q.shape[1]
    agent = lax.broadcasted_iota(jnp.int32, (tokens // pool, tokens), 0)
    token = lax.broadcasted_iota(jnp.int32, (tokens // pool, tokens), 1)
    member = ((token >= agent * pool) & (token < (agent + 1) * pool)).astype(jnp.bfloat16)
    split = [slice(h * HEAD, (h + 1) * HEAD) for h in range(heads)]
    pooled = [dot(member, block) for block in [q[0]] + [ref[0] for ref in received]]
    pooled = (jnp.concatenate(pooled) * (1.0 / pool)).astype(jnp.bfloat16)
    agents = [pooled[:, cols] for cols in split]
    queries = [jnp.concatenate([q[0, :, cols]] + [r[0, :, cols] for r in received]) for cols in split]
    keys = [jnp.concatenate([k[0, :, cols]] + [r[1, :, cols] for r in received]) for cols in split]
    values = [jnp.concatenate([v[0, :, cols]] + [r[2, :, cols] for r in received]) for cols in split]
    agent_scores = [dot_nt(a, b) for a, b in zip(agents, keys)]
    token_scores = [dot_nt(a, b) for a, b in zip(queries, agents)]
    agent_weights = [weighted(x) for x in agent_scores]
    token_weights = [weighted(x) for x in token_scores]
    agent_values = [
        (dot(w.astype(jnp.bfloat16), x) * r).astype(jnp.bfloat16)
        for (w, r), x in zip(agent_weights, values)
    ]
    results = [dot((w * r).astype(jnp.bfloat16), x) for (w, r), x in zip(token_weights, agent_values)]
    for cols, result in zip(split, results):
        result = (result * gain[:, cols]).astype(jnp.bfloat16)
        for j in range(ways):
            block = result[j * tokens : (j + 1) * tokens]
            if tiled:
                out[:, j, :, cols] = block.reshape(out.shape[0], out.shape[2], HEAD)
            else:
                out[j, :, cols] = block


def spatial(q, k, v, received, gain, base, frames, width, heads):
    tokens = q.shape[1]
    ways = len(received) + 1
    slot = tokens // frames
    pool = tokens * ways // AGENTS
    step = heads * HEAD
    tiled = slot % 8 == 0
    own = pl.BlockSpec((1, tokens, step), lambda i, base: (0, 0, base[0] // heads + i))
    other = pl.BlockSpec((3, tokens, step), lambda i, base: (0, 0, i))
    if tiled:
        shape = (frames, ways, slot, width)
        out_spec = pl.BlockSpec((frames, ways, slot, step), lambda i, base: (0, 0, 0, i))
    else:
        shape = (ways, tokens, width)
        out_spec = pl.BlockSpec((ways, tokens, step), lambda i, base: (0, 0, i))
    out = pl.pallas_call(
        partial(spatial_kernel, heads=heads, pool=pool, tiled=tiled),
        out_shape=jax.ShapeDtypeStruct(shape, jnp.bfloat16),
        grid_spec=pltpu.PrefetchScalarGridSpec(
            num_scalar_prefetch=1,
            grid=(width // step,),
            in_specs=[own] * 3
            + [other] * len(received)
            + [pl.BlockSpec((1, step), lambda i, base: (0, base[0] // heads + i))],
            out_specs=out_spec,
        ),
        cost_estimate=pl.CostEstimate(
            flops=10 * tokens * ways * AGENTS * width,
            bytes_accessed=10 * tokens * ways * width,
            transcendentals=2 * tokens * ways * width,
        ),
        compiler_params=pltpu.CompilerParams(vmem_limit_bytes=12 << 20),
        name="spatial",
    )(base, q, k, v, *received, gain)
    if not tiled:
        out = out.reshape(ways, frames, slot, width).transpose(1, 0, 2, 3)
    return out


def rows_of(ref, block, cols, tokens, tiled):
    if tiled:
        return ref[:, block, :, cols].reshape(tokens, -1)
    return ref[block, :, cols]


def squares(x, inverse):
    y = x.astype(jnp.float32) * inverse
    y = y * y
    total = y[:, :HEAD]
    for at in range(HEAD, y.shape[1], HEAD):
        total = total + y[:, at : at + HEAD]
    return total


def project_kernel(at, *refs, pieces, arrays, first, tokens, ways, tiled):
    xs = refs[:arrays]
    if first:
        w, inverse, acc, ss, held = refs[arrays:]
    else:
        w, inverse, acc_in, ss_in, acc, ss, held = refs[arrays:]
    depth = held.shape[1]
    step = pl.program_id(0)
    for i, (which, col, shift) in enumerate(pieces):

        @pl.when(step == i)
        def _():
            for j in range(ways):
                held[j * tokens : (j + 1) * tokens, :] = rows_of(
                    xs[which], (j - shift) % ways, slice(col, col + depth), tokens, tiled
                )

    @pl.when(step == 0)
    def _():
        acc[...] = jnp.zeros_like(acc) if first else acc_in[...]
        ss[...] = jnp.zeros_like(ss) if first else ss_in[...]

    ss[...] += squares(held[...], inverse[...])
    width = w.shape[2]
    tile = width // 3 if width % 3 == 0 else width
    for c in range(3):
        for n in range(0, width, tile):
            cols = slice(n, n + tile)
            acc[c, :, cols] += dot(held[...], w[c, :, cols])


def project(pieces, arrays, at, weight, inverse, depth, carried, tokens, ways, tiled):
    rows = tokens * ways
    width = weight.shape[2]
    whole = lambda shape: pl.BlockSpec(shape, lambda i, at: (0,) * len(shape))
    acc_shape, ss_shape = (3, rows, width), (rows, HEAD)
    in_specs = [whole(x.shape) for x in arrays] + [
        pl.BlockSpec((3, depth, width), lambda i, at: (0, at[i], 0)),
        pl.BlockSpec((1, depth), lambda i, at: (0, at[i])),
    ]
    operands = list(arrays) + [weight, inverse]
    if carried is not None:
        in_specs += [whole(acc_shape), whole(ss_shape)]
        operands += list(carried)
    return pl.pallas_call(
        partial(
            project_kernel,
            pieces=pieces,
            arrays=len(arrays),
            first=carried is None,
            tokens=tokens,
            ways=ways,
            tiled=tiled,
        ),
        out_shape=(
            jax.ShapeDtypeStruct(acc_shape, jnp.float32),
            jax.ShapeDtypeStruct(ss_shape, jnp.float32),
        ),
        grid_spec=pltpu.PrefetchScalarGridSpec(
            num_scalar_prefetch=1,
            grid=(len(pieces),),
            in_specs=in_specs,
            out_specs=(whole(acc_shape), whole(ss_shape)),
            scratch_shapes=[pltpu.VMEM((rows, depth), jnp.bfloat16)],
        ),
        cost_estimate=pl.CostEstimate(
            flops=6 * rows * depth * len(pieces) * width,
            bytes_accessed=6 * depth * len(pieces) * width + 8 * 3 * rows * width,
            transcendentals=0,
        ),
        compiler_params=pltpu.CompilerParams(vmem_limit_bytes=32 << 20),
        name="project",
    )(at, *operands)


def temporal_kernel(at, *refs, count, heads, tokens, ways, slot, tiled, pieces, columns):
    xs = refs[: len(columns)]
    ws = refs[len(columns) : len(columns) + count]
    inverses = refs[len(columns) + count : len(columns) + 2 * count]
    acc, ss = refs[len(columns) + 2 * count : len(columns) + 2 * count + 2]
    out, held, rstd = refs[-3:]
    depth = held.shape[2]

    @pl.when(pl.program_id(0) == 0)
    def _():
        total = ss[...]
        for i, (which, col, shift) in enumerate(pieces):
            for j in range(ways):
                held[i, j * tokens : (j + 1) * tokens, :] = rows_of(
                    xs[which], (j - shift) % ways, slice(col, col + depth), tokens, tiled
                )
            total = total + squares(held[i], inverses[i][...])
        mean = jnp.sum(total, axis=1, keepdims=True) * (1.0 / D)
        rstd[...] = jnp.broadcast_to(lax.rsqrt(mean + epsilon), rstd.shape)

    row = lax.broadcasted_iota(jnp.int32, (tokens, tokens), 0)
    col = lax.broadcasted_iota(jnp.int32, (tokens, tokens), 1)
    same = lax.rem(row, slot) == lax.rem(col, slot)
    qkv = []
    for c in range(3):
        value = acc[c]
        for i in range(count):
            value = value + dot(held[i], ws[i][c])
        qkv.append(value)
    qkv = [(x * jnp.concatenate([rstd[...]] * heads, axis=1)).astype(jnp.bfloat16) for x in qkv]
    split = [
        (j, slice(j * tokens, (j + 1) * tokens), slice(h * HEAD, (h + 1) * HEAD))
        for h in range(heads)
        for j in range(ways)
    ]
    scores = [
        jnp.where(same, dot_nt(qkv[0][rows, cols], qkv[1][rows, cols]), -1e30)
        for _, rows, cols in split
    ]
    weights = [weighted(x) for x in scores]
    me = at[count]
    for (j, rows, cols), (w, r) in zip(split, weights):
        result = dot((w * r).astype(jnp.bfloat16), qkv[2][rows, cols]).astype(jnp.bfloat16)
        target = lax.rem(me + ways - j, ways)
        if tiled:
            out[:, target, :, cols] = result.reshape(out.shape[0], slot, HEAD)
        else:
            out[target, :, cols] = result


def temporal(pieces, arrays, at, weight, inverse, depth, carried, tokens, ways, slot, tiled):
    rows = tokens * ways
    width = weight.shape[2]
    count = len(pieces)
    frames = tokens // slot
    heads = math.gcd(width // HEAD, 6)
    step = heads * HEAD
    if tiled:
        shape = (frames, ways, slot, width)
        out_spec = pl.BlockSpec((frames, ways, slot, step), lambda n, at: (0, 0, 0, n))
    else:
        shape = (ways, tokens, width)
        out_spec = pl.BlockSpec((ways, tokens, step), lambda n, at: (0, 0, n))
    whole = lambda shape: pl.BlockSpec(shape, lambda n, at: (0,) * len(shape))
    at_piece = lambda i: pl.BlockSpec((3, depth, step), lambda n, at: (0, at[i], n))
    gain_piece = lambda i: pl.BlockSpec((1, depth), lambda n, at: (0, at[i]))
    out = pl.pallas_call(
        partial(
            temporal_kernel,
            count=count,
            heads=heads,
            tokens=tokens,
            ways=ways,
            slot=slot,
            tiled=tiled,
            pieces=pieces,
            columns=tuple(range(len(arrays))),
        ),
        out_shape=jax.ShapeDtypeStruct(shape, jnp.bfloat16),
        grid_spec=pltpu.PrefetchScalarGridSpec(
            num_scalar_prefetch=1,
            grid=(width // step,),
            in_specs=[whole(x.shape) for x in arrays]
            + [at_piece(i) for i in range(count)]
            + [gain_piece(i) for i in range(count)]
            + [
                pl.BlockSpec((3, rows, step), lambda n, at: (0, 0, n)),
                whole((rows, HEAD)),
            ],
            out_specs=out_spec,
            scratch_shapes=[
                pltpu.VMEM((count, rows, depth), jnp.bfloat16),
                pltpu.VMEM((rows, HEAD), jnp.float32),
            ],
        ),
        cost_estimate=pl.CostEstimate(
            flops=6 * rows * depth * count * width,
            bytes_accessed=6 * depth * count * width + 4 * 3 * rows * width,
            transcendentals=rows * width,
        ),
        compiler_params=pltpu.CompilerParams(vmem_limit_bytes=24 << 20),
        name="temporal",
    )(at, *arrays, *[weight] * count, *[inverse] * count, *carried)
    if not tiled:
        out = out.reshape(ways, frames, slot, width).transpose(1, 0, 2, 3)
    return out


def local(spatial_q, spatial_k, spatial_v, norm_gain, temporal_weight):
    frames = lax.axis_size("frame")
    ways = lax.axis_size("row")
    me = lax.axis_index("row").astype(jnp.int32)
    tokens = spatial_q.shape[1]
    slot = tokens // frames
    tiled = slot % 8 == 0
    width = temporal_weight.shape[2]
    group = width // HEAD
    unit = group // 4 if group % 4 == 0 else 1
    depth = unit * HEAD
    units = group // unit
    chunks = (range(0, units - units // 2), range(units - units // 2, units))
    weight = jnp.transpose(temporal_weight, (1, 0, 2))
    gain = norm_gain.reshape(1, -1)
    inverse = 1.0 / gain

    def shift(x, k):
        return lax.ppermute(x, "row", [(i, (i + k) % ways) for i in range(ways)])

    received = []
    for chunk in chunks:
        parts = []
        for k in range(1, ways):
            column = lax.rem(me + k, ways) * width + chunk[0] * depth
            stack = [
                lax.dynamic_slice_in_dim(x[0], column, len(chunk) * depth, axis=1)
                for x in (spatial_q, spatial_k, spatial_v)
            ]
            parts.append(shift(jnp.stack(stack), k))
        received.append(parts)

    pieces = {}
    for chunk, parts in zip(chunks, received):
        base = (me * group + chunk[0] * unit).reshape(1)
        heads = math.gcd(group, chunk[0] * unit, len(chunk) * unit)
        out = spatial(
            spatial_q,
            spatial_k,
            spatial_v,
            parts,
            gain,
            base,
            frames,
            len(chunk) * depth,
            min(heads, unit),
        )
        moved = lax.all_to_all(out, "frame", split_axis=0, concat_axis=0, tiled=True)
        for n, u in enumerate(chunk):
            pieces[u, 0] = (moved, n * depth)
        for k in range(1, ways):
            shared = shift(moved, k)
            for n, u in enumerate(chunk):
                pieces[u, k] = (shared, n * depth)

    def gather(wanted):
        listed, arrays, at = [], [], []
        for u, k in wanted:
            array, column = pieces[u, k]
            where = [i for i, x in enumerate(arrays) if x is array]
            if not where:
                where = [len(arrays)]
                arrays.append(array)
            listed.append((where[0], column, k))
            at.append(lax.rem(me + ways - k, ways) * units + u)
        if not tiled:
            arrays = [x.transpose(1, 0, 2, 3).reshape(ways, tokens, -1) for x in arrays]
        return tuple(listed), arrays, jnp.stack(at + [me])

    sizes = dict(tokens=tokens, ways=ways, tiled=tiled)
    early = [(u, 0) for u in chunks[0]]
    late = [(u, k) for k in range(1, ways) for u in chunks[0]] + [(u, 0) for u in chunks[1]]
    final = [(u, k) for k in range(1, ways) for u in chunks[1]]
    carried = project(*gather(early), weight, inverse, depth, None, **sizes)
    carried = project(*gather(late), weight, inverse, depth, carried, **sizes)
    out = temporal(*gather(final), weight, inverse, depth, carried, slot=slot, **sizes)
    out = out.reshape(frames * ways, slot, width)
    out = lax.all_to_all(out, ("frame", "row"), split_axis=0, concat_axis=0, tiled=True)
    out = out.reshape(frames, ways, slot, width).transpose(0, 2, 1, 3)
    return out.reshape(1, tokens, ways * width)


def solution(mesh):
    return jax.shard_map(
        local,
        mesh=mesh,
        in_specs=(
            P("frame", "row", None),
            P("frame", "row", None),
            P("frame", "row", None),
            P(),
            P(None, None, "row"),
        ),
        out_specs=P("frame", "row", None),
        check_vma=False,
    )
```

```python
import math
from functools import partial

import jax
import jax.numpy as jnp
from jax import lax
from jax.experimental import pallas as pl
from jax.experimental.pallas import tpu as pltpu
from jax.sharding import PartitionSpec as P

D = 3072
HEADS = 24
AGENTS = 128
HEAD = D // HEADS
SCALE = HEAD ** (-0.5)
EXPONENT = SCALE * math.log2(math.e)

epsilon = 1e-06


def dot(left, right):
    return jnp.dot(left, right, preferred_element_type=jnp.float32)


def dot_nt(left, right):
    return lax.dot_general(
        left, right, (((1,), (1,)), ((), ())), preferred_element_type=jnp.float32
    )


def weighted(scores):
    weights = jnp.exp2((scores - jnp.max(scores, axis=1, keepdims=True)) * EXPONENT)
    return weights, 1.0 / jnp.sum(weights, axis=1, keepdims=True)


def spatial_kernel(base, q, k, v, *rest, heads, pool, tiled):
    received, gain, out = rest[:-2], rest[-2], rest[-1]
    ways = len(received) + 1
    tokens = q.shape[1]
    agent = lax.broadcasted_iota(jnp.int32, (tokens // pool, tokens), 0)
    token = lax.broadcasted_iota(jnp.int32, (tokens // pool, tokens), 1)
    member = ((token >= agent * pool) & (token < (agent + 1) * pool)).astype(jnp.bfloat16)
    split = [slice(h * HEAD, (h + 1) * HEAD) for h in range(heads)]
    pooled = [dot(member, block) for block in [q[0]] + [ref[0] for ref in received]]
    pooled = (jnp.concatenate(pooled) * (1.0 / pool)).astype(jnp.bfloat16)
    agents = [pooled[:, cols] for cols in split]
    queries = [jnp.concatenate([q[0, :, cols]] + [r[0, :, cols] for r in received]) for cols in split]
    keys = [jnp.concatenate([k[0, :, cols]] + [r[1, :, cols] for r in received]) for cols in split]
    values = [jnp.concatenate([v[0, :, cols]] + [r[2, :, cols] for r in received]) for cols in split]
    agent_scores = [dot_nt(a, b) for a, b in zip(agents, keys)]
    token_scores = [dot_nt(a, b) for a, b in zip(queries, agents)]
    agent_weights = [weighted(x) for x in agent_scores]
    token_weights = [weighted(x) for x in token_scores]
    agent_values = [
        (dot(w.astype(jnp.bfloat16), x) * r).astype(jnp.bfloat16)
        for (w, r), x in zip(agent_weights, values)
    ]
    results = [dot((w * r).astype(jnp.bfloat16), x) for (w, r), x in zip(token_weights, agent_values)]
    for cols, result in zip(split, results):
        result = (result * gain[:, cols]).astype(jnp.bfloat16)
        for j in range(ways):
            block = result[j * tokens : (j + 1) * tokens]
            if tiled:
                out[:, j, :, cols] = block.reshape(out.shape[0], out.shape[2], HEAD)
            else:
                out[j, :, cols] = block


def spatial(q, k, v, received, gain, base, frames, width, heads):
    tokens = q.shape[1]
    ways = len(received) + 1
    slot = tokens // frames
    pool = tokens * ways // AGENTS
    step = heads * HEAD
    tiled = slot % 8 == 0
    own = pl.BlockSpec((1, tokens, step), lambda i, base: (0, 0, base[0] // heads + i))
    other = pl.BlockSpec((3, tokens, step), lambda i, base: (0, 0, i))
    if tiled:
        shape = (frames, ways, slot, width)
        out_spec = pl.BlockSpec((frames, ways, slot, step), lambda i, base: (0, 0, 0, i))
    else:
        shape = (ways, tokens, width)
        out_spec = pl.BlockSpec((ways, tokens, step), lambda i, base: (0, 0, i))
    out = pl.pallas_call(
        partial(spatial_kernel, heads=heads, pool=pool, tiled=tiled),
        out_shape=jax.ShapeDtypeStruct(shape, jnp.bfloat16),
        grid_spec=pltpu.PrefetchScalarGridSpec(
            num_scalar_prefetch=1,
            grid=(width // step,),
            in_specs=[own] * 3
            + [other] * len(received)
            + [pl.BlockSpec((1, step), lambda i, base: (0, base[0] // heads + i))],
            out_specs=out_spec,
        ),
        cost_estimate=pl.CostEstimate(
            flops=10 * tokens * ways * AGENTS * width,
            bytes_accessed=10 * tokens * ways * width,
            transcendentals=2 * tokens * ways * width,
        ),
        compiler_params=pltpu.CompilerParams(vmem_limit_bytes=12 << 20),
        name="spatial",
    )(base, q, k, v, *received, gain)
    if not tiled:
        out = out.reshape(ways, frames, slot, width).transpose(1, 0, 2, 3)
    return out


def rows_of(ref, block, cols, tokens, tiled):
    if tiled:
        return ref[:, block, :, cols].reshape(tokens, -1)
    return ref[block, :, cols]


def squares(x, inverse):
    y = x.astype(jnp.float32) * inverse
    y = y * y
    total = y[:, :HEAD]
    for at in range(HEAD, y.shape[1], HEAD):
        total = total + y[:, at : at + HEAD]
    return total


def project_kernel(at, *refs, pieces, arrays, first, tokens, ways, tiled):
    xs = refs[:arrays]
    if first:
        w, inverse, acc, ss, held = refs[arrays:]
    else:
        w, inverse, acc_in, ss_in, acc, ss, held = refs[arrays:]
    depth = held.shape[1]
    step = pl.program_id(0)
    for i, (which, col, shift) in enumerate(pieces):

        @pl.when(step == i)
        def _():
            for j in range(ways):
                held[j * tokens : (j + 1) * tokens, :] = rows_of(
                    xs[which], (j - shift) % ways, slice(col, col + depth), tokens, tiled
                )

    @pl.when(step == 0)
    def _():
        acc[...] = jnp.zeros_like(acc) if first else acc_in[...]
        ss[...] = jnp.zeros_like(ss) if first else ss_in[...]

    ss[...] += squares(held[...], inverse[...])
    width = w.shape[2]
    tile = width // 3 if width % 3 == 0 else width
    for c in range(3):
        for n in range(0, width, tile):
            cols = slice(n, n + tile)
            acc[c, :, cols] += dot(held[...], w[c, :, cols])


def project(pieces, arrays, at, place, weight, inverse, depth, carried, tokens, ways, tiled):
    rows = tokens * ways
    width = weight.shape[2]
    whole = lambda shape: pl.BlockSpec(shape, lambda i, at: (0,) * len(shape))
    acc_shape, ss_shape = (3, rows, width), (rows, HEAD)
    in_specs = [whole(x.shape) for x in arrays] + [
        pl.BlockSpec((3, depth, width), lambda i, at: (0, at[place[0] + i * place[1]], 0)),
        pl.BlockSpec((1, depth), lambda i, at: (0, at[place[0] + i * place[1]])),
    ]
    operands = list(arrays) + [weight, inverse]
    if carried is not None:
        in_specs += [whole(acc_shape), whole(ss_shape)]
        operands += list(carried)
    return pl.pallas_call(
        partial(
            project_kernel,
            pieces=pieces,
            arrays=len(arrays),
            first=carried is None,
            tokens=tokens,
            ways=ways,
            tiled=tiled,
        ),
        out_shape=(
            jax.ShapeDtypeStruct(acc_shape, jnp.float32),
            jax.ShapeDtypeStruct(ss_shape, jnp.float32),
        ),
        grid_spec=pltpu.PrefetchScalarGridSpec(
            num_scalar_prefetch=1,
            grid=(len(pieces),),
            in_specs=in_specs,
            out_specs=(whole(acc_shape), whole(ss_shape)),
            scratch_shapes=[pltpu.VMEM((rows, depth), jnp.bfloat16)],
        ),
        cost_estimate=pl.CostEstimate(
            flops=6 * rows * depth * len(pieces) * width,
            bytes_accessed=6 * depth * len(pieces) * width + 8 * 3 * rows * width,
            transcendentals=0,
        ),
        input_output_aliases=(
            {} if carried is None else {len(arrays) + 3: 0, len(arrays) + 4: 1}
        ),
        compiler_params=pltpu.CompilerParams(vmem_limit_bytes=32 << 20),
        name="project",
    )(at, *operands)


def temporal_kernel(at, *refs, count, heads, tokens, ways, slot, tiled, pieces, columns):
    xs = refs[: len(columns)]
    ws = refs[len(columns) : len(columns) + count]
    inverses = refs[len(columns) + count : len(columns) + 2 * count]
    acc, ss = refs[len(columns) + 2 * count : len(columns) + 2 * count + 2]
    out, held, rstd = refs[-3:]
    depth = held.shape[2]

    @pl.when(pl.program_id(0) == 0)
    def _():
        total = ss[...]
        for i, (which, col, shift) in enumerate(pieces):
            for j in range(ways):
                held[i, j * tokens : (j + 1) * tokens, :] = rows_of(
                    xs[which], (j - shift) % ways, slice(col, col + depth), tokens, tiled
                )
            total = total + squares(held[i], inverses[i][...])
        mean = jnp.sum(total, axis=1, keepdims=True) * (1.0 / D)
        rstd[...] = jnp.broadcast_to(lax.rsqrt(mean + epsilon), rstd.shape)

    row = lax.broadcasted_iota(jnp.int32, (tokens, tokens), 0)
    col = lax.broadcasted_iota(jnp.int32, (tokens, tokens), 1)
    same = lax.rem(row, slot) == lax.rem(col, slot)
    qkv = []
    for c in range(3):
        value = acc[c]
        for i in range(count):
            value = value + dot(held[i], ws[i][c])
        qkv.append(value)
    qkv = [(x * jnp.concatenate([rstd[...]] * heads, axis=1)).astype(jnp.bfloat16) for x in qkv]
    split = [
        (j, slice(j * tokens, (j + 1) * tokens), slice(h * HEAD, (h + 1) * HEAD))
        for h in range(heads)
        for j in range(ways)
    ]
    scores = [
        jnp.where(same, dot_nt(qkv[0][rows, cols], qkv[1][rows, cols]), -1e30)
        for _, rows, cols in split
    ]
    weights = [weighted(x) for x in scores]
    me = at[at.shape[0] - 1]
    for (j, rows, cols), (w, r) in zip(split, weights):
        result = dot((w * r).astype(jnp.bfloat16), qkv[2][rows, cols]).astype(jnp.bfloat16)
        target = lax.rem(me + ways - j, ways)
        if tiled:
            out[:, target, :, cols] = result.reshape(out.shape[0], slot, HEAD)
        else:
            out[target, :, cols] = result


def temporal(pieces, arrays, at, place, weight, inverse, depth, carried, tokens, ways, slot, tiled):
    rows = tokens * ways
    width = weight.shape[2]
    count = len(pieces)
    frames = tokens // slot
    heads = math.gcd(width // HEAD, 6)
    step = heads * HEAD
    if tiled:
        shape = (frames, ways, slot, width)
        out_spec = pl.BlockSpec((frames, ways, slot, step), lambda n, at: (0, 0, 0, n))
    else:
        shape = (ways, tokens, width)
        out_spec = pl.BlockSpec((ways, tokens, step), lambda n, at: (0, 0, n))
    whole = lambda shape: pl.BlockSpec(shape, lambda n, at: (0,) * len(shape))
    at_piece = lambda i: pl.BlockSpec((3, depth, step), lambda n, at: (0, at[place[0] + i * place[1]], n))
    gain_piece = lambda i: pl.BlockSpec((1, depth), lambda n, at: (0, at[place[0] + i * place[1]]))
    out = pl.pallas_call(
        partial(
            temporal_kernel,
            count=count,
            heads=heads,
            tokens=tokens,
            ways=ways,
            slot=slot,
            tiled=tiled,
            pieces=pieces,
            columns=tuple(range(len(arrays))),
        ),
        out_shape=jax.ShapeDtypeStruct(shape, jnp.bfloat16),
        grid_spec=pltpu.PrefetchScalarGridSpec(
            num_scalar_prefetch=1,
            grid=(width // step,),
            in_specs=[whole(x.shape) for x in arrays]
            + [at_piece(i) for i in range(count)]
            + [gain_piece(i) for i in range(count)]
            + [
                pl.BlockSpec((3, rows, step), lambda n, at: (0, 0, n)),
                whole((rows, HEAD)),
            ],
            out_specs=out_spec,
            scratch_shapes=[
                pltpu.VMEM((count, rows, depth), jnp.bfloat16),
                pltpu.VMEM((rows, HEAD), jnp.float32),
            ],
        ),
        cost_estimate=pl.CostEstimate(
            flops=6 * rows * depth * count * width,
            bytes_accessed=6 * depth * count * width + 4 * 3 * rows * width,
            transcendentals=rows * width,
        ),
        compiler_params=pltpu.CompilerParams(vmem_limit_bytes=24 << 20),
        name="temporal",
    )(at, *arrays, *[weight] * count, *[inverse] * count, *carried)
    if not tiled:
        out = out.reshape(ways, frames, slot, width).transpose(1, 0, 2, 3)
    return out


def pack_kernel(at, q, k, v, out):
    for i, ref in enumerate((q, k, v)):
        out[i] = ref[0]


def pack(q, k, v, at, width):
    tokens = q.shape[1]
    count = at.shape[0]
    return pl.pallas_call(
        pack_kernel,
        out_shape=jax.ShapeDtypeStruct((3, tokens, count * width), q.dtype),
        grid_spec=pltpu.PrefetchScalarGridSpec(
            num_scalar_prefetch=1,
            grid=(count,),
            in_specs=[pl.BlockSpec((1, tokens, width), lambda i, at: (0, 0, at[i]))] * 3,
            out_specs=pl.BlockSpec((3, tokens, width), lambda i, at: (0, 0, i)),
        ),
        compiler_params=pltpu.CompilerParams(vmem_limit_bytes=8 << 20),
        name="pack",
    )(at, q, k, v)


def split_kernel(moved, *outs):
    for n, out in enumerate(outs):
        out[...] = moved[..., n * out.shape[-1] : (n + 1) * out.shape[-1]]


def split(moved, count):
    if count == 1:
        return (moved,)
    shape = moved.shape[:-1] + (moved.shape[-1] // count,)
    return pl.pallas_call(
        split_kernel,
        out_shape=(jax.ShapeDtypeStruct(shape, moved.dtype),) * count,
        compiler_params=pltpu.CompilerParams(vmem_limit_bytes=8 << 20),
        name="split",
    )(moved)


def local(spatial_q, spatial_k, spatial_v, norm_gain, temporal_weight):
    frames = lax.axis_size("frame")
    ways = lax.axis_size("row")
    me = lax.axis_index("row").astype(jnp.int32)
    tokens = spatial_q.shape[1]
    slot = tokens // frames
    tiled = slot % 8 == 0
    width = temporal_weight.shape[2]
    group = width // HEAD
    count = chunk_count(group)
    heads = group // count
    depth = heads * HEAD
    weight = jnp.transpose(temporal_weight, (1, 0, 2))
    spatial_q, spatial_k, spatial_v = (
        pltpu.with_memory_space_constraint(x, pltpu.HBM) for x in (spatial_q, spatial_k, spatial_v)
    )
    gain = norm_gain.reshape(1, -1)
    inverse = 1.0 / gain

    def shift(x, k):
        return lax.ppermute(x, "row", [(i, (i + k) % ways) for i in range(ways)])

    chunks = [c for c in (range(0, 1), range(1, count)) if c]
    received = []
    for chunk in chunks:
        parts = []
        for k in range(1, ways):
            at = lax.rem(me + k, ways) * count + jnp.arange(chunk[0], chunk[-1] + 1)
            packed = pack(spatial_q, spatial_k, spatial_v, at.astype(jnp.int32), depth)
            parts.append(shift(packed, k))
        received.append(parts)

    pieces = {}
    for chunk, parts in zip(chunks, received):
        base = (me * group + chunk[0] * heads).reshape(1)
        span = len(chunk) * depth
        out = spatial(
            spatial_q, spatial_k, spatial_v, parts, gain, base, frames, span, heads
        )
        moved = lax.all_to_all(out, "frame", split_axis=0, concat_axis=0, tiled=True)
        for u, part in zip(chunk, split(moved, len(chunk))):
            pieces[u, 0] = (part, 0)
            for k in range(1, ways):
                pieces[u, k] = (shift(part, k), 0)

    table = [lax.rem(me + ways - k, ways) * count + u for k in range(ways) for u in range(count)]
    table = jnp.stack(table + [me])

    def gather(wanted):
        listed, arrays = [], []
        for u, k in wanted:
            array, column = pieces[u, k]
            where = [n for n, x in enumerate(arrays) if x is array]
            if not where:
                where = [len(arrays)]
                arrays.append(array)
            listed.append((where[0], column, k))
        if not tiled:
            arrays = [x.transpose(1, 0, 2, 3).reshape(ways, tokens, -1) for x in arrays]
        at = [k * count + u for u, k in wanted]
        stride = at[1] - at[0] if len(at) > 1 else 0
        assert at == [at[0] + n * stride for n in range(len(at))]
        return tuple(listed), arrays, table, (at[0], stride)

    own = lambda units: [(u, 0) for u in units]
    other = lambda units: [(u, k) for u in units for k in range(1, ways)]
    last = count - 1
    steps = [own(chunks[0]) + other(u for u in chunks[0] if u < last)]
    steps += [own(chunk) for chunk in chunks[1:]]
    steps += [other([u]) for u in range(1, last)]
    sizes = dict(tokens=tokens, ways=ways, tiled=tiled)
    carried = None
    for wanted in steps:
        carried = project(*gather(wanted), weight, inverse, depth, carried, **sizes)
    final = gather(other([last]))
    out = temporal(*final, weight, inverse, depth, carried, slot=slot, **sizes)
    out = out.reshape(frames * ways, slot, width)
    out = lax.all_to_all(out, ("frame", "row"), split_axis=0, concat_axis=0, tiled=True)
    out = out.reshape(frames, ways, slot, width).transpose(0, 2, 1, 3)
    return out.reshape(1, tokens, ways * width)


def chunk_count(group):
    return 3 if group % 3 == 0 else math.gcd(group, 2)


def solution(mesh):
    return jax.shard_map(
        local,
        mesh=mesh,
        in_specs=(
            P("frame", "row", None),
            P("frame", "row", None),
            P("frame", "row", None),
            P(),
            P(None, None, "row"),
        ),
        out_specs=P("frame", "row", None),
        check_vma=False,
    )
```

```python
import math
from functools import partial

import jax
import jax.numpy as jnp
from jax import lax
from jax.experimental import pallas as pl
from jax.experimental.pallas import tpu as pltpu
from jax.sharding import PartitionSpec as P

D = 3072
HEADS = 24
AGENTS = 128
HEAD = D // HEADS
SCALE = HEAD ** (-0.5)
EXPONENT = SCALE * math.log2(math.e)

epsilon = 1e-06


def dot(left, right):
    return jnp.dot(left, right, preferred_element_type=jnp.float32)


def dot_nt(left, right):
    return lax.dot_general(
        left, right, (((1,), (1,)), ((), ())), preferred_element_type=jnp.float32
    )


def weighted(scores):
    weights = jnp.exp2((scores - jnp.max(scores, axis=1, keepdims=True)) * EXPONENT)
    return weights, 1.0 / jnp.sum(weights, axis=1, keepdims=True)


def spatial_kernel(base, q, k, v, *rest, heads, pool, tiled):
    received, gain, out = rest[:-2], rest[-2], rest[-1]
    ways = len(received) + 1
    tokens = q.shape[1]
    agent = lax.broadcasted_iota(jnp.int32, (tokens // pool, tokens), 0)
    token = lax.broadcasted_iota(jnp.int32, (tokens // pool, tokens), 1)
    member = ((token >= agent * pool) & (token < (agent + 1) * pool)).astype(jnp.bfloat16)
    split = [slice(h * HEAD, (h + 1) * HEAD) for h in range(heads)]
    pooled = [dot(member, block) for block in [q[0]] + [ref[0] for ref in received]]
    pooled = (jnp.concatenate(pooled) * (1.0 / pool)).astype(jnp.bfloat16)
    agents = [pooled[:, cols] for cols in split]
    queries = [jnp.concatenate([q[0, :, cols]] + [r[0, :, cols] for r in received]) for cols in split]
    keys = [jnp.concatenate([k[0, :, cols]] + [r[1, :, cols] for r in received]) for cols in split]
    values = [jnp.concatenate([v[0, :, cols]] + [r[2, :, cols] for r in received]) for cols in split]
    agent_scores = [dot_nt(a, b) for a, b in zip(agents, keys)]
    token_scores = [dot_nt(a, b) for a, b in zip(queries, agents)]
    agent_weights = [weighted(x) for x in agent_scores]
    token_weights = [weighted(x) for x in token_scores]
    agent_values = [
        (dot(w.astype(jnp.bfloat16), x) * r).astype(jnp.bfloat16)
        for (w, r), x in zip(agent_weights, values)
    ]
    results = [dot((w * r).astype(jnp.bfloat16), x) for (w, r), x in zip(token_weights, agent_values)]
    for cols, result in zip(split, results):
        result = (result * gain[:, cols]).astype(jnp.bfloat16)
        for j in range(ways):
            block = result[j * tokens : (j + 1) * tokens]
            if tiled:
                out[:, j, :, cols] = block.reshape(out.shape[0], out.shape[2], HEAD)
            else:
                out[j, :, cols] = block


def spatial(q, k, v, received, gain, base, frames, width, heads):
    tokens = q.shape[1]
    ways = len(received) + 1
    slot = tokens // frames
    pool = tokens * ways // AGENTS
    step = heads * HEAD
    tiled = slot % 8 == 0
    own = pl.BlockSpec((1, tokens, step), lambda i, base: (0, 0, base[0] // heads + i))
    other = pl.BlockSpec((3, tokens, step), lambda i, base: (0, 0, i))
    if tiled:
        shape = (frames, ways, slot, width)
        out_spec = pl.BlockSpec((frames, ways, slot, step), lambda i, base: (0, 0, 0, i))
    else:
        shape = (ways, tokens, width)
        out_spec = pl.BlockSpec((ways, tokens, step), lambda i, base: (0, 0, i))
    out = pl.pallas_call(
        partial(spatial_kernel, heads=heads, pool=pool, tiled=tiled),
        out_shape=jax.ShapeDtypeStruct(shape, jnp.bfloat16),
        grid_spec=pltpu.PrefetchScalarGridSpec(
            num_scalar_prefetch=1,
            grid=(width // step,),
            in_specs=[own] * 3
            + [other] * len(received)
            + [pl.BlockSpec((1, step), lambda i, base: (0, base[0] // heads + i))],
            out_specs=out_spec,
        ),
        cost_estimate=pl.CostEstimate(
            flops=10 * tokens * ways * AGENTS * width,
            bytes_accessed=10 * tokens * ways * width,
            transcendentals=2 * tokens * ways * width,
        ),
        compiler_params=pltpu.CompilerParams(vmem_limit_bytes=12 << 20),
        name="spatial",
    )(base, q, k, v, *received, gain)
    if not tiled:
        out = out.reshape(ways, frames, slot, width).transpose(1, 0, 2, 3)
    return out


def rows_of(ref, block, cols, tokens, tiled):
    if tiled:
        return ref[:, block, :, cols].reshape(tokens, -1)
    return ref[block, :, cols]


def squares(x, inverse):
    y = x.astype(jnp.float32) * inverse
    y = y * y
    total = y[:, :HEAD]
    for at in range(HEAD, y.shape[1], HEAD):
        total = total + y[:, at : at + HEAD]
    return total


def project_kernel(at, *refs, pieces, arrays, first, tokens, ways, tiled):
    xs = refs[:arrays]
    if first:
        w, inverse, acc, ss, held = refs[arrays:]
    else:
        w, inverse, acc_in, ss_in, acc, ss, held = refs[arrays:]
    depth = held.shape[1]
    step, c = pl.program_id(0), pl.program_id(1)
    for i, (which, col, shift) in enumerate(pieces):

        @pl.when((step == i) & (c == 0))
        def _():
            for j in range(ways):
                held[j * tokens : (j + 1) * tokens, :] = rows_of(
                    xs[which], (j - shift) % ways, slice(col, col + depth), tokens, tiled
                )
            before = ss[...] if i else (jnp.zeros_like(ss) if first else ss_in[...])
            ss[...] = before + squares(held[...], inverse[...])

    width = w.shape[2]
    tile = width // 3 if width % 3 == 0 else width
    if first:

        @pl.when(step == 0)
        def _():
            for n in range(0, width, tile):
                cols = slice(n, n + tile)
                acc[c, :, cols] = dot(held[...], w[0, :, cols])

        @pl.when(step > 0)
        def _():
            for n in range(0, width, tile):
                cols = slice(n, n + tile)
                acc[c, :, cols] += dot(held[...], w[0, :, cols])

    else:

        @pl.when(step == 0)
        def _():
            acc[c] = acc_in[0]

        for n in range(0, width, tile):
            cols = slice(n, n + tile)
            acc[c, :, cols] += dot(held[...], w[0, :, cols])


def project(pieces, arrays, at, place, weight, inverse, depth, carried, tokens, ways, tiled):
    rows = tokens * ways
    width = weight.shape[2]
    whole = lambda shape: pl.BlockSpec(shape, lambda i, c, at: (0,) * len(shape))
    acc_shape, ss_shape = (3, rows, width), (rows, HEAD)
    in_specs = [whole(x.shape) for x in arrays] + [
        pl.BlockSpec((1, depth, width), lambda i, c, at: (c, at[place + i], 0)),
        pl.BlockSpec((1, depth), lambda i, c, at: (0, at[place + i])),
    ]
    operands = list(arrays) + [weight, inverse]
    if carried is not None:
        fetch = lambda i, c, at: (jnp.where(i == 0, c, 2), 0, 0)
        in_specs += [pl.BlockSpec((1, rows, width), fetch), whole(ss_shape)]
        operands += list(carried)
    return pl.pallas_call(
        partial(
            project_kernel,
            pieces=pieces,
            arrays=len(arrays),
            first=carried is None,
            tokens=tokens,
            ways=ways,
            tiled=tiled,
        ),
        out_shape=(
            jax.ShapeDtypeStruct(acc_shape, jnp.float32),
            jax.ShapeDtypeStruct(ss_shape, jnp.float32),
        ),
        grid_spec=pltpu.PrefetchScalarGridSpec(
            num_scalar_prefetch=1,
            grid=(len(pieces), 3),
            in_specs=in_specs,
            out_specs=(whole(acc_shape), whole(ss_shape)),
            scratch_shapes=[pltpu.VMEM((rows, depth), jnp.bfloat16)],
        ),
        cost_estimate=pl.CostEstimate(
            flops=6 * rows * depth * len(pieces) * width,
            bytes_accessed=6 * depth * len(pieces) * width + 8 * 3 * rows * width,
            transcendentals=0,
        ),
        compiler_params=pltpu.CompilerParams(vmem_limit_bytes=32 << 20),
        name="project",
    )(at, *operands)


def temporal_kernel(at, *refs, count, heads, tokens, ways, slot, tiled, pieces, columns):
    xs = refs[: len(columns)]
    ws = refs[len(columns) : len(columns) + count]
    inverses = refs[len(columns) + count : len(columns) + 2 * count]
    acc, ss = refs[len(columns) + 2 * count : len(columns) + 2 * count + 2]
    out, held, rstd = refs[-3:]
    depth = held.shape[2]

    @pl.when(pl.program_id(0) == 0)
    def _():
        total = ss[...]
        for i, (which, col, shift) in enumerate(pieces):
            for j in range(ways):
                held[i, j * tokens : (j + 1) * tokens, :] = rows_of(
                    xs[which], (j - shift) % ways, slice(col, col + depth), tokens, tiled
                )
            total = total + squares(held[i], inverses[i][...])
        mean = jnp.sum(total, axis=1, keepdims=True) * (1.0 / D)
        rstd[...] = jnp.broadcast_to(lax.rsqrt(mean + epsilon), rstd.shape)

    row = lax.broadcasted_iota(jnp.int32, (tokens, tokens), 0)
    col = lax.broadcasted_iota(jnp.int32, (tokens, tokens), 1)
    same = lax.rem(row, slot) == lax.rem(col, slot)
    qkv = []
    for c in range(3):
        value = acc[c]
        for i in range(count):
            value = value + dot(held[i], ws[i][c])
        qkv.append(value)
    qkv = [(x * jnp.concatenate([rstd[...]] * heads, axis=1)).astype(jnp.bfloat16) for x in qkv]
    split = [
        (j, slice(j * tokens, (j + 1) * tokens), slice(h * HEAD, (h + 1) * HEAD))
        for h in range(heads)
        for j in range(ways)
    ]
    scores = [
        jnp.where(same, dot_nt(qkv[0][rows, cols], qkv[1][rows, cols]), -1e30)
        for _, rows, cols in split
    ]
    weights = [weighted(x) for x in scores]
    me = at[at.shape[0] - 1]
    for (j, rows, cols), (w, r) in zip(split, weights):
        result = dot((w * r).astype(jnp.bfloat16), qkv[2][rows, cols]).astype(jnp.bfloat16)
        target = lax.rem(me + ways - j, ways)
        if tiled:
            out[:, target, :, cols] = result.reshape(out.shape[0], slot, HEAD)
        else:
            out[target, :, cols] = result


def temporal(pieces, arrays, at, place, weight, inverse, depth, carried, tokens, ways, slot, tiled):
    rows = tokens * ways
    width = weight.shape[2]
    count = len(pieces)
    frames = tokens // slot
    heads = math.gcd(width // HEAD, 6)
    step = heads * HEAD
    if tiled:
        shape = (frames, ways, slot, width)
        out_spec = pl.BlockSpec((frames, ways, slot, step), lambda n, at: (0, 0, 0, n))
    else:
        shape = (ways, tokens, width)
        out_spec = pl.BlockSpec((ways, tokens, step), lambda n, at: (0, 0, n))
    whole = lambda shape: pl.BlockSpec(shape, lambda n, at: (0,) * len(shape))
    at_piece = lambda i: pl.BlockSpec((3, depth, step), lambda n, at: (0, at[place + i], n))
    gain_piece = lambda i: pl.BlockSpec((1, depth), lambda n, at: (0, at[place + i]))
    out = pl.pallas_call(
        partial(
            temporal_kernel,
            count=count,
            heads=heads,
            tokens=tokens,
            ways=ways,
            slot=slot,
            tiled=tiled,
            pieces=pieces,
            columns=tuple(range(len(arrays))),
        ),
        out_shape=jax.ShapeDtypeStruct(shape, jnp.bfloat16),
        grid_spec=pltpu.PrefetchScalarGridSpec(
            num_scalar_prefetch=1,
            grid=(width // step,),
            in_specs=[whole(x.shape) for x in arrays]
            + [at_piece(i) for i in range(count)]
            + [gain_piece(i) for i in range(count)]
            + [
                pl.BlockSpec((3, rows, step), lambda n, at: (0, 0, n)),
                whole((rows, HEAD)),
            ],
            out_specs=out_spec,
            scratch_shapes=[
                pltpu.VMEM((count, rows, depth), jnp.bfloat16),
                pltpu.VMEM((rows, HEAD), jnp.float32),
            ],
        ),
        cost_estimate=pl.CostEstimate(
            flops=6 * rows * depth * count * width,
            bytes_accessed=6 * depth * count * width + 4 * 3 * rows * width,
            transcendentals=rows * width,
        ),
        compiler_params=pltpu.CompilerParams(vmem_limit_bytes=24 << 20),
        name="temporal",
    )(at, *arrays, *[weight] * count, *[inverse] * count, *carried)
    if not tiled:
        out = out.reshape(ways, frames, slot, width).transpose(1, 0, 2, 3)
    return out


def pack_kernel(at, q, k, v, out):
    for i, ref in enumerate((q, k, v)):
        out[i] = ref[0]


def pack(q, k, v, at, width):
    tokens = q.shape[1]
    count = at.shape[0]
    return pl.pallas_call(
        pack_kernel,
        out_shape=jax.ShapeDtypeStruct((3, tokens, count * width), q.dtype),
        grid_spec=pltpu.PrefetchScalarGridSpec(
            num_scalar_prefetch=1,
            grid=(count,),
            in_specs=[pl.BlockSpec((1, tokens, width), lambda i, at: (0, 0, at[i]))] * 3,
            out_specs=pl.BlockSpec((3, tokens, width), lambda i, at: (0, 0, i)),
        ),
        compiler_params=pltpu.CompilerParams(vmem_limit_bytes=8 << 20),
        name="pack",
    )(at, q, k, v)


def split_kernel(moved, *outs):
    for n, out in enumerate(outs):
        out[...] = moved[..., n * out.shape[-1] : (n + 1) * out.shape[-1]]


def split(moved, count):
    if count == 1:
        return (moved,)
    shape = moved.shape[:-1] + (moved.shape[-1] // count,)
    return pl.pallas_call(
        split_kernel,
        out_shape=(jax.ShapeDtypeStruct(shape, moved.dtype),) * count,
        compiler_params=pltpu.CompilerParams(vmem_limit_bytes=8 << 20),
        name="split",
    )(moved)


def local(spatial_q, spatial_k, spatial_v, norm_gain, temporal_weight):
    frames = lax.axis_size("frame")
    ways = lax.axis_size("row")
    me = lax.axis_index("row").astype(jnp.int32)
    tokens = spatial_q.shape[1]
    slot = tokens // frames
    tiled = slot % 8 == 0
    width = temporal_weight.shape[2]
    group = width // HEAD
    count = chunk_count(group)
    heads = group // count
    depth = heads * HEAD
    weight = jnp.transpose(temporal_weight, (1, 0, 2))
    spatial_q, spatial_k, spatial_v = (
        pltpu.with_memory_space_constraint(x, pltpu.HBM) for x in (spatial_q, spatial_k, spatial_v)
    )
    gain = norm_gain.reshape(1, -1)
    inverse = 1.0 / gain

    def shift(x, k):
        return lax.ppermute(x, "row", [(i, (i + k) % ways) for i in range(ways)])

    chunks = [c for c in (range(0, 1), range(1, count)) if c]
    received = []
    for chunk in chunks:
        parts = []
        for k in range(1, ways):
            at = lax.rem(me + k, ways) * count + jnp.arange(chunk[0], chunk[-1] + 1)
            packed = pack(spatial_q, spatial_k, spatial_v, at.astype(jnp.int32), depth)
            parts.append(shift(packed, k))
        received.append(parts)

    pieces = {}
    for chunk, parts in zip(chunks, received):
        base = (me * group + chunk[0] * heads).reshape(1)
        span = len(chunk) * depth
        out = spatial(
            spatial_q, spatial_k, spatial_v, parts, gain, base, frames, span, heads
        )
        moved = lax.all_to_all(out, "frame", split_axis=0, concat_axis=0, tiled=True)
        for u, part in zip(chunk, split(moved, len(chunk))):
            pieces[u, 0] = (part, 0)
            for k in range(1, ways):
                pieces[u, k] = (shift(part, k), 0)

    other = lambda units: [(u, k) for u in units for k in range(1, ways)]
    last = count - 1
    ready = [(u, 0) for u in range(count)] + other(range(min(1, last)))
    steps = [ready] + [other([u]) for u in range(1, last)] + [other([last])]
    table = [lax.rem(me + ways - k, ways) * count + u for wanted in steps for u, k in wanted]
    table = jnp.stack(table + [me])

    def gather(step):
        listed, arrays = [], []
        for u, k in steps[step]:
            array, column = pieces[u, k]
            if all(array is not x for x in arrays):
                arrays.append(array)
            listed.append(([array is x for x in arrays].index(True), column, k))
        if not tiled:
            arrays = [x.transpose(1, 0, 2, 3).reshape(ways, tokens, -1) for x in arrays]
        return tuple(listed), arrays, table, sum(len(x) for x in steps[:step])

    sizes = dict(tokens=tokens, ways=ways, tiled=tiled)
    carried = None
    for i in range(len(steps) - 1):
        carried = project(*gather(i), weight, inverse, depth, carried, **sizes)
    final = gather(len(steps) - 1)
    out = temporal(*final, weight, inverse, depth, carried, slot=slot, **sizes)
    out = out.reshape(frames * ways, slot, width)
    out = lax.all_to_all(out, ("frame", "row"), split_axis=0, concat_axis=0, tiled=True)
    out = out.reshape(frames, ways, slot, width).transpose(0, 2, 1, 3)
    return out.reshape(1, tokens, ways * width)


def chunk_count(group):
    return 3 if group % 3 == 0 else math.gcd(group, 2)


def solution(mesh):
    return jax.shard_map(
        local,
        mesh=mesh,
        in_specs=(
            P("frame", "row", None),
            P("frame", "row", None),
            P("frame", "row", None),
            P(),
            P(None, None, "row"),
        ),
        out_specs=P("frame", "row", None),
        check_vma=False,
    )
```

```python
import math
from functools import partial

import jax
import jax.numpy as jnp
from jax import lax
from jax.experimental import pallas as pl
from jax.experimental.pallas import tpu as pltpu
from jax.sharding import PartitionSpec as P

D = 3072
HEADS = 24
AGENTS = 128
HEAD = D // HEADS
SCALE = HEAD ** (-0.5)
EXPONENT = SCALE * math.log2(math.e)

epsilon = 1e-06


def dot(left, right):
    return jnp.dot(left, right, preferred_element_type=jnp.float32)


def dot_nt(left, right):
    return lax.dot_general(
        left, right, (((1,), (1,)), ((), ())), preferred_element_type=jnp.float32
    )


def weighted(scores):
    weights = jnp.exp2((scores - jnp.max(scores, axis=1, keepdims=True)) * EXPONENT)
    return weights, 1.0 / jnp.sum(weights, axis=1, keepdims=True)


def spatial_kernel(base, q, k, v, *rest, heads, pool, tiled):
    received, gain, out = rest[:-2], rest[-2], rest[-1]
    ways = len(received) + 1
    tokens = q.shape[1]
    agent = lax.broadcasted_iota(jnp.int32, (tokens // pool, tokens), 0)
    token = lax.broadcasted_iota(jnp.int32, (tokens // pool, tokens), 1)
    member = ((token >= agent * pool) & (token < (agent + 1) * pool)).astype(jnp.bfloat16)
    split = [slice(h * HEAD, (h + 1) * HEAD) for h in range(heads)]
    pooled = [dot(member, block) for block in [q[0]] + [ref[0] for ref in received]]
    pooled = (jnp.concatenate(pooled) * (1.0 / pool)).astype(jnp.bfloat16)
    agents = [pooled[:, cols] for cols in split]
    queries = [jnp.concatenate([q[0, :, cols]] + [r[0, :, cols] for r in received]) for cols in split]
    keys = [jnp.concatenate([k[0, :, cols]] + [r[1, :, cols] for r in received]) for cols in split]
    values = [jnp.concatenate([v[0, :, cols]] + [r[2, :, cols] for r in received]) for cols in split]
    agent_scores = [dot_nt(a, b) for a, b in zip(agents, keys)]
    token_scores = [dot_nt(a, b) for a, b in zip(queries, agents)]
    agent_weights = [weighted(x) for x in agent_scores]
    token_weights = [weighted(x) for x in token_scores]
    agent_values = [
        (dot(w.astype(jnp.bfloat16), x) * r).astype(jnp.bfloat16)
        for (w, r), x in zip(agent_weights, values)
    ]
    results = [dot((w * r).astype(jnp.bfloat16), x) for (w, r), x in zip(token_weights, agent_values)]
    for cols, result in zip(split, results):
        result = (result * gain[:, cols]).astype(jnp.bfloat16)
        for j in range(ways):
            block = result[j * tokens : (j + 1) * tokens]
            if tiled:
                out[:, j, :, cols] = block.reshape(out.shape[0], out.shape[2], HEAD)
            else:
                out[j, :, cols] = block


def spatial(q, k, v, received, gain, base, frames, width, heads):
    tokens = q.shape[1]
    ways = len(received) + 1
    slot = tokens // frames
    pool = tokens * ways // AGENTS
    step = heads * HEAD
    tiled = slot % 8 == 0
    own = pl.BlockSpec((1, tokens, step), lambda i, base: (0, 0, base[0] // heads + i))
    other = pl.BlockSpec((3, tokens, step), lambda i, base: (0, 0, i))
    if tiled:
        shape = (frames, ways, slot, width)
        out_spec = pl.BlockSpec((frames, ways, slot, step), lambda i, base: (0, 0, 0, i))
    else:
        shape = (ways, tokens, width)
        out_spec = pl.BlockSpec((ways, tokens, step), lambda i, base: (0, 0, i))
    out = pl.pallas_call(
        partial(spatial_kernel, heads=heads, pool=pool, tiled=tiled),
        out_shape=jax.ShapeDtypeStruct(shape, jnp.bfloat16),
        grid_spec=pltpu.PrefetchScalarGridSpec(
            num_scalar_prefetch=1,
            grid=(width // step,),
            in_specs=[own] * 3
            + [other] * len(received)
            + [pl.BlockSpec((1, step), lambda i, base: (0, base[0] // heads + i))],
            out_specs=out_spec,
        ),
        cost_estimate=pl.CostEstimate(
            flops=10 * tokens * ways * AGENTS * width,
            bytes_accessed=10 * tokens * ways * width,
            transcendentals=2 * tokens * ways * width,
        ),
        compiler_params=pltpu.CompilerParams(vmem_limit_bytes=12 << 20),
        name="spatial",
    )(base, q, k, v, *received, gain)
    if not tiled:
        out = out.reshape(ways, frames, slot, width).transpose(1, 0, 2, 3)
    return out


def rows_of(ref, block, cols, tokens, tiled):
    if tiled:
        return ref[:, block, :, cols].reshape(tokens, -1)
    return ref[block, :, cols]


def squares(x, inverse):
    y = x.astype(jnp.float32) * inverse
    y = y * y
    total = y[:, :HEAD]
    for at in range(HEAD, y.shape[1], HEAD):
        total = total + y[:, at : at + HEAD]
    return total


VMEM = pl.BlockSpec(memory_space=pltpu.VMEM)
AHEAD = 4


def project_kernel(at, *refs, pieces, arrays, tokens, ways, tiled):
    xs = refs[:arrays]
    weight, gain, acc, ss, kept, held, buffer, sems = refs[arrays:]
    count, _, depth, width = buffer.shape
    copies = []
    for i in range(count + kept.shape[0]):
        rows = pl.ds(pl.multiple_of(at[i] * depth, HEAD), depth)
        target = buffer.at[i] if i < count else kept.at[i - count]
        for c in range(3):
            copies.append(
                pltpu.make_async_copy(weight.at[c, rows, :], target.at[c], sems.at[3 * i + c])
            )
    for copy in copies[:AHEAD]:
        copy.start()
    total = None
    tile = width // 3 if width % 3 == 0 else width
    for i, (which, col, shift) in enumerate(pieces):
        for j in range(ways):
            held[i, j * tokens : (j + 1) * tokens, :] = rows_of(
                xs[which], (j - shift) % ways, slice(col, col + depth), tokens, tiled
            )
        part = squares(held[i], 1.0 / gain[:, pl.ds(pl.multiple_of(at[i] * depth, HEAD), depth)])
        total = part if total is None else total + part
        for c in range(3):
            copies[3 * i + c].wait()
            if 3 * i + c + AHEAD < len(copies):
                copies[3 * i + c + AHEAD].start()
            for n in range(0, width, tile):
                cols = slice(n, n + tile)
                value = dot(held[i], buffer[i, c, :, cols])
                if i == 0:
                    acc[c, :, cols] = value
                else:
                    acc[c, :, cols] += value
    ss[...] = total
    for n in range(3 * count + AHEAD, len(copies)):
        copies[n].start()
    for copy in copies[3 * count :]:
        copy.wait()


def project(pieces, arrays, at, after, weight, gain, depth, tokens, ways, tiled):
    rows = tokens * ways
    width = weight.shape[2]
    count = len(pieces)
    return pl.pallas_call(
        partial(
            project_kernel,
            pieces=pieces,
            arrays=len(arrays),
            tokens=tokens,
            ways=ways,
            tiled=tiled,
        ),
        out_shape=(
            pltpu.VMEM((3, rows, width), jnp.float32),
            pltpu.VMEM((rows, HEAD), jnp.float32),
            pltpu.VMEM((after, 3, depth, width), weight.dtype),
        ),
        grid_spec=pltpu.PrefetchScalarGridSpec(
            num_scalar_prefetch=1,
            grid=(),
            in_specs=[VMEM] * len(arrays) + [pl.BlockSpec(memory_space=pl.ANY), VMEM],
            out_specs=(VMEM, VMEM, VMEM),
            scratch_shapes=[
                pltpu.VMEM((count, rows, depth), jnp.bfloat16),
                pltpu.VMEM((count, 3, depth, width), weight.dtype),
                pltpu.SemaphoreType.DMA((3 * (count + after),)),
            ],
        ),
        cost_estimate=pl.CostEstimate(
            flops=6 * rows * depth * count * width,
            bytes_accessed=6 * depth * (count + after) * width,
            transcendentals=0,
        ),
        compiler_params=pltpu.CompilerParams(vmem_limit_bytes=30 << 20),
        name="project",
    )(at, *arrays, weight, gain)


def temporal_kernel(at, *refs, pieces, arrays, first, heads, tokens, ways, slot, tiled):
    xs = refs[:arrays]
    gain, acc, ss, ws, out, held, rstd = refs[arrays:]
    depth = held.shape[2]
    step = heads * HEAD

    @pl.when(pl.program_id(0) == 0)
    def _():
        total = ss[...]
        for i, (which, col, shift) in enumerate(pieces):
            for j in range(ways):
                held[i, j * tokens : (j + 1) * tokens, :] = rows_of(
                    xs[which], (j - shift) % ways, slice(col, col + depth), tokens, tiled
                )
            lanes = pl.ds(pl.multiple_of(at[first + i] * depth, HEAD), depth)
            total = total + squares(held[i], 1.0 / gain[:, lanes])
        mean = jnp.sum(total, axis=1, keepdims=True) * (1.0 / D)
        rstd[...] = jnp.broadcast_to(lax.rsqrt(mean + epsilon), rstd.shape)

    row = lax.broadcasted_iota(jnp.int32, (tokens, tokens), 0)
    col = lax.broadcasted_iota(jnp.int32, (tokens, tokens), 1)
    same = lax.rem(row, slot) == lax.rem(col, slot)
    part = pl.ds(pl.multiple_of(pl.program_id(0) * step, step), step)
    factor = jnp.concatenate([rstd[...]] * heads, axis=1)
    qkv = []
    for c in range(3):
        value = acc[c, :, part]
        for i in range(len(pieces)):
            value = value + dot(held[i], ws[i, c, :, part])
        qkv.append((value * factor).astype(jnp.bfloat16))
    split = [
        (j, slice(j * tokens, (j + 1) * tokens), slice(h * HEAD, (h + 1) * HEAD))
        for h in range(heads)
        for j in range(ways)
    ]
    scores = [
        jnp.where(same, dot_nt(qkv[0][rows, cols], qkv[1][rows, cols]), -1e30)
        for _, rows, cols in split
    ]
    weights = [weighted(x) for x in scores]
    me = at[first + len(pieces)]
    for (j, rows, cols), (w, r) in zip(split, weights):
        result = dot((w * r).astype(jnp.bfloat16), qkv[2][rows, cols]).astype(jnp.bfloat16)
        target = lax.rem(me + ways - j, ways)
        if tiled:
            out[:, target, :, cols] = result.reshape(out.shape[0], slot, HEAD)
        else:
            out[target, :, cols] = result


def temporal(pieces, arrays, at, first, gain, depth, carried, tokens, ways, slot, tiled):
    rows = tokens * ways
    width = carried[0].shape[2]
    frames = tokens // slot
    heads = math.gcd(width // HEAD, FINAL_HEADS)
    step = heads * HEAD
    if tiled:
        shape = (frames, ways, slot, width)
        out_spec = pl.BlockSpec((frames, ways, slot, step), lambda n, at: (0, 0, 0, n))
    else:
        shape = (ways, tokens, width)
        out_spec = pl.BlockSpec((ways, tokens, step), lambda n, at: (0, 0, n))
    operands = [*arrays, gain, *carried]
    out = pl.pallas_call(
        partial(
            temporal_kernel,
            pieces=pieces,
            arrays=len(arrays),
            first=first,
            heads=heads,
            tokens=tokens,
            ways=ways,
            slot=slot,
            tiled=tiled,
        ),
        out_shape=jax.ShapeDtypeStruct(shape, jnp.bfloat16),
        grid_spec=pltpu.PrefetchScalarGridSpec(
            num_scalar_prefetch=1,
            grid=(width // step,),
            in_specs=[VMEM] * len(operands),
            out_specs=out_spec,
            scratch_shapes=[
                pltpu.VMEM((len(pieces), rows, depth), jnp.bfloat16),
                pltpu.VMEM((rows, HEAD), jnp.float32),
            ],
        ),
        cost_estimate=pl.CostEstimate(
            flops=6 * rows * depth * len(pieces) * width,
            bytes_accessed=2 * rows * width,
            transcendentals=rows * width,
        ),
        compiler_params=pltpu.CompilerParams(vmem_limit_bytes=16 << 20),
        name="temporal",
    )(at, *operands)
    if not tiled:
        out = out.reshape(ways, frames, slot, width).transpose(1, 0, 2, 3)
    return out


FINAL_HEADS = 6


def pack_kernel(at, q, k, v, out):
    for i, ref in enumerate((q, k, v)):
        out[i] = ref[0]


def pack(q, k, v, at, width):
    tokens = q.shape[1]
    count = at.shape[0]
    return pl.pallas_call(
        pack_kernel,
        out_shape=jax.ShapeDtypeStruct((3, tokens, count * width), q.dtype),
        grid_spec=pltpu.PrefetchScalarGridSpec(
            num_scalar_prefetch=1,
            grid=(count,),
            in_specs=[pl.BlockSpec((1, tokens, width), lambda i, at: (0, 0, at[i]))] * 3,
            out_specs=pl.BlockSpec((3, tokens, width), lambda i, at: (0, 0, i)),
        ),
        compiler_params=pltpu.CompilerParams(vmem_limit_bytes=8 << 20),
        name="pack",
    )(at, q, k, v)


def local(spatial_q, spatial_k, spatial_v, norm_gain, temporal_weight):
    frames = lax.axis_size("frame")
    ways = lax.axis_size("row")
    me = lax.axis_index("row").astype(jnp.int32)
    tokens = spatial_q.shape[1]
    slot = tokens // frames
    tiled = slot % 8 == 0
    width = temporal_weight.shape[2]
    group = width // HEAD
    count = chunk_count(group)
    heads = group // count
    depth = heads * HEAD
    weight = pltpu.with_memory_space_constraint(
        jnp.transpose(temporal_weight, (1, 0, 2)), pltpu.HBM
    )
    spatial_q, spatial_k, spatial_v = (
        pltpu.with_memory_space_constraint(x, pltpu.HBM) for x in (spatial_q, spatial_k, spatial_v)
    )
    gain = norm_gain.reshape(1, -1)

    def shift(x, k):
        return lax.ppermute(x, "row", [(i, (i + k) % ways) for i in range(ways)])

    chunks = [c for c in (range(0, 1), range(1, count)) if c]
    received = []
    for chunk in chunks:
        parts = []
        for k in range(1, ways):
            at = lax.rem(me + k, ways) * count + jnp.arange(chunk[0], chunk[-1] + 1)
            packed = pack(spatial_q, spatial_k, spatial_v, at.astype(jnp.int32), depth)
            parts.append(shift(packed, k))
        received.append(parts)

    pieces = {}
    for chunk, parts in zip(chunks, received):
        base = (me * group + chunk[0] * heads).reshape(1)
        span = len(chunk) * depth
        out = spatial(
            spatial_q, spatial_k, spatial_v, parts, gain, base, frames, span, heads
        )
        moved = lax.all_to_all(out, "frame", split_axis=0, concat_axis=0, tiled=True)
        shared = [moved] + [shift(moved, k) for k in range(1, ways)]
        for n, u in enumerate(chunk):
            for k in range(ways):
                pieces[u, k] = (shared[k], n * depth)

    other = lambda units: [(u, k) for u in units for k in range(1, ways)]
    ready = [(u, 0) for u in range(count)] + [key for c in chunks[:-1] for key in other(c)]
    steps = [ready, other(chunks[-1])]
    table = [lax.rem(me + ways - k, ways) * count + u for wanted in steps for u, k in wanted]
    table = jnp.stack(table + [me])

    def gather(step):
        listed, arrays = [], []
        for u, k in steps[step]:
            array, column = pieces[u, k]
            if all(array is not x for x in arrays):
                arrays.append(array)
            listed.append(([array is x for x in arrays].index(True), column, k))
        if not tiled:
            arrays = [x.transpose(1, 0, 2, 3).reshape(ways, tokens, -1) for x in arrays]
        return tuple(listed), arrays, table

    sizes = dict(tokens=tokens, ways=ways, tiled=tiled)
    carried = project(*gather(0), len(steps[1]), weight, gain, depth, **sizes)
    out = temporal(*gather(1), len(ready), gain, depth, carried, slot=slot, **sizes)
    out = out.reshape(frames * ways, slot, width)
    out = lax.all_to_all(out, ("frame", "row"), split_axis=0, concat_axis=0, tiled=True)
    out = out.reshape(frames, ways, slot, width).transpose(0, 2, 1, 3)
    return out.reshape(1, tokens, ways * width)


def chunk_count(group):
    return 3 if group % 3 == 0 else math.gcd(group, 2)


def solution(mesh):
    return jax.shard_map(
        local,
        mesh=mesh,
        in_specs=(
            P("frame", "row", None),
            P("frame", "row", None),
            P("frame", "row", None),
            P(),
            P(None, None, "row"),
        ),
        out_specs=P("frame", "row", None),
        check_vma=False,
    )
```

```python
import math
from functools import partial

import jax
import jax.numpy as jnp
from jax import lax
from jax.experimental import pallas as pl
from jax.experimental.pallas import tpu as pltpu
from jax.sharding import PartitionSpec as P

D = 3072
HEADS = 24
AGENTS = 128
HEAD = D // HEADS
SCALE = HEAD ** (-0.5)
EXPONENT = SCALE * math.log2(math.e)

epsilon = 1e-06


def dot(left, right):
    return jnp.dot(left, right, preferred_element_type=jnp.float32)


def dot_nt(left, right):
    return lax.dot_general(
        left, right, (((1,), (1,)), ((), ())), preferred_element_type=jnp.float32
    )


VMEM = pl.BlockSpec(memory_space=pltpu.VMEM)


def weighted(scores):
    weights = jnp.exp2((scores - jnp.max(scores, axis=1, keepdims=True)) * EXPONENT)
    return weights, 1.0 / jnp.sum(weights, axis=1, keepdims=True)


def spatial_kernel(at, *refs, index, pool, tiled, lines):
    inputs, rest, (own, factor, sems) = refs[:3], refs[3:-3], refs[-3:]
    if lines:
        rest, outs, out, own = rest[: -lines - 1], rest[-lines - 1 : -1], rest[-1], own
        received, gain = rest[:-1], rest[-1]
        frame = at[at.shape[0] - 1]
    else:
        received, gain, out = rest[:-2], rest[-2], rest[-1]
    ways = len(received) + 1
    tokens, width = own.shape[1:]
    lanes = pl.ds(pl.multiple_of(at[index] * HEAD, HEAD), width)
    copies = [
        pltpu.make_async_copy(ref.at[0, :, lanes], own.at[i], sems.at[i])
        for i, ref in enumerate(inputs)
    ]
    copies.append(pltpu.make_async_copy(gain.at[:, lanes], factor, sems.at[3]))
    for copy in copies:
        copy.start()
    agent = lax.broadcasted_iota(jnp.int32, (tokens // pool, tokens), 0)
    token = lax.broadcasted_iota(jnp.int32, (tokens // pool, tokens), 1)
    member = ((token >= agent * pool) & (token < (agent + 1) * pool)).astype(jnp.bfloat16)
    for copy in copies:
        copy.wait()
    blocks = [own, *received]
    for start in range(0, width, TOGETHER * HEAD):
        stop = min(width, start + TOGETHER * HEAD)
        pooled = [dot(member, ref[0, :, start:stop]) for ref in blocks]
        pooled = (jnp.concatenate(pooled) * (1.0 / pool)).astype(jnp.bfloat16)
        split = [slice(n, n + HEAD) for n in range(start, stop, HEAD)]
        agents = [pooled[:, n.start - start : n.stop - start] for n in split]
        queries, keys, values = (
            [jnp.concatenate([ref[i, :, cols] for ref in blocks]) for cols in split]
            for i in range(3)
        )
        agent_scores = [dot_nt(a, b) for a, b in zip(agents, keys)]
        token_scores = [dot_nt(a, b) for a, b in zip(queries, agents)]
        agent_weights = [weighted(x) for x in agent_scores]
        token_weights = [weighted(x) for x in token_scores]
        agent_values = [
            (dot(w.astype(jnp.bfloat16), x) * r).astype(jnp.bfloat16)
            for (w, r), x in zip(agent_weights, values)
        ]
        results = [
            dot((w * r).astype(jnp.bfloat16), x) for (w, r), x in zip(token_weights, agent_values)
        ]
        for cols, result in zip(split, results):
            result = (result * factor[:, cols]).astype(jnp.bfloat16)
            for j in range(ways):
                block = result[j * tokens : (j + 1) * tokens]
                if lines:
                    slot = out.shape[2]
                    for f in range(out.shape[0]):
                        out[f ^ frame, j, :, cols] = block[f * slot : (f + 1) * slot]
                elif tiled:
                    out[:, j, :, cols] = block.reshape(out.shape[0], out.shape[2], HEAD)
                else:
                    out[j, :, cols] = block
    if lines:
        for n, target in enumerate(outs):
            size = target.shape[0]
            target[...] = out[n * size : (n + 1) * size]


TOGETHER = 4


def spatial(q, k, v, received, gain, at, index, frames, lines=0):
    tokens = q.shape[1]
    width = received[0].shape[2] if received else q.shape[2]
    ways = len(received) + 1
    slot = tokens // frames
    tiled = slot % 8 == 0
    shape = (frames, ways, slot, width) if tiled else (ways, tokens, width)
    hbm = pl.BlockSpec(memory_space=pl.ANY)
    out = pl.pallas_call(
        partial(
            spatial_kernel, index=index, pool=tokens * ways // AGENTS, tiled=tiled, lines=lines
        ),
        out_shape=(
            [jax.ShapeDtypeStruct((frames // lines, *shape[1:]), jnp.bfloat16)] * lines
            if lines
            else jax.ShapeDtypeStruct(shape, jnp.bfloat16)
        ),
        grid_spec=pltpu.PrefetchScalarGridSpec(
            num_scalar_prefetch=1,
            grid=(),
            in_specs=[hbm] * 3 + [VMEM] * len(received) + [hbm],
            out_specs=[VMEM] * lines if lines else VMEM,
            scratch_shapes=([pltpu.VMEM(shape, jnp.bfloat16)] if lines else [])
            + [
                pltpu.VMEM((3, tokens, width), jnp.bfloat16),
                pltpu.VMEM((1, width), jnp.float32),
                pltpu.SemaphoreType.DMA((4,)),
            ],
        ),
        cost_estimate=pl.CostEstimate(
            flops=10 * tokens * ways * AGENTS * width,
            bytes_accessed=10 * tokens * ways * width,
            transcendentals=2 * tokens * ways * width,
        ),
        compiler_params=pltpu.CompilerParams(vmem_limit_bytes=16 << 20),
        name="spatial",
    )(at, q, k, v, *received, gain)
    if not tiled and not lines:
        out = out.reshape(ways, frames, slot, width).transpose(1, 0, 2, 3)
    return out


def rows_of(ref, block, tokens, tiled):
    if tiled:
        return ref[:, block, :, :].reshape(tokens, -1)
    return ref[block]


def squares(x, inverse):
    y = x.astype(jnp.float32) * inverse
    y = y * y
    total = y[:, :HEAD]
    for at in range(HEAD, y.shape[1], HEAD):
        total = total + y[:, at : at + HEAD]
    return total


AHEAD = 4


def hold(held, xs, depths, shifts, tokens, ways, tiled):
    column = 0
    for x, depth, shift in zip(xs, depths, shifts):
        for j in range(ways):
            held[j * tokens : (j + 1) * tokens, column : column + depth] = rows_of(
                x, (j - shift) % ways, tokens, tiled
            )
        column += depth


def project_kernel(at, *refs, groups, shifts, depths, tokens, ways, tiled):
    xs = refs[: len(shifts)]
    weight, gain, acc, ss = refs[len(shifts) : len(shifts) + 4]
    rest = refs[len(shifts) + 4 :]
    kept = rest[: len(groups) - sum(g is not None for g in groups)]
    sems = rest[-1]
    used = [g for g in groups if g is not None]
    scratch = rest[len(kept) : -1]
    held, buffers = scratch[: len(used)], scratch[len(used) :]
    targets = [*buffers, *kept]
    copies = []
    for i, target in enumerate(targets):
        rows = pl.ds(pl.multiple_of(at[i] * HEAD, HEAD), target.shape[1])
        for c in range(3):
            copies.append(
                pltpu.make_async_copy(weight.at[c, rows, :], target.at[c], sems.at[3 * i + c])
            )
    for copy in copies[:AHEAD]:
        copy.start()
    width = weight.shape[2]
    tile = width // 3 if width % 3 == 0 else width
    total = None
    for i, members in enumerate(used):
        hold(
            held[i],
            [xs[m] for m in members],
            [depths[m] for m in members],
            [shifts[m] for m in members],
            tokens,
            ways,
            tiled,
        )
        lanes = pl.ds(pl.multiple_of(at[i] * HEAD, HEAD), held[i].shape[1])
        part = squares(held[i][...], 1.0 / gain[:, lanes])
        total = part if total is None else total + part
        for c in range(3):
            copies[3 * i + c].wait()
            if 3 * i + c + AHEAD < len(copies):
                copies[3 * i + c + AHEAD].start()
            for n in range(0, width, tile):
                cols = slice(n, n + tile)
                value = dot(held[i][...], buffers[i][c, :, cols])
                if i == 0:
                    acc[c, :, cols] = value
                else:
                    acc[c, :, cols] += value
    ss[...] = total
    for n in range(3 * len(used) + AHEAD, len(copies)):
        copies[n].start()
    for copy in copies[3 * len(used) :]:
        copy.wait()


def project(groups, arrays, shifts, at, later, weight, gain, tokens, ways, tiled):
    rows = tokens * ways
    width = weight.shape[2]
    depths = [x.shape[-1] for x in arrays]
    sums = [sum(depths[m] for m in g) for g in groups]
    return pl.pallas_call(
        partial(
            project_kernel,
            groups=(*groups, *[None] * len(later)),
            shifts=shifts,
            depths=depths,
            tokens=tokens,
            ways=ways,
            tiled=tiled,
        ),
        out_shape=(
            pltpu.VMEM((3, rows, width), jnp.float32),
            pltpu.VMEM((rows, HEAD), jnp.float32),
            *[pltpu.VMEM((3, depth, width), weight.dtype) for depth in later],
        ),
        grid_spec=pltpu.PrefetchScalarGridSpec(
            num_scalar_prefetch=1,
            grid=(),
            in_specs=[VMEM] * len(arrays) + [pl.BlockSpec(memory_space=pl.ANY), VMEM],
            out_specs=(VMEM,) * (2 + len(later)),
            scratch_shapes=[pltpu.VMEM((rows, depth), jnp.bfloat16) for depth in sums]
            + [pltpu.VMEM((3, depth, width), weight.dtype) for depth in sums]
            + [pltpu.SemaphoreType.DMA((3 * (len(sums) + len(later)),))],
        ),
        cost_estimate=pl.CostEstimate(
            flops=6 * rows * sum(sums) * width,
            bytes_accessed=6 * (sum(sums) + sum(later)) * width,
            transcendentals=0,
        ),
        compiler_params=pltpu.CompilerParams(vmem_limit_bytes=32 << 20),
        name="project",
    )(at, *arrays, weight, gain)


def temporal_kernel(at, *refs, first, shifts, heads, tokens, ways, slot, tiled):
    count = len(shifts)
    xs = refs[:count]
    gain, acc, ss = refs[count : count + 3]
    ws = refs[count + 3 : 2 * count + 3]
    out, *held, rstd = refs[2 * count + 3 :]
    step = heads * HEAD

    @pl.when(pl.program_id(0) == 0)
    def _():
        total = ss[...]
        for i in range(count):
            depth = ws[i].shape[1]
            hold(held[i], [xs[i]], [depth], [shifts[i]], tokens, ways, tiled)
            lanes = pl.ds(pl.multiple_of(at[first + i] * HEAD, HEAD), depth)
            total = total + squares(held[i][...], 1.0 / gain[:, lanes])
        mean = jnp.sum(total, axis=1, keepdims=True) * (1.0 / D)
        rstd[...] = jnp.broadcast_to(lax.rsqrt(mean + epsilon), rstd.shape)

    row = lax.broadcasted_iota(jnp.int32, (tokens, tokens), 0)
    col = lax.broadcasted_iota(jnp.int32, (tokens, tokens), 1)
    same = lax.rem(row, slot) == lax.rem(col, slot)
    part = pl.ds(pl.multiple_of(pl.program_id(0) * step, step), step)
    factor = jnp.concatenate([rstd[...]] * heads, axis=1)
    qkv = []
    for c in range(3):
        value = acc[c, :, part]
        for i in range(count):
            value = value + dot(held[i][...], ws[i][c, :, part])
        qkv.append((value * factor).astype(jnp.bfloat16))
    split = [
        (j, slice(j * tokens, (j + 1) * tokens), slice(h * HEAD, (h + 1) * HEAD))
        for h in range(heads)
        for j in range(ways)
    ]
    scores = [
        jnp.where(same, dot_nt(qkv[0][rows, cols], qkv[1][rows, cols]), -1e30)
        for _, rows, cols in split
    ]
    weights = [weighted(x) for x in scores]
    me = at[first + count]
    for (j, rows, cols), (w, r) in zip(split, weights):
        result = dot((w * r).astype(jnp.bfloat16), qkv[2][rows, cols]).astype(jnp.bfloat16)
        target = lax.rem(me + ways - j, ways)
        if tiled:
            out[:, target, :, cols] = result.reshape(out.shape[0], slot, HEAD)
        else:
            out[target, :, cols] = result


def temporal(arrays, shifts, at, first, gain, carried, tokens, ways, slot, tiled):
    rows = tokens * ways
    width = carried[0].shape[2]
    depths = [x.shape[-1] for x in arrays]
    frames = tokens // slot
    heads = math.gcd(width // HEAD, FINAL_HEADS)
    step = heads * HEAD
    if tiled:
        shape = (frames, ways, slot, width)
        out_spec = pl.BlockSpec((frames, ways, slot, step), lambda n, at: (0, 0, 0, n))
    else:
        shape = (ways, tokens, width)
        out_spec = pl.BlockSpec((ways, tokens, step), lambda n, at: (0, 0, n))
    operands = [*arrays, gain, *carried]
    out = pl.pallas_call(
        partial(
            temporal_kernel,
            first=first,
            shifts=shifts,
            heads=heads,
            tokens=tokens,
            ways=ways,
            slot=slot,
            tiled=tiled,
        ),
        out_shape=jax.ShapeDtypeStruct(shape, jnp.bfloat16),
        grid_spec=pltpu.PrefetchScalarGridSpec(
            num_scalar_prefetch=1,
            grid=(width // step,),
            in_specs=[VMEM] * len(operands),
            out_specs=out_spec,
            scratch_shapes=[pltpu.VMEM((rows, depth), jnp.bfloat16) for depth in depths]
            + [pltpu.VMEM((rows, HEAD), jnp.float32)],
        ),
        cost_estimate=pl.CostEstimate(
            flops=6 * rows * sum(depths) * width,
            bytes_accessed=2 * rows * width,
            transcendentals=rows * width,
        ),
        compiler_params=pltpu.CompilerParams(vmem_limit_bytes=16 << 20),
        name="temporal",
    )(at, *operands)
    if not tiled:
        out = out.reshape(ways, frames, slot, width).transpose(1, 0, 2, 3)
    return out


FINAL_HEADS = 6


def pack_kernel(at, q, k, v, out, sems, *, index):
    lanes = pl.ds(pl.multiple_of(at[index] * HEAD, HEAD), out.shape[2])
    copies = [
        pltpu.make_async_copy(ref.at[0, :, lanes], out.at[i], sems.at[i])
        for i, ref in enumerate((q, k, v))
    ]
    for copy in copies:
        copy.start()
    for copy in copies:
        copy.wait()


def pack(q, k, v, at, index, width):
    return pl.pallas_call(
        partial(pack_kernel, index=index),
        out_shape=pltpu.VMEM((3, q.shape[1], width), q.dtype),
        grid_spec=pltpu.PrefetchScalarGridSpec(
            num_scalar_prefetch=1,
            grid=(),
            in_specs=[pl.BlockSpec(memory_space=pl.ANY)] * 3,
            out_specs=VMEM,
            scratch_shapes=[pltpu.SemaphoreType.DMA((3,))],
        ),
        compiler_params=pltpu.CompilerParams(vmem_limit_bytes=8 << 20),
        name="pack",
    )(at, q, k, v)


def collect_kernel(*refs, picks):
    out = refs[-1]
    for n, (which, block) in enumerate(picks):
        out[n] = refs[which][block]


def collect(parts, picks):
    return pl.pallas_call(
        partial(collect_kernel, picks=tuple(picks)),
        out_shape=jax.ShapeDtypeStruct((len(picks), *parts[0].shape[1:]), parts[0].dtype),
        in_specs=[VMEM] * len(parts),
        out_specs=VMEM,
        compiler_params=pltpu.CompilerParams(vmem_limit_bytes=8 << 20),
        name="collect",
    )(*parts)


def assemble_kernel(at, *refs, places):
    out = refs[-1]
    frame = at[at.shape[0] - 1]
    for ref, keys in zip(refs[:-1], places):
        for n, key in enumerate(keys):
            if key is not None:
                out[key ^ frame] = ref[n]


def assemble(parts, places, at):
    count = sum(key is not None for keys in places for key in keys)
    return pl.pallas_call(
        partial(assemble_kernel, places=places),
        out_shape=jax.ShapeDtypeStruct((count, *parts[0].shape[1:]), parts[0].dtype),
        grid_spec=pltpu.PrefetchScalarGridSpec(
            num_scalar_prefetch=1,
            grid=(),
            in_specs=[VMEM] * len(parts),
            out_specs=VMEM,
        ),
        compiler_params=pltpu.CompilerParams(vmem_limit_bytes=8 << 20),
        name="assemble",
    )(at, *parts)


def stages(frames):
    pair = 2
    line = min(4, frames // pair)
    return line, frames // (line * pair), pair


def spread_by_permutes(outs, at, frames):
    line, side, pair = stages(frames)
    rest = side * pair

    def swap(x, key):
        return lax.ppermute(x, "frame", [(i, i ^ key) for i in range(frames)])

    lined = {0: outs[0]}
    for a in range(line - 1, 0, -1):
        lined[a] = swap(outs[a], a * rest)
    sided = {}
    for b in range(1, side):
        picks = [(a, b * pair + c) for a in range(line) for c in range(pair)]
        sided[b] = swap(collect([lined[a] for a in range(line)], picks), b * pair)
    parts = [lined[a] for a in range(line)] + [sided[b] for b in range(1, side)]
    picks = [(a, 1) for a in range(line)]
    picks += [(line + b - 1, a * pair + 1) for b in range(1, side) for a in range(line)]
    parts.append(swap(collect(parts, picks), 1))
    places = [(a * rest,) + (None,) * (rest - 1) for a in range(line)]
    places += [
        tuple(
            a * rest + b * pair if c == 0 else None for a in range(line) for c in range(pair)
        )
        for b in range(1, side)
    ]
    places.append(tuple(a * rest + b * pair + 1 for b in range(side) for a in range(line)))
    return assemble(parts, tuple(places), at)


def local(spatial_q, spatial_k, spatial_v, norm_gain, temporal_weight):
    frames = lax.axis_size("frame")
    ways = lax.axis_size("row")
    me = lax.axis_index("row").astype(jnp.int32)
    tokens = spatial_q.shape[1]
    slot = tokens // frames
    tiled = slot % 8 == 0
    width = temporal_weight.shape[2]
    group = width // HEAD
    hbm = lambda x: pltpu.with_memory_space_constraint(x, pltpu.HBM)
    weight = hbm(jnp.transpose(temporal_weight, (1, 0, 2)))
    spatial_q, spatial_k, spatial_v = (hbm(x) for x in (spatial_q, spatial_k, spatial_v))
    gain = norm_gain.reshape(1, -1)

    staged = three_chunks(group, ways, frames, slot)
    if staged:
        sizes = MIXED if group == sum(MIXED) else (group // 3, group // 3, group - 2 * (group // 3))
    else:
        first = max(1, group * 5 // 12)
        sizes = (first, group - first) if group > 1 else (1,)
    chunks = [(sum(sizes[:i]), size) for i, size in enumerate(sizes)]
    last = len(chunks) - 1
    behind = [lax.rem(me + ways - k, ways) * group + c for c, _ in chunks for k in range(ways)]
    ahead = [lax.rem(me + k, ways) * group + c for c, _ in chunks for k in range(ways)]
    table = jnp.stack(behind + ahead + [me, lax.axis_index("frame").astype(jnp.int32)])

    def shift(x, k):
        return lax.ppermute(x, "row", [(i, (i + k) % ways) for i in range(ways)])

    received = []
    for i, (_, size) in enumerate(chunks):
        parts = []
        for k in range(1, ways):
            index = len(behind) + i * ways + k
            packed = pack(spatial_q, spatial_k, spatial_v, table, index, size * HEAD)
            parts.append(shift(packed, k))
        received.append(parts)

    pieces = {}
    for i, parts in enumerate(received):
        lines = stages(frames)[0] if staged and i == 1 else 0
        out = spatial(
            spatial_q, spatial_k, spatial_v, parts, hbm(gain), table, i * ways, frames, lines
        )
        if lines:
            pieces[i, 0] = spread_by_permutes(out, table, frames)
        else:
            out = lax.all_to_all(out, "frame", split_axis=0, concat_axis=0, tiled=True)
            pieces[i, 0] = out
        for k in range(1, ways):
            pieces[i, k] = shift(pieces[i, 0], k)
    if not tiled:
        flat = lambda x: x.transpose(1, 0, 2, 3).reshape(ways, tokens, -1)
        pieces = {key: flat(x) for key, x in pieces.items()}

    early = [[(0, k)] for k in range(1, ways)] if last else []
    early.append([(i, 0) for i in range(last + 1)])
    final = [(i, k) for i in range(min(1, last), last + 1) for k in range(1, ways)]
    order = [g[0] for g in early] + final
    at = jnp.stack([behind[i * ways + k] for i, k in order] + [me])
    flat = [key for g in early for key in g]
    groups = tuple(tuple(flat.index(key) for key in g) for g in early)
    shared = dict(tokens=tokens, ways=ways, tiled=tiled)
    carried = project(
        groups,
        [pieces[key] for key in flat],
        tuple(k for _, k in flat),
        at,
        [chunks[i][1] * HEAD for i, _ in final],
        weight,
        gain,
        **shared,
    )
    arrays, shifts = [pieces[key] for key in final], tuple(k for _, k in final)
    out = temporal(arrays, shifts, at, len(early), gain, carried, slot=slot, **shared)
    out = out.reshape(frames * ways, slot, width)
    out = lax.all_to_all(out, ("frame", "row"), split_axis=0, concat_axis=0, tiled=True)
    out = out.reshape(frames, ways, slot, width).transpose(0, 2, 1, 3)
    return out.reshape(1, tokens, ways * width)


MIXED = (4, 4, 4)


def three_chunks(group, ways, frames, slot):
    return group >= 3 and ways == 2 and frames & (frames - 1) == 0 and slot % 8 == 0 and frames > 2


def solution(mesh):
    return jax.shard_map(
        local,
        mesh=mesh,
        in_specs=(
            P("frame", "row", None),
            P("frame", "row", None),
            P("frame", "row", None),
            P(),
            P(None, None, "row"),
        ),
        out_specs=P("frame", "row", None),
        check_vma=False,
    )
```

```python
import math
from functools import partial

import jax
import jax.numpy as jnp
from jax import lax
from jax.experimental import pallas as pl
from jax.experimental.pallas import tpu as pltpu
from jax.sharding import PartitionSpec as P

D = 3072
HEADS = 24
AGENTS = 128
HEAD = D // HEADS
SCALE = HEAD ** (-0.5)
EXPONENT = SCALE * math.log2(math.e)

epsilon = 1e-06


def dot(left, right):
    return jnp.dot(left, right, preferred_element_type=jnp.float32)


def dot_nt(left, right):
    return lax.dot_general(
        left, right, (((1,), (1,)), ((), ())), preferred_element_type=jnp.float32
    )


VMEM = pl.BlockSpec(memory_space=pltpu.VMEM)


def weighted(scores):
    weights = jnp.exp2((scores - jnp.max(scores, axis=1, keepdims=True)) * EXPONENT)
    return weights, 1.0 / jnp.sum(weights, axis=1, keepdims=True)


def spatial_kernel(at, *refs, index, pool, tiled, lines):
    inputs, rest, (own, factor, sems) = refs[:3], refs[3:-3], refs[-3:]
    if lines:
        rest, outs, out, own = rest[: -lines - 1], rest[-lines - 1 : -1], rest[-1], own
        received, gain = rest[:-1], rest[-1]
        frame = at[at.shape[0] - 1]
    else:
        received, gain, out = rest[:-2], rest[-2], rest[-1]
    ways = len(received) + 1
    tokens, width = own.shape[1:]
    lanes = pl.ds(pl.multiple_of(at[index] * HEAD, HEAD), width)
    copies = [
        pltpu.make_async_copy(ref.at[0, :, lanes], own.at[i], sems.at[i])
        for i, ref in enumerate(inputs)
    ]
    copies.append(pltpu.make_async_copy(gain.at[:, lanes], factor, sems.at[3]))
    for copy in copies:
        copy.start()
    agent = lax.broadcasted_iota(jnp.int32, (tokens // pool, tokens), 0)
    token = lax.broadcasted_iota(jnp.int32, (tokens // pool, tokens), 1)
    member = ((token >= agent * pool) & (token < (agent + 1) * pool)).astype(jnp.bfloat16)
    for copy in copies:
        copy.wait()
    blocks = [own, *received]
    for start in range(0, width, TOGETHER * HEAD):
        stop = min(width, start + TOGETHER * HEAD)
        pooled = [dot(member, ref[0, :, start:stop]) for ref in blocks]
        pooled = (jnp.concatenate(pooled) * (1.0 / pool)).astype(jnp.bfloat16)
        split = [slice(n, n + HEAD) for n in range(start, stop, HEAD)]
        agents = [pooled[:, n.start - start : n.stop - start] for n in split]
        queries, keys, values = (
            [jnp.concatenate([ref[i, :, cols] for ref in blocks]) for cols in split]
            for i in range(3)
        )
        agent_scores = [dot_nt(a, b) for a, b in zip(agents, keys)]
        token_scores = [dot_nt(a, b) for a, b in zip(queries, agents)]
        agent_weights = [weighted(x) for x in agent_scores]
        token_weights = [weighted(x) for x in token_scores]
        agent_values = [
            (dot(w.astype(jnp.bfloat16), x) * r).astype(jnp.bfloat16)
            for (w, r), x in zip(agent_weights, values)
        ]
        results = [
            dot((w * r).astype(jnp.bfloat16), x) for (w, r), x in zip(token_weights, agent_values)
        ]
        for cols, result in zip(split, results):
            result = (result * factor[:, cols]).astype(jnp.bfloat16)
            for j in range(ways):
                block = result[j * tokens : (j + 1) * tokens]
                if lines:
                    slot = out.shape[2]
                    for f in range(out.shape[0]):
                        out[f ^ frame, j, :, cols] = block[f * slot : (f + 1) * slot]
                elif tiled:
                    out[:, j, :, cols] = block.reshape(out.shape[0], out.shape[2], HEAD)
                else:
                    out[j, :, cols] = block
    if lines:
        for n, target in enumerate(outs):
            size = target.shape[0]
            target[...] = out[n * size : (n + 1) * size]


TOGETHER = 3


def spatial(q, k, v, received, gain, at, index, frames, lines=0):
    tokens = q.shape[1]
    width = received[0].shape[2] if received else q.shape[2]
    ways = len(received) + 1
    slot = tokens // frames
    tiled = slot % 8 == 0
    shape = (frames, ways, slot, width) if tiled else (ways, tokens, width)
    hbm = pl.BlockSpec(memory_space=pl.ANY)
    out = pl.pallas_call(
        partial(
            spatial_kernel, index=index, pool=tokens * ways // AGENTS, tiled=tiled, lines=lines
        ),
        out_shape=(
            [jax.ShapeDtypeStruct((frames // lines, *shape[1:]), jnp.bfloat16)] * lines
            if lines
            else jax.ShapeDtypeStruct(shape, jnp.bfloat16)
        ),
        grid_spec=pltpu.PrefetchScalarGridSpec(
            num_scalar_prefetch=1,
            grid=(),
            in_specs=[hbm] * 3 + [VMEM] * len(received) + [hbm],
            out_specs=[VMEM] * lines if lines else VMEM,
            scratch_shapes=([pltpu.VMEM(shape, jnp.bfloat16)] if lines else [])
            + [
                pltpu.VMEM((3, tokens, width), jnp.bfloat16),
                pltpu.VMEM((1, width), jnp.float32),
                pltpu.SemaphoreType.DMA((4,)),
            ],
        ),
        cost_estimate=pl.CostEstimate(
            flops=10 * tokens * ways * AGENTS * width,
            bytes_accessed=10 * tokens * ways * width,
            transcendentals=2 * tokens * ways * width,
        ),
        compiler_params=pltpu.CompilerParams(vmem_limit_bytes=16 << 20),
        name="spatial",
    )(at, q, k, v, *received, gain)
    if not tiled and not lines:
        out = out.reshape(ways, frames, slot, width).transpose(1, 0, 2, 3)
    return out


def rows_of(ref, block, tokens, tiled):
    if tiled:
        return ref[:, block, :, :].reshape(tokens, -1)
    return ref[block]


def squares(x, inverse):
    y = x.astype(jnp.float32) * inverse
    y = y * y
    total = y[:, :HEAD]
    for at in range(HEAD, y.shape[1], HEAD):
        total = total + y[:, at : at + HEAD]
    return total


AHEAD = 4


def hold(held, xs, depths, shifts, tokens, ways, tiled):
    column = 0
    for x, depth, shift in zip(xs, depths, shifts):
        for j in range(ways):
            held[j * tokens : (j + 1) * tokens, column : column + depth] = rows_of(
                x, (j - shift) % ways, tokens, tiled
            )
        column += depth


def project_kernel(at, *refs, groups, shifts, depths, tokens, ways, tiled):
    xs = refs[: len(shifts)]
    weight, gain, acc, ss = refs[len(shifts) : len(shifts) + 4]
    rest = refs[len(shifts) + 4 :]
    kept = rest[: len(groups) - sum(g is not None for g in groups)]
    sems = rest[-1]
    used = [g for g in groups if g is not None]
    scratch = rest[len(kept) : -1]
    held, buffers = scratch[: len(used)], scratch[len(used) :]
    targets = [*buffers, *kept]
    copies = []
    for i, target in enumerate(targets):
        rows = pl.ds(pl.multiple_of(at[i] * HEAD, HEAD), target.shape[1])
        for c in range(3):
            copies.append(
                pltpu.make_async_copy(weight.at[c, rows, :], target.at[c], sems.at[3 * i + c])
            )
    for copy in copies[:AHEAD]:
        copy.start()
    width = weight.shape[2]
    tile = width // 3 if width % 3 == 0 else width
    total = None
    for i, members in enumerate(used):
        hold(
            held[i],
            [xs[m] for m in members],
            [depths[m] for m in members],
            [shifts[m] for m in members],
            tokens,
            ways,
            tiled,
        )
        lanes = pl.ds(pl.multiple_of(at[i] * HEAD, HEAD), held[i].shape[1])
        part = squares(held[i][...], 1.0 / gain[:, lanes])
        total = part if total is None else total + part
        for c in range(3):
            copies[3 * i + c].wait()
            if 3 * i + c + AHEAD < len(copies):
                copies[3 * i + c + AHEAD].start()
            for n in range(0, width, tile):
                cols = slice(n, n + tile)
                value = dot(held[i][...], buffers[i][c, :, cols])
                if i == 0:
                    acc[c, :, cols] = value
                else:
                    acc[c, :, cols] += value
    ss[...] = total
    for n in range(3 * len(used) + AHEAD, len(copies)):
        copies[n].start()
    for copy in copies[3 * len(used) :]:
        copy.wait()


def project(groups, arrays, shifts, at, later, weight, gain, tokens, ways, tiled):
    rows = tokens * ways
    width = weight.shape[2]
    depths = [x.shape[-1] for x in arrays]
    sums = [sum(depths[m] for m in g) for g in groups]
    return pl.pallas_call(
        partial(
            project_kernel,
            groups=(*groups, *[None] * len(later)),
            shifts=shifts,
            depths=depths,
            tokens=tokens,
            ways=ways,
            tiled=tiled,
        ),
        out_shape=(
            pltpu.VMEM((3, rows, width), jnp.float32),
            pltpu.VMEM((rows, HEAD), jnp.float32),
            *[pltpu.VMEM((3, depth, width), weight.dtype) for depth in later],
        ),
        grid_spec=pltpu.PrefetchScalarGridSpec(
            num_scalar_prefetch=1,
            grid=(),
            in_specs=[VMEM] * len(arrays) + [pl.BlockSpec(memory_space=pl.ANY), VMEM],
            out_specs=(VMEM,) * (2 + len(later)),
            scratch_shapes=[pltpu.VMEM((rows, depth), jnp.bfloat16) for depth in sums]
            + [pltpu.VMEM((3, depth, width), weight.dtype) for depth in sums]
            + [pltpu.SemaphoreType.DMA((3 * (len(sums) + len(later)),))],
        ),
        cost_estimate=pl.CostEstimate(
            flops=6 * rows * sum(sums) * width,
            bytes_accessed=6 * (sum(sums) + sum(later)) * width,
            transcendentals=0,
        ),
        compiler_params=pltpu.CompilerParams(vmem_limit_bytes=32 << 20),
        name="project",
    )(at, *arrays, weight, gain)


def temporal_kernel(at, *refs, first, shifts, heads, tokens, ways, slot, tiled):
    count = len(shifts)
    xs = refs[:count]
    gain, acc, ss = refs[count : count + 3]
    ws = refs[count + 3 : 2 * count + 3]
    out, *held, rstd = refs[2 * count + 3 :]
    step = heads * HEAD

    @pl.when(pl.program_id(0) == 0)
    def _():
        total = ss[...]
        for i in range(count):
            depth = ws[i].shape[1]
            hold(held[i], [xs[i]], [depth], [shifts[i]], tokens, ways, tiled)
            lanes = pl.ds(pl.multiple_of(at[first + i] * HEAD, HEAD), depth)
            total = total + squares(held[i][...], 1.0 / gain[:, lanes])
        mean = jnp.sum(total, axis=1, keepdims=True) * (1.0 / D)
        rstd[...] = jnp.broadcast_to(lax.rsqrt(mean + epsilon), rstd.shape)

    row = lax.broadcasted_iota(jnp.int32, (tokens, tokens), 0)
    col = lax.broadcasted_iota(jnp.int32, (tokens, tokens), 1)
    same = lax.rem(row, slot) == lax.rem(col, slot)
    part = pl.ds(pl.multiple_of(pl.program_id(0) * step, step), step)
    factor = jnp.concatenate([rstd[...]] * heads, axis=1)
    qkv = []
    for c in range(3):
        value = acc[c, :, part]
        for i in range(count):
            value = value + dot(held[i][...], ws[i][c, :, part])
        qkv.append((value * factor).astype(jnp.bfloat16))
    split = [
        (j, slice(j * tokens, (j + 1) * tokens), slice(h * HEAD, (h + 1) * HEAD))
        for h in range(heads)
        for j in range(ways)
    ]
    scores = [
        jnp.where(same, dot_nt(qkv[0][rows, cols], qkv[1][rows, cols]), -1e30)
        for _, rows, cols in split
    ]
    weights = [weighted(x) for x in scores]
    me = at[first + count]
    for (j, rows, cols), (w, r) in zip(split, weights):
        result = dot((w * r).astype(jnp.bfloat16), qkv[2][rows, cols]).astype(jnp.bfloat16)
        target = lax.rem(me + ways - j, ways)
        if tiled:
            out[:, target, :, cols] = result.reshape(out.shape[0], slot, HEAD)
        else:
            out[target, :, cols] = result


def temporal(arrays, shifts, at, first, gain, carried, tokens, ways, slot, tiled):
    rows = tokens * ways
    width = carried[0].shape[2]
    depths = [x.shape[-1] for x in arrays]
    frames = tokens // slot
    heads = math.gcd(width // HEAD, FINAL_HEADS)
    step = heads * HEAD
    if tiled:
        shape = (frames, ways, slot, width)
        out_spec = pl.BlockSpec((frames, ways, slot, step), lambda n, at: (0, 0, 0, n))
    else:
        shape = (ways, tokens, width)
        out_spec = pl.BlockSpec((ways, tokens, step), lambda n, at: (0, 0, n))
    operands = [*arrays, gain, *carried]
    out = pl.pallas_call(
        partial(
            temporal_kernel,
            first=first,
            shifts=shifts,
            heads=heads,
            tokens=tokens,
            ways=ways,
            slot=slot,
            tiled=tiled,
        ),
        out_shape=jax.ShapeDtypeStruct(shape, jnp.bfloat16),
        grid_spec=pltpu.PrefetchScalarGridSpec(
            num_scalar_prefetch=1,
            grid=(width // step,),
            in_specs=[VMEM] * len(operands),
            out_specs=out_spec,
            scratch_shapes=[pltpu.VMEM((rows, depth), jnp.bfloat16) for depth in depths]
            + [pltpu.VMEM((rows, HEAD), jnp.float32)],
        ),
        cost_estimate=pl.CostEstimate(
            flops=6 * rows * sum(depths) * width,
            bytes_accessed=2 * rows * width,
            transcendentals=rows * width,
        ),
        compiler_params=pltpu.CompilerParams(vmem_limit_bytes=16 << 20),
        name="temporal",
    )(at, *operands)
    if not tiled:
        out = out.reshape(ways, frames, slot, width).transpose(1, 0, 2, 3)
    return out


FINAL_HEADS = 6


def pack_kernel(at, q, k, v, out, sems, *, index):
    lanes = pl.ds(pl.multiple_of(at[index] * HEAD, HEAD), out.shape[2])
    copies = [
        pltpu.make_async_copy(ref.at[0, :, lanes], out.at[i], sems.at[i])
        for i, ref in enumerate((q, k, v))
    ]
    for copy in copies:
        copy.start()
    for copy in copies:
        copy.wait()


def pack_blocks_kernel(at, q, k, v, out):
    for i, ref in enumerate((q, k, v)):
        out[i] = ref[0]


def pack(q, k, v, at, index, width, aligned):
    if aligned:
        blocks = width // HEAD
        return pl.pallas_call(
            pack_blocks_kernel,
            out_shape=jax.ShapeDtypeStruct((3, q.shape[1], width), q.dtype),
            grid_spec=pltpu.PrefetchScalarGridSpec(
                num_scalar_prefetch=1,
                grid=(1,),
                in_specs=[
                    pl.BlockSpec(
                        (1, q.shape[1], width), lambda i, at: (0, 0, at[index] // blocks)
                    )
                ]
                * 3,
                out_specs=pl.BlockSpec((3, q.shape[1], width), lambda i, at: (0, 0, 0)),
            ),
            compiler_params=pltpu.CompilerParams(vmem_limit_bytes=8 << 20),
            name="pack",
        )(at, q, k, v)
    return pl.pallas_call(
        partial(pack_kernel, index=index),
        out_shape=pltpu.VMEM((3, q.shape[1], width), q.dtype),
        grid_spec=pltpu.PrefetchScalarGridSpec(
            num_scalar_prefetch=1,
            grid=(),
            in_specs=[pl.BlockSpec(memory_space=pl.ANY)] * 3,
            out_specs=VMEM,
            scratch_shapes=[pltpu.SemaphoreType.DMA((3,))],
        ),
        compiler_params=pltpu.CompilerParams(vmem_limit_bytes=8 << 20),
        name="pack",
    )(at, q, k, v)


def collect_kernel(*refs, picks):
    out = refs[-1]
    for n, (which, block) in enumerate(picks):
        out[n] = refs[which][block]


def collect(parts, picks):
    return pl.pallas_call(
        partial(collect_kernel, picks=tuple(picks)),
        out_shape=jax.ShapeDtypeStruct((len(picks), *parts[0].shape[1:]), parts[0].dtype),
        in_specs=[VMEM] * len(parts),
        out_specs=VMEM,
        compiler_params=pltpu.CompilerParams(vmem_limit_bytes=8 << 20),
        name="collect",
    )(*parts)


def assemble_kernel(at, *refs, places):
    out = refs[-1]
    frame = at[at.shape[0] - 1]
    for ref, keys in zip(refs[:-1], places):
        for n, key in enumerate(keys):
            if key is not None:
                out[key ^ frame] = ref[n]


def assemble(parts, places, at):
    count = sum(key is not None for keys in places for key in keys)
    return pl.pallas_call(
        partial(assemble_kernel, places=places),
        out_shape=jax.ShapeDtypeStruct((count, *parts[0].shape[1:]), parts[0].dtype),
        grid_spec=pltpu.PrefetchScalarGridSpec(
            num_scalar_prefetch=1,
            grid=(),
            in_specs=[VMEM] * len(parts),
            out_specs=VMEM,
        ),
        compiler_params=pltpu.CompilerParams(vmem_limit_bytes=8 << 20),
        name="assemble",
    )(at, *parts)


def stages(frames):
    pair = 2
    line = min(4, frames // pair)
    return line, frames // (line * pair), pair


def spread_by_permutes(outs, at, frames):
    line, side, pair = stages(frames)
    rest = side * pair

    def swap(x, key):
        return lax.ppermute(x, "frame", [(i, i ^ key) for i in range(frames)])

    lined = {0: outs[0]}
    for a in range(line - 1, 0, -1):
        lined[a] = swap(outs[a], a * rest)
    sided = {}
    for b in range(1, side):
        picks = [(a, b * pair + c) for a in range(line) for c in range(pair)]
        sided[b] = swap(collect([lined[a] for a in range(line)], picks), b * pair)
    parts = [lined[a] for a in range(line)] + [sided[b] for b in range(1, side)]
    picks = [(a, 1) for a in range(line)]
    picks += [(line + b - 1, a * pair + 1) for b in range(1, side) for a in range(line)]
    parts.append(swap(collect(parts, picks), 1))
    places = [(a * rest,) + (None,) * (rest - 1) for a in range(line)]
    places += [
        tuple(
            a * rest + b * pair if c == 0 else None for a in range(line) for c in range(pair)
        )
        for b in range(1, side)
    ]
    places.append(tuple(a * rest + b * pair + 1 for b in range(side) for a in range(line)))
    return assemble(parts, tuple(places), at)


def local(spatial_q, spatial_k, spatial_v, norm_gain, temporal_weight):
    frames = lax.axis_size("frame")
    ways = lax.axis_size("row")
    me = lax.axis_index("row").astype(jnp.int32)
    tokens = spatial_q.shape[1]
    slot = tokens // frames
    tiled = slot % 8 == 0
    width = temporal_weight.shape[2]
    group = width // HEAD
    hbm = lambda x: pltpu.with_memory_space_constraint(x, pltpu.HBM)
    weight = hbm(jnp.transpose(temporal_weight, (1, 0, 2)))
    spatial_q, spatial_k, spatial_v = (hbm(x) for x in (spatial_q, spatial_k, spatial_v))
    gain = norm_gain.reshape(1, -1)

    staged = three_chunks(group, ways, frames, slot)
    if staged:
        sizes = MIXED if group == sum(MIXED) else (group // 3, group // 3, group - 2 * (group // 3))
    else:
        first = max(1, group * 5 // 12)
        sizes = (first, group - first) if group > 1 else (1,)
    chunks = [(sum(sizes[:i]), size) for i, size in enumerate(sizes)]
    last = len(chunks) - 1
    aligned = lambda i: group % chunks[i][1] == 0 and chunks[i][0] % chunks[i][1] == 0
    behind = [lax.rem(me + ways - k, ways) * group + c for c, _ in chunks for k in range(ways)]
    ahead = [lax.rem(me + k, ways) * group + c for c, _ in chunks for k in range(ways)]
    table = jnp.stack(behind + ahead + [me, lax.axis_index("frame").astype(jnp.int32)])

    def shift(x, k):
        return lax.ppermute(x, "row", [(i, (i + k) % ways) for i in range(ways)])

    received = []
    for i, (_, size) in enumerate(chunks):
        parts = []
        for k in range(1, ways):
            index = len(behind) + i * ways + k
            packed = pack(spatial_q, spatial_k, spatial_v, table, index, size * HEAD, aligned(i))
            parts.append(shift(packed, k))
        received.append(parts)

    pieces = {}
    for i, parts in enumerate(received):
        lines = stages(frames)[0] if staged and i == 1 else 0
        out = spatial(
            spatial_q, spatial_k, spatial_v, parts, hbm(gain), table, i * ways, frames, lines
        )
        if lines:
            pieces[i, 0] = spread_by_permutes(out, table, frames)
        else:
            out = lax.all_to_all(out, "frame", split_axis=0, concat_axis=0, tiled=True)
            pieces[i, 0] = out
        for k in range(1, ways):
            pieces[i, k] = shift(pieces[i, 0], k)
    if not tiled:
        flat = lambda x: x.transpose(1, 0, 2, 3).reshape(ways, tokens, -1)
        pieces = {key: flat(x) for key, x in pieces.items()}

    early = [[(0, k)] for k in range(1, ways)] if last else []
    early.append([(i, 0) for i in range(last + 1)])
    final = [(i, k) for i in range(min(1, last), last + 1) for k in range(1, ways)]
    order = [g[0] for g in early] + final
    at = jnp.stack([behind[i * ways + k] for i, k in order] + [me])
    flat = [key for g in early for key in g]
    groups = tuple(tuple(flat.index(key) for key in g) for g in early)
    shared = dict(tokens=tokens, ways=ways, tiled=tiled)
    carried = project(
        groups,
        [pieces[key] for key in flat],
        tuple(k for _, k in flat),
        at,
        [chunks[i][1] * HEAD for i, _ in final],
        weight,
        gain,
        **shared,
    )
    arrays, shifts = [pieces[key] for key in final], tuple(k for _, k in final)
    out = temporal(arrays, shifts, at, len(early), gain, carried, slot=slot, **shared)
    out = out.reshape(frames * ways, slot, width)
    out = lax.all_to_all(out, ("frame", "row"), split_axis=0, concat_axis=0, tiled=True)
    out = out.reshape(frames, ways, slot, width).transpose(0, 2, 1, 3)
    return out.reshape(1, tokens, ways * width)


MIXED = (6, 3, 3)


def three_chunks(group, ways, frames, slot):
    return group >= 3 and ways == 2 and frames & (frames - 1) == 0 and slot % 8 == 0 and frames > 2


def solution(mesh):
    return jax.shard_map(
        local,
        mesh=mesh,
        in_specs=(
            P("frame", "row", None),
            P("frame", "row", None),
            P("frame", "row", None),
            P(),
            P(None, None, "row"),
        ),
        out_specs=P("frame", "row", None),
        check_vma=False,
    )
```

```python
import math
from functools import partial

import jax
import jax.numpy as jnp
from jax import lax
from jax.experimental import pallas as pl
from jax.experimental.pallas import tpu as pltpu
from jax.sharding import PartitionSpec as P

D = 3072
HEADS = 24
AGENTS = 128
HEAD = D // HEADS
SCALE = HEAD ** (-0.5)
EXPONENT = SCALE * math.log2(math.e)

epsilon = 1e-06


def dot(left, right):
    return jnp.dot(left, right, preferred_element_type=jnp.float32)


def dot_nt(left, right):
    return lax.dot_general(
        left, right, (((1,), (1,)), ((), ())), preferred_element_type=jnp.float32
    )


VMEM = pl.BlockSpec(memory_space=pltpu.VMEM)


def weighted(scores):
    weights = jnp.exp2((scores - jnp.max(scores, axis=1, keepdims=True)) * EXPONENT)
    return weights, 1.0 / jnp.sum(weights, axis=1, keepdims=True)


def spatial_kernel(at, *refs, index, pool, tiled, lines):
    inputs, rest, (own, factor, sems) = refs[:3], refs[3:-3], refs[-3:]
    if lines:
        rest, outs, out, own = rest[: -lines - 1], rest[-lines - 1 : -1], rest[-1], own
        received, gain = rest[:-1], rest[-1]
        frame = at[at.shape[0] - 1]
    else:
        received, gain, out = rest[:-2], rest[-2], rest[-1]
    ways = len(received) + 1
    tokens, width = own.shape[1:]
    lanes = pl.ds(pl.multiple_of(at[index] * HEAD, HEAD), width)
    copies = [
        pltpu.make_async_copy(ref.at[0, :, lanes], own.at[i], sems.at[i])
        for i, ref in enumerate(inputs)
    ]
    copies.append(pltpu.make_async_copy(gain.at[:, lanes], factor, sems.at[3]))
    for copy in copies:
        copy.start()
    agent = lax.broadcasted_iota(jnp.int32, (tokens // pool, tokens), 0)
    token = lax.broadcasted_iota(jnp.int32, (tokens // pool, tokens), 1)
    member = ((token >= agent * pool) & (token < (agent + 1) * pool)).astype(jnp.bfloat16)
    for copy in copies:
        copy.wait()
    blocks = [own, *received]
    for start in range(0, width, TOGETHER * HEAD):
        stop = min(width, start + TOGETHER * HEAD)
        pooled = [dot(member, ref[0, :, start:stop]) for ref in blocks]
        pooled = (jnp.concatenate(pooled) * (1.0 / pool)).astype(jnp.bfloat16)
        split = [slice(n, n + HEAD) for n in range(start, stop, HEAD)]
        agents = [pooled[:, n.start - start : n.stop - start] for n in split]
        queries, keys, values = (
            [jnp.concatenate([ref[i, :, cols] for ref in blocks]) for cols in split]
            for i in range(3)
        )
        agent_scores = [dot_nt(a, b) for a, b in zip(agents, keys)]
        token_scores = [dot_nt(a, b) for a, b in zip(queries, agents)]
        agent_weights = [weighted(x) for x in agent_scores]
        token_weights = [weighted(x) for x in token_scores]
        agent_values = [
            (dot(w.astype(jnp.bfloat16), x) * r).astype(jnp.bfloat16)
            for (w, r), x in zip(agent_weights, values)
        ]
        results = [
            dot((w * r).astype(jnp.bfloat16), x) for (w, r), x in zip(token_weights, agent_values)
        ]
        for cols, result in zip(split, results):
            result = (result * factor[:, cols]).astype(jnp.bfloat16)
            for j in range(ways):
                block = result[j * tokens : (j + 1) * tokens]
                if lines:
                    slot = out.shape[2]
                    for f in range(out.shape[0]):
                        out[f ^ frame, j, :, cols] = block[f * slot : (f + 1) * slot]
                elif tiled:
                    out[:, j, :, cols] = block.reshape(out.shape[0], out.shape[2], HEAD)
                else:
                    out[j, :, cols] = block
    if lines:
        for n, target in enumerate(outs):
            size = target.shape[0]
            target[...] = out[n * size : (n + 1) * size]


TOGETHER = 4


def spatial(q, k, v, received, gain, at, index, frames, lines=0):
    tokens = q.shape[1]
    width = received[0].shape[2] if received else q.shape[2]
    ways = len(received) + 1
    slot = tokens // frames
    tiled = slot % 8 == 0
    shape = (frames, ways, slot, width) if tiled else (ways, tokens, width)
    hbm = pl.BlockSpec(memory_space=pl.ANY)
    out = pl.pallas_call(
        partial(
            spatial_kernel, index=index, pool=tokens * ways // AGENTS, tiled=tiled, lines=lines
        ),
        out_shape=(
            [jax.ShapeDtypeStruct((frames // lines, *shape[1:]), jnp.bfloat16)] * lines
            if lines
            else jax.ShapeDtypeStruct(shape, jnp.bfloat16)
        ),
        grid_spec=pltpu.PrefetchScalarGridSpec(
            num_scalar_prefetch=1,
            grid=(),
            in_specs=[hbm] * 3 + [VMEM] * len(received) + [hbm],
            out_specs=[VMEM] * lines if lines else VMEM,
            scratch_shapes=([pltpu.VMEM(shape, jnp.bfloat16)] if lines else [])
            + [
                pltpu.VMEM((3, tokens, width), jnp.bfloat16),
                pltpu.VMEM((1, width), jnp.float32),
                pltpu.SemaphoreType.DMA((4,)),
            ],
        ),
        cost_estimate=pl.CostEstimate(
            flops=10 * tokens * ways * AGENTS * width,
            bytes_accessed=10 * tokens * ways * width,
            transcendentals=2 * tokens * ways * width,
        ),
        compiler_params=pltpu.CompilerParams(vmem_limit_bytes=16 << 20),
        name="spatial",
    )(at, q, k, v, *received, gain)
    if not tiled and not lines:
        out = out.reshape(ways, frames, slot, width).transpose(1, 0, 2, 3)
    return out


def rows_of(ref, block, tokens, tiled):
    if tiled:
        return ref[:, block, :, :].reshape(tokens, -1)
    return ref[block]


def squares(x, inverse):
    y = x.astype(jnp.float32) * inverse
    y = y * y
    total = y[:, :HEAD]
    for at in range(HEAD, y.shape[1], HEAD):
        total = total + y[:, at : at + HEAD]
    return total


AHEAD = 4


def hold(held, xs, depths, shifts, tokens, ways, tiled):
    column = 0
    for x, depth, shift in zip(xs, depths, shifts):
        for j in range(ways):
            held[j * tokens : (j + 1) * tokens, column : column + depth] = rows_of(
                x, (j - shift) % ways, tokens, tiled
            )
        column += depth


def project_kernel(at, *refs, groups, places, shifts, depths, carried, tokens, ways, tiled):
    xs = refs[: len(shifts)]
    weight, gain = refs[len(shifts) : len(shifts) + 2]
    before, refs = refs[len(shifts) + 2 :][: 2 * carried], refs[len(shifts) + 2 + 2 * carried :]
    acc, ss, *rest = refs
    kept = rest[: len(groups) - sum(g is not None for g in groups)]
    sems = rest[-1]
    used = [g for g in groups if g is not None]
    scratch = rest[len(kept) : -1]
    held, buffers = scratch[: len(used)], scratch[len(used) :]
    targets = [*buffers, *kept]
    copies = []
    for i, target in enumerate(targets):
        rows = pl.ds(pl.multiple_of(at[places[i]] * HEAD, HEAD), target.shape[1])
        for c in range(3):
            copies.append(
                pltpu.make_async_copy(weight.at[c, rows, :], target.at[c], sems.at[3 * i + c])
            )
    for copy in copies[:AHEAD]:
        copy.start()
    width = weight.shape[2]
    tile = width // 3 if width % 3 == 0 else width
    total = before[1][...] if carried else None
    for i, members in enumerate(used):
        hold(
            held[i],
            [xs[m] for m in members],
            [depths[m] for m in members],
            [shifts[m] for m in members],
            tokens,
            ways,
            tiled,
        )
        lanes = pl.ds(pl.multiple_of(at[places[i]] * HEAD, HEAD), held[i].shape[1])
        part = squares(held[i][...], 1.0 / gain[:, lanes])
        total = part if total is None else total + part
        for c in range(3):
            copies[3 * i + c].wait()
            if 3 * i + c + AHEAD < len(copies):
                copies[3 * i + c + AHEAD].start()
            for n in range(0, width, tile):
                cols = slice(n, n + tile)
                value = dot(held[i][...], buffers[i][c, :, cols])
                if i == 0:
                    acc[c, :, cols] = before[0][c, :, cols] + value if carried else value
                else:
                    acc[c, :, cols] += value
    ss[...] = total
    for n in range(3 * len(used) + AHEAD, len(copies)):
        copies[n].start()
    for copy in copies[3 * len(used) :]:
        copy.wait()


def project(groups, places, arrays, shifts, at, later, carried, weight, gain, tokens, ways, tiled):
    rows = tokens * ways
    width = weight.shape[2]
    depths = [x.shape[-1] for x in arrays]
    sums = [sum(depths[m] for m in g) for g in groups]
    return pl.pallas_call(
        partial(
            project_kernel,
            groups=(*groups, *[None] * len(later)),
            places=places,
            shifts=shifts,
            depths=depths,
            carried=bool(carried),
            tokens=tokens,
            ways=ways,
            tiled=tiled,
        ),
        out_shape=(
            pltpu.VMEM((3, rows, width), jnp.float32),
            pltpu.VMEM((rows, HEAD), jnp.float32),
            *[pltpu.VMEM((3, depth, width), weight.dtype) for depth in later],
        ),
        grid_spec=pltpu.PrefetchScalarGridSpec(
            num_scalar_prefetch=1,
            grid=(),
            in_specs=[VMEM] * len(arrays)
            + [pl.BlockSpec(memory_space=pl.ANY)]
            + [VMEM] * (1 + len(carried)),
            out_specs=(VMEM,) * (2 + len(later)),
            scratch_shapes=[pltpu.VMEM((rows, depth), jnp.bfloat16) for depth in sums]
            + [pltpu.VMEM((3, depth, width), weight.dtype) for depth in sums]
            + [pltpu.SemaphoreType.DMA((3 * (len(sums) + len(later)),))],
        ),
        cost_estimate=pl.CostEstimate(
            flops=6 * rows * sum(sums) * width,
            bytes_accessed=6 * (sum(sums) + sum(later)) * width,
            transcendentals=0,
        ),
        input_output_aliases=(
            {len(arrays) + 3: 0, len(arrays) + 4: 1} if carried else {}
        ),
        compiler_params=pltpu.CompilerParams(vmem_limit_bytes=32 << 20),
        name="project",
    )(at, *arrays, weight, gain, *carried)


def temporal_kernel(at, *refs, places, shifts, heads, tokens, ways, slot, tiled):
    count = len(shifts)
    xs = refs[:count]
    gain, acc, ss = refs[count : count + 3]
    ws = refs[count + 3 : 2 * count + 3]
    out, *held, rstd = refs[2 * count + 3 :]
    step = heads * HEAD

    @pl.when(pl.program_id(0) == 0)
    def _():
        total = ss[...]
        for i in range(count):
            depth = ws[i].shape[1]
            hold(held[i], [xs[i]], [depth], [shifts[i]], tokens, ways, tiled)
            lanes = pl.ds(pl.multiple_of(at[places[i]] * HEAD, HEAD), depth)
            total = total + squares(held[i][...], 1.0 / gain[:, lanes])
        mean = jnp.sum(total, axis=1, keepdims=True) * (1.0 / D)
        rstd[...] = jnp.broadcast_to(lax.rsqrt(mean + epsilon), rstd.shape)

    row = lax.broadcasted_iota(jnp.int32, (tokens, tokens), 0)
    col = lax.broadcasted_iota(jnp.int32, (tokens, tokens), 1)
    same = lax.rem(row, slot) == lax.rem(col, slot)
    part = pl.ds(pl.multiple_of(pl.program_id(0) * step, step), step)
    factor = jnp.concatenate([rstd[...]] * heads, axis=1)
    qkv = []
    for c in range(3):
        value = acc[c, :, part]
        for i in range(count):
            value = value + dot(held[i][...], ws[i][c, :, part])
        qkv.append((value * factor).astype(jnp.bfloat16))
    split = [
        (j, slice(j * tokens, (j + 1) * tokens), slice(h * HEAD, (h + 1) * HEAD))
        for h in range(heads)
        for j in range(ways)
    ]
    scores = [
        jnp.where(same, dot_nt(qkv[0][rows, cols], qkv[1][rows, cols]), -1e30)
        for _, rows, cols in split
    ]
    weights = [weighted(x) for x in scores]
    me = at[at.shape[0] - 2]
    for (j, rows, cols), (w, r) in zip(split, weights):
        result = dot((w * r).astype(jnp.bfloat16), qkv[2][rows, cols]).astype(jnp.bfloat16)
        target = lax.rem(me + ways - j, ways)
        if tiled:
            out[:, target, :, cols] = result.reshape(out.shape[0], slot, HEAD)
        else:
            out[target, :, cols] = result


def temporal(arrays, shifts, at, places, gain, carried, tokens, ways, slot, tiled):
    rows = tokens * ways
    width = carried[0].shape[2]
    depths = [x.shape[-1] for x in arrays]
    frames = tokens // slot
    heads = math.gcd(width // HEAD, FINAL_HEADS)
    step = heads * HEAD
    if tiled:
        shape = (frames, ways, slot, width)
        out_spec = pl.BlockSpec((frames, ways, slot, step), lambda n, at: (0, 0, 0, n))
    else:
        shape = (ways, tokens, width)
        out_spec = pl.BlockSpec((ways, tokens, step), lambda n, at: (0, 0, n))
    operands = [*arrays, gain, *carried]
    out = pl.pallas_call(
        partial(
            temporal_kernel,
            places=places,
            shifts=shifts,
            heads=heads,
            tokens=tokens,
            ways=ways,
            slot=slot,
            tiled=tiled,
        ),
        out_shape=jax.ShapeDtypeStruct(shape, jnp.bfloat16),
        grid_spec=pltpu.PrefetchScalarGridSpec(
            num_scalar_prefetch=1,
            grid=(width // step,),
            in_specs=[VMEM] * len(operands),
            out_specs=out_spec,
            scratch_shapes=[pltpu.VMEM((rows, depth), jnp.bfloat16) for depth in depths]
            + [pltpu.VMEM((rows, HEAD), jnp.float32)],
        ),
        cost_estimate=pl.CostEstimate(
            flops=6 * rows * sum(depths) * width,
            bytes_accessed=2 * rows * width,
            transcendentals=rows * width,
        ),
        compiler_params=pltpu.CompilerParams(vmem_limit_bytes=16 << 20),
        name="temporal",
    )(at, *operands)
    if not tiled:
        out = out.reshape(ways, frames, slot, width).transpose(1, 0, 2, 3)
    return out


FINAL_HEADS = 6


def pack_kernel(at, q, k, v, out, sems, *, index):
    lanes = pl.ds(pl.multiple_of(at[index] * HEAD, HEAD), out.shape[2])
    copies = [
        pltpu.make_async_copy(ref.at[0, :, lanes], out.at[i], sems.at[i])
        for i, ref in enumerate((q, k, v))
    ]
    for copy in copies:
        copy.start()
    for copy in copies:
        copy.wait()


def pack(q, k, v, at, index, width):
    return pl.pallas_call(
        partial(pack_kernel, index=index),
        out_shape=pltpu.VMEM((3, q.shape[1], width), q.dtype),
        grid_spec=pltpu.PrefetchScalarGridSpec(
            num_scalar_prefetch=1,
            grid=(),
            in_specs=[pl.BlockSpec(memory_space=pl.ANY)] * 3,
            out_specs=VMEM,
            scratch_shapes=[pltpu.SemaphoreType.DMA((3,))],
        ),
        compiler_params=pltpu.CompilerParams(vmem_limit_bytes=8 << 20),
        name="pack",
    )(at, q, k, v)


def collect_kernel(*refs, picks):
    out = refs[-1]
    for n, (which, block) in enumerate(picks):
        out[n] = refs[which][block]


def collect(parts, picks):
    return pl.pallas_call(
        partial(collect_kernel, picks=tuple(picks)),
        out_shape=jax.ShapeDtypeStruct((len(picks), *parts[0].shape[1:]), parts[0].dtype),
        in_specs=[VMEM] * len(parts),
        out_specs=VMEM,
        compiler_params=pltpu.CompilerParams(vmem_limit_bytes=8 << 20),
        name="collect",
    )(*parts)


def assemble_kernel(at, *refs, places):
    out = refs[-1]
    frame = at[at.shape[0] - 1]
    for ref, keys in zip(refs[:-1], places):
        for n, key in enumerate(keys):
            if key is not None:
                out[key ^ frame] = ref[n]


def assemble(parts, places, at):
    count = sum(key is not None for keys in places for key in keys)
    return pl.pallas_call(
        partial(assemble_kernel, places=places),
        out_shape=jax.ShapeDtypeStruct((count, *parts[0].shape[1:]), parts[0].dtype),
        grid_spec=pltpu.PrefetchScalarGridSpec(
            num_scalar_prefetch=1,
            grid=(),
            in_specs=[VMEM] * len(parts),
            out_specs=VMEM,
        ),
        compiler_params=pltpu.CompilerParams(vmem_limit_bytes=8 << 20),
        name="assemble",
    )(at, *parts)


def stages(frames):
    pair = 2
    line = min(4, frames // pair)
    return line, frames // (line * pair), pair


def spread_by_permutes(outs, at, frames):
    line, side, pair = stages(frames)
    rest = side * pair

    def swap(x, key):
        return lax.ppermute(x, "frame", [(i, i ^ key) for i in range(frames)])

    lined = {0: outs[0]}
    for a in range(line - 1, 0, -1):
        lined[a] = swap(outs[a], a * rest)
    sided = {}
    for b in range(1, side):
        picks = [(a, b * pair + c) for a in range(line) for c in range(pair)]
        sided[b] = swap(collect([lined[a] for a in range(line)], picks), b * pair)
    parts = [lined[a] for a in range(line)] + [sided[b] for b in range(1, side)]
    picks = [(a, 1) for a in range(line)]
    picks += [(line + b - 1, a * pair + 1) for b in range(1, side) for a in range(line)]
    parts.append(swap(collect(parts, picks), 1))
    places = [(a * rest,) + (None,) * (rest - 1) for a in range(line)]
    places += [
        tuple(
            a * rest + b * pair if c == 0 else None for a in range(line) for c in range(pair)
        )
        for b in range(1, side)
    ]
    places.append(tuple(a * rest + b * pair + 1 for b in range(side) for a in range(line)))
    return assemble(parts, tuple(places), at)


def local(spatial_q, spatial_k, spatial_v, norm_gain, temporal_weight):
    frames = lax.axis_size("frame")
    ways = lax.axis_size("row")
    me = lax.axis_index("row").astype(jnp.int32)
    tokens = spatial_q.shape[1]
    slot = tokens // frames
    tiled = slot % 8 == 0
    width = temporal_weight.shape[2]
    group = width // HEAD
    hbm = lambda x: pltpu.with_memory_space_constraint(x, pltpu.HBM)
    weight = hbm(jnp.transpose(temporal_weight, (1, 0, 2)))
    spatial_q, spatial_k, spatial_v = (hbm(x) for x in (spatial_q, spatial_k, spatial_v))
    gain = norm_gain.reshape(1, -1)

    staged = three_chunks(group, ways, frames, slot)
    if staged:
        sizes = MIXED if group == sum(MIXED) else (group // 3, group // 3, group - 2 * (group // 3))
    else:
        first = max(1, group * 5 // 12)
        sizes = (first, group - first) if group > 1 else (1,)
    chunks = [(sum(sizes[:i]), size) for i, size in enumerate(sizes)]
    last = len(chunks) - 1
    behind = [lax.rem(me + ways - k, ways) * group + c for c, _ in chunks for k in range(ways)]
    ahead = [lax.rem(me + k, ways) * group + c for c, _ in chunks for k in range(ways)]
    table = jnp.stack(behind + ahead + [me, lax.axis_index("frame").astype(jnp.int32)])

    def shift(x, k):
        return lax.ppermute(x, "row", [(i, (i + k) % ways) for i in range(ways)])

    received = []
    for i, (_, size) in enumerate(chunks):
        parts = []
        for k in range(1, ways):
            index = len(behind) + i * ways + k
            packed = pack(spatial_q, spatial_k, spatial_v, table, index, size * HEAD)
            parts.append(shift(packed, k))
        received.append(parts)

    pieces = {}
    for i, parts in enumerate(received):
        lines = stages(frames)[0] if staged and i != 1 else 0
        out = spatial(
            spatial_q, spatial_k, spatial_v, parts, hbm(gain), table, i * ways, frames, lines
        )
        if lines:
            pieces[i, 0] = spread_by_permutes(out, table, frames)
        else:
            out = lax.all_to_all(out, "frame", split_axis=0, concat_axis=0, tiled=True)
            pieces[i, 0] = out
        for k in range(1, ways):
            pieces[i, k] = shift(pieces[i, 0], k)
    if not tiled:
        flat = lambda x: x.transpose(1, 0, 2, 3).reshape(ways, tokens, -1)
        pieces = {key: flat(x) for key, x in pieces.items()}

    others = lambda i: [[(i, k)] for k in range(1, ways)]
    if staged:
        steps = [[[(0, 0), (1, 0)]], others(0), [[(2, 0)]] + others(1)]
    else:
        steps = [[key for i in range(last) for key in others(i)] + [[(i, 0) for i in range(last + 1)]]]
    final = [g[0] for g in others(last)]
    place = lambda key: key[0] * ways + key[1]
    shared = dict(tokens=tokens, ways=ways, tiled=tiled)
    carried = ()
    for n, wanted in enumerate(steps):
        flat = [key for g in wanted for key in g]
        later = final if n == len(steps) - 1 else []
        carried = project(
            tuple(tuple(flat.index(key) for key in g) for g in wanted),
            tuple(place(key) for key in [g[0] for g in wanted] + later),
            [pieces[key] for key in flat],
            tuple(k for _, k in flat),
            table,
            [chunks[i][1] * HEAD for i, _ in later],
            carried,
            weight,
            gain,
            **shared,
        )
    arrays, shifts = [pieces[key] for key in final], tuple(k for _, k in final)
    places = tuple(place(key) for key in final)
    out = temporal(arrays, shifts, table, places, gain, carried, slot=slot, **shared)
    out = out.reshape(frames * ways, slot, width)
    out = lax.all_to_all(out, ("frame", "row"), split_axis=0, concat_axis=0, tiled=True)
    out = out.reshape(frames, ways, slot, width).transpose(0, 2, 1, 3)
    return out.reshape(1, tokens, ways * width)


MIXED = (4, 4, 4)


def three_chunks(group, ways, frames, slot):
    return group >= 3 and ways == 2 and frames & (frames - 1) == 0 and slot % 8 == 0 and frames > 2


def solution(mesh):
    return jax.shard_map(
        local,
        mesh=mesh,
        in_specs=(
            P("frame", "row", None),
            P("frame", "row", None),
            P("frame", "row", None),
            P(),
            P(None, None, "row"),
        ),
        out_specs=P("frame", "row", None),
        check_vma=False,
    )
```

```python
import math
from functools import partial

import jax
import jax.numpy as jnp
from jax import lax
from jax.experimental import pallas as pl
from jax.experimental.pallas import tpu as pltpu
from jax.sharding import PartitionSpec as P

D = 3072
HEADS = 24
AGENTS = 128
HEAD = D // HEADS
SCALE = HEAD ** (-0.5)
EXPONENT = SCALE * math.log2(math.e)

epsilon = 1e-06


def dot(left, right):
    return jnp.dot(left, right, preferred_element_type=jnp.float32)


def dot_nt(left, right):
    return lax.dot_general(
        left, right, (((1,), (1,)), ((), ())), preferred_element_type=jnp.float32
    )


VMEM = pl.BlockSpec(memory_space=pltpu.VMEM)


def weighted(scores):
    weights = jnp.exp2((scores - jnp.max(scores, axis=1, keepdims=True)) * EXPONENT)
    return weights, 1.0 / jnp.sum(weights, axis=1, keepdims=True)


def spatial_kernel(at, *refs, index, pool, tiled, lines):
    inputs, rest, (own, factor, sems) = refs[:3], refs[3:-3], refs[-3:]
    if lines:
        rest, outs, out, own = rest[: -lines - 1], rest[-lines - 1 : -1], rest[-1], own
        received, gain = rest[:-1], rest[-1]
        frame = at[at.shape[0] - 1]
    else:
        received, gain, out = rest[:-2], rest[-2], rest[-1]
    ways = len(received) + 1
    tokens, width = own.shape[1:]
    lanes = pl.ds(pl.multiple_of(at[index] * HEAD, HEAD), width)
    copies = [
        pltpu.make_async_copy(ref.at[0, :, lanes], own.at[i], sems.at[i])
        for i, ref in enumerate(inputs)
    ]
    copies.append(pltpu.make_async_copy(gain.at[:, lanes], factor, sems.at[3]))
    for copy in copies:
        copy.start()
    agent = lax.broadcasted_iota(jnp.int32, (tokens // pool, tokens), 0)
    token = lax.broadcasted_iota(jnp.int32, (tokens // pool, tokens), 1)
    member = ((token >= agent * pool) & (token < (agent + 1) * pool)).astype(jnp.bfloat16)
    for copy in copies:
        copy.wait()
    blocks = [own, *received]
    for start in range(0, width, TOGETHER * HEAD):
        stop = min(width, start + TOGETHER * HEAD)
        pooled = [dot(member, ref[0, :, start:stop]) for ref in blocks]
        pooled = (jnp.concatenate(pooled) * (1.0 / pool)).astype(jnp.bfloat16)
        split = [slice(n, n + HEAD) for n in range(start, stop, HEAD)]
        agents = [pooled[:, n.start - start : n.stop - start] for n in split]
        queries, keys, values = (
            [jnp.concatenate([ref[i, :, cols] for ref in blocks]) for cols in split]
            for i in range(3)
        )
        agent_scores = [dot_nt(a, b) for a, b in zip(agents, keys)]
        token_scores = [dot_nt(a, b) for a, b in zip(queries, agents)]
        agent_weights = [weighted(x) for x in agent_scores]
        token_weights = [weighted(x) for x in token_scores]
        agent_values = [
            (dot(w.astype(jnp.bfloat16), x) * r).astype(jnp.bfloat16)
            for (w, r), x in zip(agent_weights, values)
        ]
        results = [
            dot((w * r).astype(jnp.bfloat16), x) for (w, r), x in zip(token_weights, agent_values)
        ]
        for cols, result in zip(split, results):
            result = (result * factor[:, cols]).astype(jnp.bfloat16)
            for j in range(ways):
                block = result[j * tokens : (j + 1) * tokens]
                if lines:
                    slot = out.shape[2]
                    for f in range(out.shape[0]):
                        out[f ^ frame, j, :, cols] = block[f * slot : (f + 1) * slot]
                elif tiled:
                    out[:, j, :, cols] = block.reshape(out.shape[0], out.shape[2], HEAD)
                else:
                    out[j, :, cols] = block
    if lines:
        for n, target in enumerate(outs):
            size = target.shape[0]
            target[...] = out[n * size : (n + 1) * size]


TOGETHER = 4


def spatial(q, k, v, received, gain, at, index, frames, lines=0):
    tokens = q.shape[1]
    width = received[0].shape[2] if received else q.shape[2]
    ways = len(received) + 1
    slot = tokens // frames
    tiled = slot % 8 == 0
    shape = (frames, ways, slot, width) if tiled else (ways, tokens, width)
    hbm = pl.BlockSpec(memory_space=pl.ANY)
    out = pl.pallas_call(
        partial(
            spatial_kernel, index=index, pool=tokens * ways // AGENTS, tiled=tiled, lines=lines
        ),
        out_shape=(
            [jax.ShapeDtypeStruct((frames // lines, *shape[1:]), jnp.bfloat16)] * lines
            if lines
            else jax.ShapeDtypeStruct(shape, jnp.bfloat16)
        ),
        grid_spec=pltpu.PrefetchScalarGridSpec(
            num_scalar_prefetch=1,
            grid=(),
            in_specs=[hbm] * 3 + [VMEM] * len(received) + [hbm],
            out_specs=[VMEM] * lines if lines else VMEM,
            scratch_shapes=([pltpu.VMEM(shape, jnp.bfloat16)] if lines else [])
            + [
                pltpu.VMEM((3, tokens, width), jnp.bfloat16),
                pltpu.VMEM((1, width), jnp.float32),
                pltpu.SemaphoreType.DMA((4,)),
            ],
        ),
        cost_estimate=pl.CostEstimate(
            flops=10 * tokens * ways * AGENTS * width,
            bytes_accessed=10 * tokens * ways * width,
            transcendentals=2 * tokens * ways * width,
        ),
        compiler_params=pltpu.CompilerParams(vmem_limit_bytes=16 << 20),
        name="spatial",
    )(at, q, k, v, *received, gain)
    if not tiled and not lines:
        out = out.reshape(ways, frames, slot, width).transpose(1, 0, 2, 3)
    return out


def rows_of(ref, block, tokens, tiled):
    if tiled:
        return ref[:, block, :, :].reshape(tokens, -1)
    return ref[block]


def squares(x, inverse):
    y = x.astype(jnp.float32) * inverse
    y = y * y
    total = y[:, :HEAD]
    for at in range(HEAD, y.shape[1], HEAD):
        total = total + y[:, at : at + HEAD]
    return total


AHEAD = 4


def hold(held, xs, depths, shifts, tokens, ways, tiled):
    column = 0
    for x, depth, shift in zip(xs, depths, shifts):
        for j in range(ways):
            held[j * tokens : (j + 1) * tokens, column : column + depth] = rows_of(
                x, (j - shift) % ways, tokens, tiled
            )
        column += depth


def project_kernel(
    at, *refs, groups, places, shifts, depths, carried, given, tokens, ways, tiled
):
    xs = refs[: len(shifts)]
    weight, gain = refs[len(shifts) : len(shifts) + 2]
    refs = refs[len(shifts) + 2 :]
    before, there = refs[: 2 * carried], refs[2 * carried : 2 * carried + given]
    refs = refs[2 * carried + given :]
    acc, ss, *rest = refs
    kept = rest[: len(groups) - sum(g is not None for g in groups)]
    sems = rest[-1]
    used = [g for g in groups if g is not None]
    scratch = rest[len(kept) : -1]
    held, buffers = scratch[: len(used)], [*there, *scratch[len(used) :]]
    targets = [*buffers, *kept]
    copies = []
    for i, target in enumerate(targets):
        if i < given:
            continue
        rows = pl.ds(pl.multiple_of(at[places[i]] * HEAD, HEAD), target.shape[1])
        for c in range(3):
            copies.append(
                pltpu.make_async_copy(weight.at[c, rows, :], target.at[c], sems.at[3 * i + c])
            )
    for copy in copies[:AHEAD]:
        copy.start()
    width = weight.shape[2]
    tile = width // 3 if width % 3 == 0 else width
    total = before[1][...] if carried else None
    for i, members in enumerate(used):
        hold(
            held[i],
            [xs[m] for m in members],
            [depths[m] for m in members],
            [shifts[m] for m in members],
            tokens,
            ways,
            tiled,
        )
        lanes = pl.ds(pl.multiple_of(at[places[i]] * HEAD, HEAD), held[i].shape[1])
        part = squares(held[i][...], 1.0 / gain[:, lanes])
        total = part if total is None else total + part
        for c in range(3):
            now = 3 * (i - given) + c
            if now >= 0:
                copies[now].wait()
                if now + AHEAD < len(copies):
                    copies[now + AHEAD].start()
            for n in range(0, width, tile):
                cols = slice(n, n + tile)
                value = dot(held[i][...], buffers[i][c, :, cols])
                if i == 0:
                    acc[c, :, cols] = before[0][c, :, cols] + value if carried else value
                else:
                    acc[c, :, cols] += value
    ss[...] = total
    done = 3 * (len(used) - given)
    for n in range(done + AHEAD, len(copies)):
        copies[n].start()
    for copy in copies[done:]:
        copy.wait()


def project(
    groups, places, arrays, shifts, at, later, carried, given, weight, gain, tokens, ways, tiled
):
    rows = tokens * ways
    width = weight.shape[2]
    depths = [x.shape[-1] for x in arrays]
    sums = [sum(depths[m] for m in g) for g in groups]
    return pl.pallas_call(
        partial(
            project_kernel,
            groups=(*groups, *[None] * len(later)),
            places=places,
            shifts=shifts,
            depths=depths,
            carried=bool(carried),
            given=len(given),
            tokens=tokens,
            ways=ways,
            tiled=tiled,
        ),
        out_shape=(
            pltpu.VMEM((3, rows, width), jnp.float32),
            pltpu.VMEM((rows, HEAD), jnp.float32),
            *[pltpu.VMEM((3, depth, width), weight.dtype) for depth in later],
        ),
        grid_spec=pltpu.PrefetchScalarGridSpec(
            num_scalar_prefetch=1,
            grid=(),
            in_specs=[VMEM] * len(arrays)
            + [pl.BlockSpec(memory_space=pl.ANY)]
            + [VMEM] * (1 + len(carried) + len(given)),
            out_specs=(VMEM,) * (2 + len(later)),
            scratch_shapes=[pltpu.VMEM((rows, depth), jnp.bfloat16) for depth in sums]
            + [pltpu.VMEM((3, depth, width), weight.dtype) for depth in sums[len(given) :]]
            + [pltpu.SemaphoreType.DMA((3 * (len(sums) + len(later)),))],
        ),
        cost_estimate=pl.CostEstimate(
            flops=6 * rows * sum(sums) * width,
            bytes_accessed=6 * (sum(sums) + sum(later)) * width,
            transcendentals=0,
        ),
        input_output_aliases=(
            {len(arrays) + 3: 0, len(arrays) + 4: 1} if carried else {}
        ),
        compiler_params=pltpu.CompilerParams(vmem_limit_bytes=32 << 20),
        name="project",
    )(at, *arrays, weight, gain, *carried, *given)


def temporal_kernel(at, *refs, places, shifts, heads, tokens, ways, slot, tiled):
    count = len(shifts)
    xs = refs[:count]
    gain, acc, ss = refs[count : count + 3]
    ws = refs[count + 3 : 2 * count + 3]
    out, *held, rstd = refs[2 * count + 3 :]
    step = heads * HEAD

    @pl.when(pl.program_id(0) == 0)
    def _():
        total = ss[...]
        for i in range(count):
            depth = ws[i].shape[1]
            hold(held[i], [xs[i]], [depth], [shifts[i]], tokens, ways, tiled)
            lanes = pl.ds(pl.multiple_of(at[places[i]] * HEAD, HEAD), depth)
            total = total + squares(held[i][...], 1.0 / gain[:, lanes])
        mean = jnp.sum(total, axis=1, keepdims=True) * (1.0 / D)
        rstd[...] = jnp.broadcast_to(lax.rsqrt(mean + epsilon), rstd.shape)

    row = lax.broadcasted_iota(jnp.int32, (tokens, tokens), 0)
    col = lax.broadcasted_iota(jnp.int32, (tokens, tokens), 1)
    same = lax.rem(row, slot) == lax.rem(col, slot)
    part = pl.ds(pl.multiple_of(pl.program_id(0) * step, step), step)
    factor = jnp.concatenate([rstd[...]] * heads, axis=1)
    qkv = []
    for c in range(3):
        value = acc[c, :, part]
        for i in range(count):
            value = value + dot(held[i][...], ws[i][c, :, part])
        qkv.append((value * factor).astype(jnp.bfloat16))
    split = [
        (j, slice(j * tokens, (j + 1) * tokens), slice(h * HEAD, (h + 1) * HEAD))
        for h in range(heads)
        for j in range(ways)
    ]
    scores = [
        jnp.where(same, dot_nt(qkv[0][rows, cols], qkv[1][rows, cols]), -1e30)
        for _, rows, cols in split
    ]
    weights = [weighted(x) for x in scores]
    me = at[at.shape[0] - 2]
    for (j, rows, cols), (w, r) in zip(split, weights):
        result = dot((w * r).astype(jnp.bfloat16), qkv[2][rows, cols]).astype(jnp.bfloat16)
        target = lax.rem(me + ways - j, ways)
        if tiled:
            out[:, target, :, cols] = result.reshape(out.shape[0], slot, HEAD)
        else:
            out[target, :, cols] = result


def temporal(arrays, shifts, at, places, gain, carried, tokens, ways, slot, tiled):
    rows = tokens * ways
    width = carried[0].shape[2]
    depths = [x.shape[-1] for x in arrays]
    frames = tokens // slot
    heads = math.gcd(width // HEAD, FINAL_HEADS)
    step = heads * HEAD
    if tiled:
        shape = (frames, ways, slot, width)
        out_spec = pl.BlockSpec((frames, ways, slot, step), lambda n, at: (0, 0, 0, n))
    else:
        shape = (ways, tokens, width)
        out_spec = pl.BlockSpec((ways, tokens, step), lambda n, at: (0, 0, n))
    operands = [*arrays, gain, *carried]
    out = pl.pallas_call(
        partial(
            temporal_kernel,
            places=places,
            shifts=shifts,
            heads=heads,
            tokens=tokens,
            ways=ways,
            slot=slot,
            tiled=tiled,
        ),
        out_shape=jax.ShapeDtypeStruct(shape, jnp.bfloat16),
        grid_spec=pltpu.PrefetchScalarGridSpec(
            num_scalar_prefetch=1,
            grid=(width // step,),
            in_specs=[VMEM] * len(operands),
            out_specs=out_spec,
            scratch_shapes=[pltpu.VMEM((rows, depth), jnp.bfloat16) for depth in depths]
            + [pltpu.VMEM((rows, HEAD), jnp.float32)],
        ),
        cost_estimate=pl.CostEstimate(
            flops=6 * rows * sum(depths) * width,
            bytes_accessed=2 * rows * width,
            transcendentals=rows * width,
        ),
        compiler_params=pltpu.CompilerParams(vmem_limit_bytes=16 << 20),
        name="temporal",
    )(at, *operands)
    if not tiled:
        out = out.reshape(ways, frames, slot, width).transpose(1, 0, 2, 3)
    return out


FINAL_HEADS = 6


def pack_kernel(at, q, k, v, out, sems, *, index):
    lanes = pl.ds(pl.multiple_of(at[index] * HEAD, HEAD), out.shape[2])
    copies = [
        pltpu.make_async_copy(ref.at[0, :, lanes], out.at[i], sems.at[i])
        for i, ref in enumerate((q, k, v))
    ]
    for copy in copies:
        copy.start()
    for copy in copies:
        copy.wait()


def pack_blocks_kernel(at, q, k, v, out):
    for i, ref in enumerate((q, k, v)):
        out[i] = ref[0]


def pack(q, k, v, at, index, width, aligned):
    if aligned:
        blocks = width // HEAD
        return pl.pallas_call(
            pack_blocks_kernel,
            out_shape=jax.ShapeDtypeStruct((3, q.shape[1], width), q.dtype),
            grid_spec=pltpu.PrefetchScalarGridSpec(
                num_scalar_prefetch=1,
                grid=(1,),
                in_specs=[
                    pl.BlockSpec(
                        (1, q.shape[1], width), lambda i, at: (0, 0, at[index] // blocks)
                    )
                ]
                * 3,
                out_specs=pl.BlockSpec((3, q.shape[1], width), lambda i, at: (0, 0, 0)),
            ),
            compiler_params=pltpu.CompilerParams(vmem_limit_bytes=8 << 20),
            name="pack",
        )(at, q, k, v)
    return pl.pallas_call(
        partial(pack_kernel, index=index),
        out_shape=pltpu.VMEM((3, q.shape[1], width), q.dtype),
        grid_spec=pltpu.PrefetchScalarGridSpec(
            num_scalar_prefetch=1,
            grid=(),
            in_specs=[pl.BlockSpec(memory_space=pl.ANY)] * 3,
            out_specs=VMEM,
            scratch_shapes=[pltpu.SemaphoreType.DMA((3,))],
        ),
        compiler_params=pltpu.CompilerParams(vmem_limit_bytes=8 << 20),
        name="pack",
    )(at, q, k, v)


def collect_kernel(*refs, picks):
    out = refs[-1]
    for n, (which, block) in enumerate(picks):
        out[n] = refs[which][block]


def collect(parts, picks):
    return pl.pallas_call(
        partial(collect_kernel, picks=tuple(picks)),
        out_shape=jax.ShapeDtypeStruct((len(picks), *parts[0].shape[1:]), parts[0].dtype),
        in_specs=[VMEM] * len(parts),
        out_specs=VMEM,
        compiler_params=pltpu.CompilerParams(vmem_limit_bytes=8 << 20),
        name="collect",
    )(*parts)


def assemble_kernel(at, *refs, places):
    out = refs[-1]
    frame = at[at.shape[0] - 1]
    for ref, keys in zip(refs[:-1], places):
        for n, key in enumerate(keys):
            if key is not None:
                out[key ^ frame] = ref[n]


def assemble(parts, places, at):
    count = sum(key is not None for keys in places for key in keys)
    return pl.pallas_call(
        partial(assemble_kernel, places=places),
        out_shape=jax.ShapeDtypeStruct((count, *parts[0].shape[1:]), parts[0].dtype),
        grid_spec=pltpu.PrefetchScalarGridSpec(
            num_scalar_prefetch=1,
            grid=(),
            in_specs=[VMEM] * len(parts),
            out_specs=VMEM,
        ),
        compiler_params=pltpu.CompilerParams(vmem_limit_bytes=8 << 20),
        name="assemble",
    )(at, *parts)


def stages(frames):
    pair = 2
    line = min(4, frames // pair)
    return line, frames // (line * pair), pair


def spread_by_permutes(outs, at, frames):
    line, side, pair = stages(frames)
    rest = side * pair

    def swap(x, key):
        return lax.ppermute(x, "frame", [(i, i ^ key) for i in range(frames)])

    lined = {0: outs[0]}
    for a in range(line - 1, 0, -1):
        lined[a] = swap(outs[a], a * rest)
    sided = {}
    for b in range(1, side):
        picks = [(a, b * pair + c) for a in range(line) for c in range(pair)]
        sided[b] = swap(collect([lined[a] for a in range(line)], picks), b * pair)
    parts = [lined[a] for a in range(line)] + [sided[b] for b in range(1, side)]
    picks = [(a, 1) for a in range(line)]
    picks += [(line + b - 1, a * pair + 1) for b in range(1, side) for a in range(line)]
    parts.append(swap(collect(parts, picks), 1))
    places = [(a * rest,) + (None,) * (rest - 1) for a in range(line)]
    places += [
        tuple(
            a * rest + b * pair if c == 0 else None for a in range(line) for c in range(pair)
        )
        for b in range(1, side)
    ]
    places.append(tuple(a * rest + b * pair + 1 for b in range(side) for a in range(line)))
    return assemble(parts, tuple(places), at)


def local(spatial_q, spatial_k, spatial_v, norm_gain, temporal_weight):
    frames = lax.axis_size("frame")
    ways = lax.axis_size("row")
    me = lax.axis_index("row").astype(jnp.int32)
    tokens = spatial_q.shape[1]
    slot = tokens // frames
    tiled = slot % 8 == 0
    width = temporal_weight.shape[2]
    group = width // HEAD
    hbm = lambda x: pltpu.with_memory_space_constraint(x, pltpu.HBM)
    weight = hbm(jnp.transpose(temporal_weight, (1, 0, 2)))
    spatial_q, spatial_k, spatial_v = (hbm(x) for x in (spatial_q, spatial_k, spatial_v))
    gain = norm_gain.reshape(1, -1)

    staged = three_chunks(group, ways, frames, slot)
    if staged:
        sizes = MIXED if group == sum(MIXED) else (group // 3, group // 3, group - 2 * (group // 3))
    else:
        first = max(1, group * 5 // 12)
        sizes = (first, group - first) if group > 1 else (1,)
    chunks = [(sum(sizes[:i]), size) for i, size in enumerate(sizes)]
    last = len(chunks) - 1
    aligned = lambda i: group % chunks[i][1] == 0 and chunks[i][0] % chunks[i][1] == 0
    behind = [lax.rem(me + ways - k, ways) * group + c for c, _ in chunks for k in range(ways)]
    ahead = [lax.rem(me + k, ways) * group + c for c, _ in chunks for k in range(ways)]
    table = jnp.stack(behind + ahead + [me, lax.axis_index("frame").astype(jnp.int32)])

    def shift(x, k):
        return lax.ppermute(x, "row", [(i, (i + k) % ways) for i in range(ways)])

    received = []
    for i, (_, size) in enumerate(chunks):
        parts = []
        for k in range(1, ways):
            index = len(behind) + i * ways + k
            packed = pack(spatial_q, spatial_k, spatial_v, table, index, size * HEAD, aligned(i))
            parts.append(shift(packed, k))
        received.append(parts)

    pieces = {}
    for i, parts in enumerate(received):
        lines = stages(frames)[0] if staged and i != 1 else 0
        out = spatial(
            spatial_q, spatial_k, spatial_v, parts, hbm(gain), table, i * ways, frames, lines
        )
        if lines:
            pieces[i, 0] = spread_by_permutes(out, table, frames)
        else:
            out = lax.all_to_all(out, "frame", split_axis=0, concat_axis=0, tiled=True)
            pieces[i, 0] = out
        for k in range(1, ways):
            pieces[i, k] = shift(pieces[i, 0], k)
    if not tiled:
        flat = lambda x: x.transpose(1, 0, 2, 3).reshape(ways, tokens, -1)
        pieces = {key: flat(x) for key, x in pieces.items()}

    others = lambda i: [[(i, k)] for k in range(1, ways)]
    if staged:
        steps = [[[(0, 0)]], [[(1, 0)]], [[(2, 0)]] + others(0) + others(1)]
    else:
        steps = [[key for i in range(last) for key in others(i)] + [[(i, 0) for i in range(last + 1)]]]
    final = [g[0] for g in others(last)]
    place = lambda key: key[0] * ways + key[1]
    shared = dict(tokens=tokens, ways=ways, tiled=tiled)
    carried, given = (), ()
    for n, wanted in enumerate(steps):
        flat = [key for g in wanted for key in g]
        later = final if n == len(steps) - 1 else steps[n + 1][0] if n == len(steps) - 2 else []
        acc, ss, *brought = project(
            tuple(tuple(flat.index(key) for key in g) for g in wanted),
            tuple(place(key) for key in [g[0] for g in wanted] + later),
            [pieces[key] for key in flat],
            tuple(k for _, k in flat),
            table,
            [chunks[i][1] * HEAD for i, _ in later],
            carried,
            given,
            weight,
            gain,
            **shared,
        )
        carried, given = (acc, ss), brought
    carried = (*carried, *given)
    arrays, shifts = [pieces[key] for key in final], tuple(k for _, k in final)
    places = tuple(place(key) for key in final)
    out = temporal(arrays, shifts, table, places, gain, carried, slot=slot, **shared)
    out = out.reshape(frames * ways, slot, width)
    out = lax.all_to_all(out, ("frame", "row"), split_axis=0, concat_axis=0, tiled=True)
    out = out.reshape(frames, ways, slot, width).transpose(0, 2, 1, 3)
    return out.reshape(1, tokens, ways * width)


MIXED = (4, 4, 4)


def three_chunks(group, ways, frames, slot):
    return group >= 3 and ways == 2 and frames & (frames - 1) == 0 and slot % 8 == 0 and frames > 2


def solution(mesh):
    return jax.shard_map(
        local,
        mesh=mesh,
        in_specs=(
            P("frame", "row", None),
            P("frame", "row", None),
            P("frame", "row", None),
            P(),
            P(None, None, "row"),
        ),
        out_specs=P("frame", "row", None),
        check_vma=False,
    )
```

```python
import math
from functools import partial

import jax
import jax.numpy as jnp
from jax import lax
from jax.experimental import pallas as pl
from jax.experimental.pallas import tpu as pltpu
from jax.sharding import PartitionSpec as P

D = 3072
HEADS = 24
AGENTS = 128
HEAD = D // HEADS
SCALE = HEAD ** (-0.5)
EXPONENT = SCALE * math.log2(math.e)

epsilon = 1e-06


def dot(left, right):
    return jnp.dot(left, right, preferred_element_type=jnp.float32)


def dot_nt(left, right):
    return lax.dot_general(
        left, right, (((1,), (1,)), ((), ())), preferred_element_type=jnp.float32
    )


VMEM = pl.BlockSpec(memory_space=pltpu.VMEM)


def weighted(scores):
    weights = jnp.exp2((scores - jnp.max(scores, axis=1, keepdims=True)) * EXPONENT)
    return weights, 1.0 / jnp.sum(weights, axis=1, keepdims=True)


def spatial_kernel(at, *refs, index, pool, tiled, lines):
    inputs, rest, (own, factor, sems) = refs[:3], refs[3:-3], refs[-3:]
    if lines:
        rest, outs, out, own = rest[: -lines - 1], rest[-lines - 1 : -1], rest[-1], own
        received, gain = rest[:-1], rest[-1]
        frame = at[at.shape[0] - 1]
    else:
        received, gain, out = rest[:-2], rest[-2], rest[-1]
    ways = len(received) + 1
    tokens, width = own.shape[1:]
    lanes = pl.ds(pl.multiple_of(at[index] * HEAD, HEAD), width)
    copies = [
        pltpu.make_async_copy(ref.at[0, :, lanes], own.at[i], sems.at[i])
        for i, ref in enumerate(inputs)
    ]
    copies.append(pltpu.make_async_copy(gain.at[:, lanes], factor, sems.at[3]))
    for copy in copies:
        copy.start()
    agent = lax.broadcasted_iota(jnp.int32, (tokens // pool, tokens), 0)
    token = lax.broadcasted_iota(jnp.int32, (tokens // pool, tokens), 1)
    member = ((token >= agent * pool) & (token < (agent + 1) * pool)).astype(jnp.bfloat16)
    for copy in copies:
        copy.wait()
    blocks = [own, *received]
    for start in range(0, width, TOGETHER * HEAD):
        stop = min(width, start + TOGETHER * HEAD)
        pooled = [dot(member, ref[0, :, start:stop]) for ref in blocks]
        pooled = (jnp.concatenate(pooled) * (1.0 / pool)).astype(jnp.bfloat16)
        split = [slice(n, n + HEAD) for n in range(start, stop, HEAD)]
        agents = [pooled[:, n.start - start : n.stop - start] for n in split]
        queries, keys, values = (
            [jnp.concatenate([ref[i, :, cols] for ref in blocks]) for cols in split]
            for i in range(3)
        )
        agent_scores = [dot_nt(a, b) for a, b in zip(agents, keys)]
        token_scores = [dot_nt(a, b) for a, b in zip(queries, agents)]
        agent_weights = [weighted(x) for x in agent_scores]
        token_weights = [weighted(x) for x in token_scores]
        agent_values = [
            (dot(w.astype(jnp.bfloat16), x) * r).astype(jnp.bfloat16)
            for (w, r), x in zip(agent_weights, values)
        ]
        results = [
            dot((w * r).astype(jnp.bfloat16), x) for (w, r), x in zip(token_weights, agent_values)
        ]
        for cols, result in zip(split, results):
            result = (result * factor[:, cols]).astype(jnp.bfloat16)
            for j in range(ways):
                block = result[j * tokens : (j + 1) * tokens]
                if lines:
                    slot = out.shape[2]
                    for f in range(out.shape[0]):
                        out[f ^ frame, j, :, cols] = block[f * slot : (f + 1) * slot]
                elif tiled:
                    out[:, j, :, cols] = block.reshape(out.shape[0], out.shape[2], HEAD)
                else:
                    out[j, :, cols] = block
    if lines:
        for n, target in enumerate(outs):
            size = target.shape[0]
            target[...] = out[n * size : (n + 1) * size]


TOGETHER = 4


def spatial(q, k, v, received, gain, at, index, frames, lines=0):
    tokens = q.shape[1]
    width = received[0].shape[2] if received else q.shape[2]
    ways = len(received) + 1
    slot = tokens // frames
    tiled = slot % 8 == 0
    shape = (frames, ways, slot, width) if tiled else (ways, tokens, width)
    hbm = pl.BlockSpec(memory_space=pl.ANY)
    out = pl.pallas_call(
        partial(
            spatial_kernel, index=index, pool=tokens * ways // AGENTS, tiled=tiled, lines=lines
        ),
        out_shape=(
            [jax.ShapeDtypeStruct((frames // lines, *shape[1:]), jnp.bfloat16)] * lines
            if lines
            else jax.ShapeDtypeStruct(shape, jnp.bfloat16)
        ),
        grid_spec=pltpu.PrefetchScalarGridSpec(
            num_scalar_prefetch=1,
            grid=(),
            in_specs=[hbm] * 3 + [VMEM] * len(received) + [hbm],
            out_specs=[VMEM] * lines if lines else VMEM,
            scratch_shapes=([pltpu.VMEM(shape, jnp.bfloat16)] if lines else [])
            + [
                pltpu.VMEM((3, tokens, width), jnp.bfloat16),
                pltpu.VMEM((1, width), jnp.float32),
                pltpu.SemaphoreType.DMA((4,)),
            ],
        ),
        cost_estimate=pl.CostEstimate(
            flops=10 * tokens * ways * AGENTS * width,
            bytes_accessed=10 * tokens * ways * width,
            transcendentals=2 * tokens * ways * width,
        ),
        compiler_params=pltpu.CompilerParams(vmem_limit_bytes=16 << 20),
        name="spatial",
    )(at, q, k, v, *received, gain)
    if not tiled and not lines:
        out = out.reshape(ways, frames, slot, width).transpose(1, 0, 2, 3)
    return out


def rows_of(ref, block, tokens, tiled):
    if tiled:
        return ref[:, block, :, :].reshape(tokens, -1)
    return ref[block]


def squares(x, inverse):
    y = x.astype(jnp.float32) * inverse
    y = y * y
    total = y[:, :HEAD]
    for at in range(HEAD, y.shape[1], HEAD):
        total = total + y[:, at : at + HEAD]
    return total


AHEAD = 4


def hold(held, xs, depths, shifts, tokens, ways, tiled):
    column = 0
    for x, depth, shift in zip(xs, depths, shifts):
        for j in range(ways):
            held[j * tokens : (j + 1) * tokens, column : column + depth] = rows_of(
                x, (j - shift) % ways, tokens, tiled
            )
        column += depth


def project_kernel(
    at, *refs, groups, places, shifts, depths, carried, given, tokens, ways, tiled
):
    xs = refs[: len(shifts)]
    weight, gain = refs[len(shifts) : len(shifts) + 2]
    refs = refs[len(shifts) + 2 :]
    before, there = refs[: 2 * carried], refs[2 * carried : 2 * carried + given]
    refs = refs[2 * carried + given :]
    acc, ss, *rest = refs
    kept = rest[: len(groups) - sum(g is not None for g in groups)]
    sems = rest[-1]
    used = [g for g in groups if g is not None]
    scratch = rest[len(kept) : -1]
    held, buffers = scratch[: len(used)], [*there, *scratch[len(used) :]]
    targets = [*buffers, *kept]
    copies = []
    for i, target in enumerate(targets):
        if i < given:
            continue
        rows = pl.ds(pl.multiple_of(at[places[i]] * HEAD, HEAD), target.shape[1])
        for c in range(3):
            copies.append(
                pltpu.make_async_copy(weight.at[c, rows, :], target.at[c], sems.at[3 * i + c])
            )
    for copy in copies[:AHEAD]:
        copy.start()
    width = weight.shape[2]
    tile = width // 3 if width % 3 == 0 else width
    total = before[1][...] if carried else None
    for i, members in enumerate(used):
        hold(
            held[i],
            [xs[m] for m in members],
            [depths[m] for m in members],
            [shifts[m] for m in members],
            tokens,
            ways,
            tiled,
        )
        lanes = pl.ds(pl.multiple_of(at[places[i]] * HEAD, HEAD), held[i].shape[1])
        part = squares(held[i][...], 1.0 / gain[:, lanes])
        total = part if total is None else total + part
        for c in range(3):
            now = 3 * (i - given) + c
            if now >= 0:
                copies[now].wait()
                if now + AHEAD < len(copies):
                    copies[now + AHEAD].start()
            for n in range(0, width, tile):
                cols = slice(n, n + tile)
                value = dot(held[i][...], buffers[i][c, :, cols])
                if i == 0:
                    acc[c, :, cols] = before[0][c, :, cols] + value if carried else value
                else:
                    acc[c, :, cols] += value
    ss[...] = total
    done = 3 * (len(used) - given)
    for n in range(done + AHEAD, len(copies)):
        copies[n].start()
    for copy in copies[done:]:
        copy.wait()


def project(
    groups, places, arrays, shifts, at, later, carried, given, weight, gain, tokens, ways, tiled
):
    rows = tokens * ways
    width = weight.shape[2]
    depths = [x.shape[-1] for x in arrays]
    sums = [sum(depths[m] for m in g) for g in groups]
    return pl.pallas_call(
        partial(
            project_kernel,
            groups=(*groups, *[None] * len(later)),
            places=places,
            shifts=shifts,
            depths=depths,
            carried=bool(carried),
            given=len(given),
            tokens=tokens,
            ways=ways,
            tiled=tiled,
        ),
        out_shape=(
            pltpu.VMEM((3, rows, width), jnp.float32),
            pltpu.VMEM((rows, HEAD), jnp.float32),
            *[pltpu.VMEM((3, depth, width), weight.dtype) for depth in later],
        ),
        grid_spec=pltpu.PrefetchScalarGridSpec(
            num_scalar_prefetch=1,
            grid=(),
            in_specs=[VMEM] * len(arrays)
            + [pl.BlockSpec(memory_space=pl.ANY)]
            + [VMEM] * (1 + len(carried) + len(given)),
            out_specs=(VMEM,) * (2 + len(later)),
            scratch_shapes=[pltpu.VMEM((rows, depth), jnp.bfloat16) for depth in sums]
            + [pltpu.VMEM((3, depth, width), weight.dtype) for depth in sums[len(given) :]]
            + [pltpu.SemaphoreType.DMA((3 * (len(sums) + len(later)),))],
        ),
        cost_estimate=pl.CostEstimate(
            flops=6 * rows * sum(sums) * width,
            bytes_accessed=6 * (sum(sums) + sum(later)) * width,
            transcendentals=0,
        ),
        input_output_aliases=(
            {len(arrays) + 3: 0, len(arrays) + 4: 1} if carried else {}
        ),
        compiler_params=pltpu.CompilerParams(vmem_limit_bytes=32 << 20),
        name="project",
    )(at, *arrays, weight, gain, *carried, *given)


def temporal_kernel(at, *refs, places, shifts, heads, tokens, ways, slot, tiled):
    count = len(shifts)
    xs = refs[:count]
    gain, acc, ss = refs[count : count + 3]
    ws = refs[count + 3 : 2 * count + 3]
    out, *held, rstd = refs[2 * count + 3 :]
    step = heads * HEAD

    @pl.when(pl.program_id(0) == 0)
    def _():
        total = ss[...]
        for i in range(count):
            depth = ws[i].shape[1]
            hold(held[i], [xs[i]], [depth], [shifts[i]], tokens, ways, tiled)
            lanes = pl.ds(pl.multiple_of(at[places[i]] * HEAD, HEAD), depth)
            total = total + squares(held[i][...], 1.0 / gain[:, lanes])
        mean = jnp.sum(total, axis=1, keepdims=True) * (1.0 / D)
        rstd[...] = jnp.broadcast_to(lax.rsqrt(mean + epsilon), rstd.shape)

    row = lax.broadcasted_iota(jnp.int32, (tokens, tokens), 0)
    col = lax.broadcasted_iota(jnp.int32, (tokens, tokens), 1)
    same = lax.rem(row, slot) == lax.rem(col, slot)
    part = pl.ds(pl.multiple_of(pl.program_id(0) * step, step), step)
    factor = jnp.concatenate([rstd[...]] * heads, axis=1)
    qkv = []
    for c in range(3):
        value = acc[c, :, part]
        for i in range(count):
            value = value + dot(held[i][...], ws[i][c, :, part])
        qkv.append((value * factor).astype(jnp.bfloat16))
    split = [
        (j, slice(j * tokens, (j + 1) * tokens), slice(h * HEAD, (h + 1) * HEAD))
        for h in range(heads)
        for j in range(ways)
    ]
    scores = [
        jnp.where(same, dot_nt(qkv[0][rows, cols], qkv[1][rows, cols]), -1e30)
        for _, rows, cols in split
    ]
    weights = [weighted(x) for x in scores]
    me = at[at.shape[0] - 2]
    for (j, rows, cols), (w, r) in zip(split, weights):
        result = dot((w * r).astype(jnp.bfloat16), qkv[2][rows, cols]).astype(jnp.bfloat16)
        target = lax.rem(me + ways - j, ways)
        if tiled:
            out[:, target, :, cols] = result.reshape(out.shape[0], slot, HEAD)
        else:
            out[target, :, cols] = result


def temporal(arrays, shifts, at, places, gain, carried, tokens, ways, slot, tiled):
    rows = tokens * ways
    width = carried[0].shape[2]
    depths = [x.shape[-1] for x in arrays]
    frames = tokens // slot
    heads = math.gcd(width // HEAD, FINAL_HEADS)
    step = heads * HEAD
    if tiled:
        shape = (frames, ways, slot, width)
        out_spec = pl.BlockSpec((frames, ways, slot, step), lambda n, at: (0, 0, 0, n))
    else:
        shape = (ways, tokens, width)
        out_spec = pl.BlockSpec((ways, tokens, step), lambda n, at: (0, 0, n))
    operands = [*arrays, gain, *carried]
    out = pl.pallas_call(
        partial(
            temporal_kernel,
            places=places,
            shifts=shifts,
            heads=heads,
            tokens=tokens,
            ways=ways,
            slot=slot,
            tiled=tiled,
        ),
        out_shape=jax.ShapeDtypeStruct(shape, jnp.bfloat16),
        grid_spec=pltpu.PrefetchScalarGridSpec(
            num_scalar_prefetch=1,
            grid=(width // step,),
            in_specs=[VMEM] * len(operands),
            out_specs=out_spec,
            scratch_shapes=[pltpu.VMEM((rows, depth), jnp.bfloat16) for depth in depths]
            + [pltpu.VMEM((rows, HEAD), jnp.float32)],
        ),
        cost_estimate=pl.CostEstimate(
            flops=6 * rows * sum(depths) * width,
            bytes_accessed=2 * rows * width,
            transcendentals=rows * width,
        ),
        compiler_params=pltpu.CompilerParams(vmem_limit_bytes=16 << 20),
        name="temporal",
    )(at, *operands)
    if not tiled:
        out = out.reshape(ways, frames, slot, width).transpose(1, 0, 2, 3)
    return out


FINAL_HEADS = 12


def pack_kernel(at, q, k, v, out, sems, *, index):
    lanes = pl.ds(pl.multiple_of(at[index] * HEAD, HEAD), out.shape[2])
    copies = [
        pltpu.make_async_copy(ref.at[0, :, lanes], out.at[i], sems.at[i])
        for i, ref in enumerate((q, k, v))
    ]
    for copy in copies:
        copy.start()
    for copy in copies:
        copy.wait()


def pack_blocks_kernel(at, q, k, v, out):
    for i, ref in enumerate((q, k, v)):
        out[i] = ref[0]


def pack(q, k, v, at, index, width, aligned):
    if aligned:
        blocks = width // HEAD
        return pl.pallas_call(
            pack_blocks_kernel,
            out_shape=jax.ShapeDtypeStruct((3, q.shape[1], width), q.dtype),
            grid_spec=pltpu.PrefetchScalarGridSpec(
                num_scalar_prefetch=1,
                grid=(1,),
                in_specs=[
                    pl.BlockSpec(
                        (1, q.shape[1], width), lambda i, at: (0, 0, at[index] // blocks)
                    )
                ]
                * 3,
                out_specs=pl.BlockSpec((3, q.shape[1], width), lambda i, at: (0, 0, 0)),
            ),
            compiler_params=pltpu.CompilerParams(vmem_limit_bytes=8 << 20),
            name="pack",
        )(at, q, k, v)
    return pl.pallas_call(
        partial(pack_kernel, index=index),
        out_shape=pltpu.VMEM((3, q.shape[1], width), q.dtype),
        grid_spec=pltpu.PrefetchScalarGridSpec(
            num_scalar_prefetch=1,
            grid=(),
            in_specs=[pl.BlockSpec(memory_space=pl.ANY)] * 3,
            out_specs=VMEM,
            scratch_shapes=[pltpu.SemaphoreType.DMA((3,))],
        ),
        compiler_params=pltpu.CompilerParams(vmem_limit_bytes=8 << 20),
        name="pack",
    )(at, q, k, v)


def collect_kernel(*refs, picks):
    out = refs[-1]
    for n, (which, block) in enumerate(picks):
        out[n] = refs[which][block]


def collect(parts, picks):
    return pl.pallas_call(
        partial(collect_kernel, picks=tuple(picks)),
        out_shape=jax.ShapeDtypeStruct((len(picks), *parts[0].shape[1:]), parts[0].dtype),
        in_specs=[VMEM] * len(parts),
        out_specs=VMEM,
        compiler_params=pltpu.CompilerParams(vmem_limit_bytes=8 << 20),
        name="collect",
    )(*parts)


def assemble_kernel(at, *refs, places):
    out = refs[-1]
    frame = at[at.shape[0] - 1]
    for ref, keys in zip(refs[:-1], places):
        for n, key in enumerate(keys):
            if key is not None:
                out[key ^ frame] = ref[n]


def assemble(parts, places, at):
    count = sum(key is not None for keys in places for key in keys)
    return pl.pallas_call(
        partial(assemble_kernel, places=places),
        out_shape=jax.ShapeDtypeStruct((count, *parts[0].shape[1:]), parts[0].dtype),
        grid_spec=pltpu.PrefetchScalarGridSpec(
            num_scalar_prefetch=1,
            grid=(),
            in_specs=[VMEM] * len(parts),
            out_specs=VMEM,
        ),
        compiler_params=pltpu.CompilerParams(vmem_limit_bytes=8 << 20),
        name="assemble",
    )(at, *parts)


def stages(frames):
    pair = 2
    line = min(4, frames // pair)
    return line, frames // (line * pair), pair


def spread_by_permutes(outs, at, frames):
    line, side, pair = stages(frames)
    rest = side * pair

    def swap(x, key):
        return lax.ppermute(x, "frame", [(i, i ^ key) for i in range(frames)])

    lined = {0: outs[0]}
    for a in range(line - 1, 0, -1):
        lined[a] = swap(outs[a], a * rest)
    sided = {}
    for b in range(1, side):
        picks = [(a, b * pair + c) for a in range(line) for c in range(pair)]
        sided[b] = swap(collect([lined[a] for a in range(line)], picks), b * pair)
    parts = [lined[a] for a in range(line)] + [sided[b] for b in range(1, side)]
    picks = [(a, 1) for a in range(line)]
    picks += [(line + b - 1, a * pair + 1) for b in range(1, side) for a in range(line)]
    parts.append(swap(collect(parts, picks), 1))
    places = [(a * rest,) + (None,) * (rest - 1) for a in range(line)]
    places += [
        tuple(
            a * rest + b * pair if c == 0 else None for a in range(line) for c in range(pair)
        )
        for b in range(1, side)
    ]
    places.append(tuple(a * rest + b * pair + 1 for b in range(side) for a in range(line)))
    return assemble(parts, tuple(places), at)


def local(spatial_q, spatial_k, spatial_v, norm_gain, temporal_weight):
    frames = lax.axis_size("frame")
    ways = lax.axis_size("row")
    me = lax.axis_index("row").astype(jnp.int32)
    tokens = spatial_q.shape[1]
    slot = tokens // frames
    tiled = slot % 8 == 0
    width = temporal_weight.shape[2]
    group = width // HEAD
    hbm = lambda x: pltpu.with_memory_space_constraint(x, pltpu.HBM)
    weight = hbm(jnp.transpose(temporal_weight, (1, 0, 2)))
    spatial_q, spatial_k, spatial_v = (hbm(x) for x in (spatial_q, spatial_k, spatial_v))
    gain = norm_gain.reshape(1, -1)

    staged = three_chunks(group, ways, frames, slot)
    if staged:
        sizes = MIXED if group == sum(MIXED) else (group // 3, group // 3, group - 2 * (group // 3))
    else:
        first = max(1, group * 5 // 12)
        sizes = (first, group - first) if group > 1 else (1,)
    chunks = [(sum(sizes[:i]), size) for i, size in enumerate(sizes)]
    last = len(chunks) - 1
    aligned = lambda i: group % chunks[i][1] == 0 and chunks[i][0] % chunks[i][1] == 0
    behind = [lax.rem(me + ways - k, ways) * group + c for c, _ in chunks for k in range(ways)]
    ahead = [lax.rem(me + k, ways) * group + c for c, _ in chunks for k in range(ways)]
    table = jnp.stack(behind + [me, lax.axis_index("frame").astype(jnp.int32)])

    def shift(x, k):
        return lax.ppermute(x, "row", [(i, (i + k) % ways) for i in range(ways)])

    received = []
    for i, (_, size) in enumerate(chunks):
        parts = []
        for k in range(1, ways):
            at = ahead[i * ways + k].reshape(1)
            packed = pack(spatial_q, spatial_k, spatial_v, at, 0, size * HEAD, aligned(i))
            parts.append(shift(packed, k))
        received.append(parts)

    pieces = {}
    for i, parts in enumerate(received):
        lines = stages(frames)[0] if staged and i != 1 else 0
        out = spatial(
            spatial_q, spatial_k, spatial_v, parts, hbm(gain), table, i * ways, frames, lines
        )
        if lines:
            pieces[i, 0] = spread_by_permutes(out, table, frames)
        else:
            out = lax.all_to_all(out, "frame", split_axis=0, concat_axis=0, tiled=True)
            pieces[i, 0] = out
        for k in range(1, ways):
            pieces[i, k] = shift(pieces[i, 0], k)
    if not tiled:
        flat = lambda x: x.transpose(1, 0, 2, 3).reshape(ways, tokens, -1)
        pieces = {key: flat(x) for key, x in pieces.items()}

    others = lambda i: [[(i, k)] for k in range(1, ways)]
    if staged:
        steps = [[[(0, 0)]], [[(1, 0)]], [[(2, 0)]] + others(0) + others(1)]
    else:
        steps = [[key for i in range(last) for key in others(i)] + [[(i, 0) for i in range(last + 1)]]]
    final = [g[0] for g in others(last)]
    place = lambda key: key[0] * ways + key[1]
    shared = dict(tokens=tokens, ways=ways, tiled=tiled)
    carried, given = (), ()
    for n, wanted in enumerate(steps):
        flat = [key for g in wanted for key in g]
        later = final if n == len(steps) - 1 else steps[n + 1][0] if n == len(steps) - 2 else []
        acc, ss, *brought = project(
            tuple(tuple(flat.index(key) for key in g) for g in wanted),
            tuple(place(key) for key in [g[0] for g in wanted] + later),
            [pieces[key] for key in flat],
            tuple(k for _, k in flat),
            table,
            [chunks[i][1] * HEAD for i, _ in later],
            carried,
            given,
            weight,
            gain,
            **shared,
        )
        carried, given = (acc, ss), brought
    carried = (*carried, *given)
    arrays, shifts = [pieces[key] for key in final], tuple(k for _, k in final)
    places = tuple(place(key) for key in final)
    out = temporal(arrays, shifts, table, places, gain, carried, slot=slot, **shared)
    out = out.reshape(frames * ways, slot, width)
    out = lax.all_to_all(out, ("frame", "row"), split_axis=0, concat_axis=0, tiled=True)
    out = out.reshape(frames, ways, slot, width).transpose(0, 2, 1, 3)
    return out.reshape(1, tokens, ways * width)


MIXED = (4, 4, 4)


def three_chunks(group, ways, frames, slot):
    return group >= 3 and ways == 2 and frames & (frames - 1) == 0 and slot % 8 == 0 and frames > 2


def solution(mesh):
    return jax.shard_map(
        local,
        mesh=mesh,
        in_specs=(
            P("frame", "row", None),
            P("frame", "row", None),
            P("frame", "row", None),
            P(),
            P(None, None, "row"),
        ),
        out_specs=P("frame", "row", None),
        check_vma=False,
    )
```

```python
import math
from functools import partial

import jax
import jax.numpy as jnp
from jax import lax
from jax.experimental import pallas as pl
from jax.experimental.pallas import tpu as pltpu
from jax.sharding import PartitionSpec as P

D = 3072
HEADS = 24
AGENTS = 128
HEAD = D // HEADS
SCALE = HEAD ** (-0.5)
EXPONENT = SCALE * math.log2(math.e)

epsilon = 1e-06


def dot(left, right):
    return jnp.dot(left, right, preferred_element_type=jnp.float32)


def dot_nt(left, right):
    return lax.dot_general(
        left, right, (((1,), (1,)), ((), ())), preferred_element_type=jnp.float32
    )


VMEM = pl.BlockSpec(memory_space=pltpu.VMEM)


def with_scalars(kernel, count):
    return lambda *refs: kernel([ref[0] for ref in refs[:count]], *refs[count:])


def weighted(scores):
    weights = jnp.exp2((scores - jnp.max(scores, axis=1, keepdims=True)) * EXPONENT)
    return weights, 1.0 / jnp.sum(weights, axis=1, keepdims=True)


def spatial_kernel(at, *refs, pool, tiled, lines):
    inputs, rest, (own, factor, sems) = refs[:3], refs[3:-3], refs[-3:]
    if lines:
        rest, outs, out, own = rest[: -lines - 1], rest[-lines - 1 : -1], rest[-1], own
        received, gain = rest[:-1], rest[-1]
        frame = at[1]
    else:
        received, gain, out = rest[:-2], rest[-2], rest[-1]
    ways = len(received) + 1
    tokens, width = own.shape[1:]
    lanes = pl.ds(pl.multiple_of(at[0] * HEAD, HEAD), width)
    copies = [
        pltpu.make_async_copy(ref.at[0, :, lanes], own.at[i], sems.at[i])
        for i, ref in enumerate(inputs)
    ]
    copies.append(pltpu.make_async_copy(gain.at[:, lanes], factor, sems.at[3]))
    for copy in copies:
        copy.start()
    agent = lax.broadcasted_iota(jnp.int32, (tokens // pool, tokens), 0)
    token = lax.broadcasted_iota(jnp.int32, (tokens // pool, tokens), 1)
    member = ((token >= agent * pool) & (token < (agent + 1) * pool)).astype(jnp.bfloat16)
    for copy in copies:
        copy.wait()
    blocks = [own, *received]
    for start in range(0, width, TOGETHER * HEAD):
        stop = min(width, start + TOGETHER * HEAD)
        pooled = [dot(member, ref[0, :, start:stop]) for ref in blocks]
        pooled = (jnp.concatenate(pooled) * (1.0 / pool)).astype(jnp.bfloat16)
        split = [slice(n, n + HEAD) for n in range(start, stop, HEAD)]
        agents = [pooled[:, n.start - start : n.stop - start] for n in split]
        queries, keys, values = (
            [jnp.concatenate([ref[i, :, cols] for ref in blocks]) for cols in split]
            for i in range(3)
        )
        agent_scores = [dot_nt(a, b) for a, b in zip(agents, keys)]
        token_scores = [dot_nt(a, b) for a, b in zip(queries, agents)]
        agent_weights = [weighted(x) for x in agent_scores]
        token_weights = [weighted(x) for x in token_scores]
        agent_values = [
            (dot(w.astype(jnp.bfloat16), x) * r).astype(jnp.bfloat16)
            for (w, r), x in zip(agent_weights, values)
        ]
        results = [
            dot((w * r).astype(jnp.bfloat16), x) for (w, r), x in zip(token_weights, agent_values)
        ]
        for cols, result in zip(split, results):
            result = (result * factor[:, cols]).astype(jnp.bfloat16)
            for j in range(ways):
                block = result[j * tokens : (j + 1) * tokens]
                if lines:
                    slot = out.shape[2]
                    for f in range(out.shape[0]):
                        out[f ^ frame, j, :, cols] = block[f * slot : (f + 1) * slot]
                elif tiled:
                    out[:, j, :, cols] = block.reshape(out.shape[0], out.shape[2], HEAD)
                else:
                    out[j, :, cols] = block
    if lines:
        for n, target in enumerate(outs):
            size = target.shape[0]
            target[...] = out[n * size : (n + 1) * size]


TOGETHER = 4


def spatial(q, k, v, received, gain, at, frames, lines=0):
    tokens = q.shape[1]
    width = received[0].shape[2] if received else q.shape[2]
    ways = len(received) + 1
    slot = tokens // frames
    tiled = slot % 8 == 0
    shape = (frames, ways, slot, width) if tiled else (ways, tokens, width)
    hbm = pl.BlockSpec(memory_space=pl.ANY)
    out = pl.pallas_call(
        with_scalars(
            partial(spatial_kernel, pool=tokens * ways // AGENTS, tiled=tiled, lines=lines), len(at)
        ),
        out_shape=(
            [jax.ShapeDtypeStruct((frames // lines, *shape[1:]), jnp.bfloat16)] * lines
            if lines
            else jax.ShapeDtypeStruct(shape, jnp.bfloat16)
        ),
        grid_spec=pltpu.PrefetchScalarGridSpec(
            num_scalar_prefetch=len(at),
            grid=(),
            in_specs=[hbm] * 3 + [VMEM] * len(received) + [hbm],
            out_specs=[VMEM] * lines if lines else VMEM,
            scratch_shapes=([pltpu.VMEM(shape, jnp.bfloat16)] if lines else [])
            + [
                pltpu.VMEM((3, tokens, width), jnp.bfloat16),
                pltpu.VMEM((1, width), jnp.float32),
                pltpu.SemaphoreType.DMA((4,)),
            ],
        ),
        cost_estimate=pl.CostEstimate(
            flops=10 * tokens * ways * AGENTS * width,
            bytes_accessed=10 * tokens * ways * width,
            transcendentals=2 * tokens * ways * width,
        ),
        compiler_params=pltpu.CompilerParams(vmem_limit_bytes=16 << 20),
        name="spatial",
    )(*at, q, k, v, *received, gain)
    if not tiled and not lines:
        out = out.reshape(ways, frames, slot, width).transpose(1, 0, 2, 3)
    return out


def rows_of(ref, block, tokens, tiled):
    if tiled:
        return ref[:, block, :, :].reshape(tokens, -1)
    return ref[block]


def squares(x, inverse):
    y = x.astype(jnp.float32) * inverse
    y = y * y
    total = y[:, :HEAD]
    for at in range(HEAD, y.shape[1], HEAD):
        total = total + y[:, at : at + HEAD]
    return total


AHEAD = 9


def hold(held, xs, depths, shifts, tokens, ways, tiled):
    column = 0
    for x, depth, shift in zip(xs, depths, shifts):
        for j in range(ways):
            held[j * tokens : (j + 1) * tokens, column : column + depth] = rows_of(
                x, (j - shift) % ways, tokens, tiled
            )
        column += depth


def project_kernel(
    at, *refs, groups, shifts, depths, carried, given, tokens, ways, tiled
):
    xs = refs[: len(shifts)]
    weight, gain = refs[len(shifts) : len(shifts) + 2]
    refs = refs[len(shifts) + 2 :]
    before, there = refs[: 2 * carried], refs[2 * carried : 2 * carried + given]
    refs = refs[2 * carried + given :]
    acc, ss, *rest = refs
    kept = rest[: len(groups) - sum(g is not None for g in groups)]
    sems = rest[-1]
    used = [g for g in groups if g is not None]
    scratch = rest[len(kept) : -1]
    held, buffers = scratch[: len(used)], [*there, *scratch[len(used) :]]
    targets = [*buffers, *kept]
    copies = []
    for i, target in enumerate(targets):
        if i < given:
            continue
        rows = pl.ds(pl.multiple_of(at[i] * HEAD, HEAD), target.shape[1])
        for c in range(3):
            copies.append(
                pltpu.make_async_copy(weight.at[c, rows, :], target.at[c], sems.at[3 * i + c])
            )
    for copy in copies[:AHEAD]:
        copy.start()
    width = weight.shape[2]
    tile = width // 3 if width % 3 == 0 else width
    total = before[1][...] if carried else None
    for i, members in enumerate(used):
        hold(
            held[i],
            [xs[m] for m in members],
            [depths[m] for m in members],
            [shifts[m] for m in members],
            tokens,
            ways,
            tiled,
        )
        lanes = pl.ds(pl.multiple_of(at[i] * HEAD, HEAD), held[i].shape[1])
        part = squares(held[i][...], 1.0 / gain[:, lanes])
        total = part if total is None else total + part
        for c in range(3):
            now = 3 * (i - given) + c
            if now >= 0:
                copies[now].wait()
                if now + AHEAD < len(copies):
                    copies[now + AHEAD].start()
            for n in range(0, width, tile):
                cols = slice(n, n + tile)
                value = dot(held[i][...], buffers[i][c, :, cols])
                if i == 0:
                    acc[c, :, cols] = before[0][c, :, cols] + value if carried else value
                else:
                    acc[c, :, cols] += value
    ss[...] = total
    done = 3 * (len(used) - given)
    for n in range(done + AHEAD, len(copies)):
        copies[n].start()
    for copy in copies[done:]:
        copy.wait()


def project(
    groups, arrays, shifts, at, later, carried, given, weight, gain, tokens, ways, tiled
):
    rows = tokens * ways
    width = weight.shape[2]
    depths = [x.shape[-1] for x in arrays]
    sums = [sum(depths[m] for m in g) for g in groups]
    return pl.pallas_call(
        with_scalars(
            partial(
            project_kernel,
            groups=(*groups, *[None] * len(later)),
            shifts=shifts,
            depths=depths,
            carried=bool(carried),
            given=len(given),
            tokens=tokens,
            ways=ways,
            tiled=tiled,
            ),
            len(at),
        ),
        out_shape=(
            pltpu.VMEM((3, rows, width), jnp.float32),
            pltpu.VMEM((rows, HEAD), jnp.float32),
            *[pltpu.VMEM((3, depth, width), weight.dtype) for depth in later],
        ),
        grid_spec=pltpu.PrefetchScalarGridSpec(
            num_scalar_prefetch=len(at),
            grid=(),
            in_specs=[VMEM] * len(arrays)
            + [pl.BlockSpec(memory_space=pl.ANY)]
            + [VMEM] * (1 + len(carried) + len(given)),
            out_specs=(VMEM,) * (2 + len(later)),
            scratch_shapes=[pltpu.VMEM((rows, depth), jnp.bfloat16) for depth in sums]
            + [pltpu.VMEM((3, depth, width), weight.dtype) for depth in sums[len(given) :]]
            + [pltpu.SemaphoreType.DMA((3 * (len(sums) + len(later)),))],
        ),
        cost_estimate=pl.CostEstimate(
            flops=6 * rows * sum(sums) * width,
            bytes_accessed=6 * (sum(sums) + sum(later)) * width,
            transcendentals=0,
        ),
        input_output_aliases=(
            {len(at) + len(arrays) + 2: 0, len(at) + len(arrays) + 3: 1} if carried else {}
        ),
        compiler_params=pltpu.CompilerParams(vmem_limit_bytes=32 << 20),
        name="project",
    )(*at, *arrays, weight, gain, *carried, *given)


def temporal_kernel(at, *refs, shifts, heads, tokens, ways, slot, tiled):
    count = len(shifts)
    xs = refs[:count]
    gain, acc, ss = refs[count : count + 3]
    ws = refs[count + 3 : 2 * count + 3]
    out, *held, rstd = refs[2 * count + 3 :]
    step = heads * HEAD

    @pl.when(pl.program_id(0) == 0)
    def _():
        total = ss[...]
        for i in range(count):
            depth = ws[i].shape[1]
            hold(held[i], [xs[i]], [depth], [shifts[i]], tokens, ways, tiled)
            lanes = pl.ds(pl.multiple_of(at[i] * HEAD, HEAD), depth)
            total = total + squares(held[i][...], 1.0 / gain[:, lanes])
        mean = jnp.sum(total, axis=1, keepdims=True) * (1.0 / D)
        rstd[...] = jnp.broadcast_to(lax.rsqrt(mean + epsilon), rstd.shape)

    row = lax.broadcasted_iota(jnp.int32, (tokens, tokens), 0)
    col = lax.broadcasted_iota(jnp.int32, (tokens, tokens), 1)
    same = lax.rem(row, slot) == lax.rem(col, slot)
    part = pl.ds(pl.multiple_of(pl.program_id(0) * step, step), step)
    factor = jnp.concatenate([rstd[...]] * heads, axis=1)
    qkv = []
    for c in range(3):
        value = acc[c, :, part]
        for i in range(count):
            value = value + dot(held[i][...], ws[i][c, :, part])
        qkv.append((value * factor).astype(jnp.bfloat16))
    split = [
        (j, slice(j * tokens, (j + 1) * tokens), slice(h * HEAD, (h + 1) * HEAD))
        for h in range(heads)
        for j in range(ways)
    ]
    scores = [
        jnp.where(same, dot_nt(qkv[0][rows, cols], qkv[1][rows, cols]), -1e30)
        for _, rows, cols in split
    ]
    weights = [weighted(x) for x in scores]
    me = at[count]
    for (j, rows, cols), (w, r) in zip(split, weights):
        result = dot((w * r).astype(jnp.bfloat16), qkv[2][rows, cols]).astype(jnp.bfloat16)
        target = lax.rem(me + ways - j, ways)
        if tiled:
            out[:, target, :, cols] = result.reshape(out.shape[0], slot, HEAD)
        else:
            out[target, :, cols] = result


def temporal(arrays, shifts, at, gain, carried, tokens, ways, slot, tiled):
    rows = tokens * ways
    width = carried[0].shape[2]
    depths = [x.shape[-1] for x in arrays]
    frames = tokens // slot
    heads = math.gcd(width // HEAD, FINAL_HEADS)
    step = heads * HEAD
    if tiled:
        shape = (frames, ways, slot, width)
        out_spec = pl.BlockSpec((frames, ways, slot, step), lambda n, *at: (0, 0, 0, n))
    else:
        shape = (ways, tokens, width)
        out_spec = pl.BlockSpec((ways, tokens, step), lambda n, *at: (0, 0, n))
    operands = [*arrays, gain, *carried]
    out = pl.pallas_call(
        with_scalars(
            partial(
            temporal_kernel,
            shifts=shifts,
            heads=heads,
            tokens=tokens,
            ways=ways,
            slot=slot,
            tiled=tiled,
            ),
            len(at),
        ),
        out_shape=jax.ShapeDtypeStruct(shape, jnp.bfloat16),
        grid_spec=pltpu.PrefetchScalarGridSpec(
            num_scalar_prefetch=len(at),
            grid=(width // step,),
            in_specs=[VMEM] * len(operands),
            out_specs=out_spec,
            scratch_shapes=[pltpu.VMEM((rows, depth), jnp.bfloat16) for depth in depths]
            + [pltpu.VMEM((rows, HEAD), jnp.float32)],
        ),
        cost_estimate=pl.CostEstimate(
            flops=6 * rows * sum(depths) * width,
            bytes_accessed=2 * rows * width,
            transcendentals=rows * width,
        ),
        compiler_params=pltpu.CompilerParams(vmem_limit_bytes=16 << 20),
        name="temporal",
    )(*at, *operands)
    if not tiled:
        out = out.reshape(ways, frames, slot, width).transpose(1, 0, 2, 3)
    return out


FINAL_HEADS = 12


def pack_kernel(at, q, k, v, out, sems, *, index):
    lanes = pl.ds(pl.multiple_of(at[index] * HEAD, HEAD), out.shape[2])
    copies = [
        pltpu.make_async_copy(ref.at[0, :, lanes], out.at[i], sems.at[i])
        for i, ref in enumerate((q, k, v))
    ]
    for copy in copies:
        copy.start()
    for copy in copies:
        copy.wait()


def pack_blocks_kernel(at, q, k, v, out):
    for i, ref in enumerate((q, k, v)):
        out[i] = ref[0]


def pack(q, k, v, at, index, width, aligned):
    if aligned:
        blocks = width // HEAD
        return pl.pallas_call(
            pack_blocks_kernel,
            out_shape=jax.ShapeDtypeStruct((3, q.shape[1], width), q.dtype),
            grid_spec=pltpu.PrefetchScalarGridSpec(
                num_scalar_prefetch=1,
                grid=(1,),
                in_specs=[
                    pl.BlockSpec(
                        (1, q.shape[1], width), lambda i, at: (0, 0, at[index] // blocks)
                    )
                ]
                * 3,
                out_specs=pl.BlockSpec((3, q.shape[1], width), lambda i, at: (0, 0, 0)),
            ),
            compiler_params=pltpu.CompilerParams(vmem_limit_bytes=8 << 20),
            name="pack",
        )(at, q, k, v)
    return pl.pallas_call(
        partial(pack_kernel, index=index),
        out_shape=pltpu.VMEM((3, q.shape[1], width), q.dtype),
        grid_spec=pltpu.PrefetchScalarGridSpec(
            num_scalar_prefetch=1,
            grid=(),
            in_specs=[pl.BlockSpec(memory_space=pl.ANY)] * 3,
            out_specs=VMEM,
            scratch_shapes=[pltpu.SemaphoreType.DMA((3,))],
        ),
        compiler_params=pltpu.CompilerParams(vmem_limit_bytes=8 << 20),
        name="pack",
    )(at, q, k, v)


def collect_kernel(*refs, picks):
    out = refs[-1]
    for n, (which, block) in enumerate(picks):
        out[n] = refs[which][block]


def collect(parts, picks):
    return pl.pallas_call(
        partial(collect_kernel, picks=tuple(picks)),
        out_shape=jax.ShapeDtypeStruct((len(picks), *parts[0].shape[1:]), parts[0].dtype),
        in_specs=[VMEM] * len(parts),
        out_specs=VMEM,
        compiler_params=pltpu.CompilerParams(vmem_limit_bytes=8 << 20),
        name="collect",
    )(*parts)


def assemble_kernel(at, *refs, places):
    out = refs[-1]
    frame = at[0]
    for ref, keys in zip(refs[:-1], places):
        for n, key in enumerate(keys):
            if key is not None:
                out[key ^ frame] = ref[n]


def assemble(parts, places, at):
    count = sum(key is not None for keys in places for key in keys)
    return pl.pallas_call(
        partial(assemble_kernel, places=places),
        out_shape=jax.ShapeDtypeStruct((count, *parts[0].shape[1:]), parts[0].dtype),
        grid_spec=pltpu.PrefetchScalarGridSpec(
            num_scalar_prefetch=1,
            grid=(),
            in_specs=[VMEM] * len(parts),
            out_specs=VMEM,
        ),
        compiler_params=pltpu.CompilerParams(vmem_limit_bytes=8 << 20),
        name="assemble",
    )(at, *parts)


def stages(frames):
    pair = 2
    line = min(4, frames // pair)
    return line, frames // (line * pair), pair


def spread_by_permutes(outs, at, frames):
    line, side, pair = stages(frames)
    rest = side * pair

    def swap(x, key):
        return lax.ppermute(x, "frame", [(i, i ^ key) for i in range(frames)])

    lined = {0: outs[0]}
    for a in range(line - 1, 0, -1):
        lined[a] = swap(outs[a], a * rest)
    sided = {}
    for b in range(1, side):
        picks = [(a, b * pair + c) for a in range(line) for c in range(pair)]
        sided[b] = swap(collect([lined[a] for a in range(line)], picks), b * pair)
    parts = [lined[a] for a in range(line)] + [sided[b] for b in range(1, side)]
    picks = [(a, 1) for a in range(line)]
    picks += [(line + b - 1, a * pair + 1) for b in range(1, side) for a in range(line)]
    parts.append(swap(collect(parts, picks), 1))
    places = [(a * rest,) + (None,) * (rest - 1) for a in range(line)]
    places += [
        tuple(
            a * rest + b * pair if c == 0 else None for a in range(line) for c in range(pair)
        )
        for b in range(1, side)
    ]
    places.append(tuple(a * rest + b * pair + 1 for b in range(side) for a in range(line)))
    return assemble(parts, tuple(places), at)


def local(spatial_q, spatial_k, spatial_v, norm_gain, temporal_weight):
    frames = lax.axis_size("frame")
    ways = lax.axis_size("row")
    me = lax.axis_index("row").astype(jnp.int32)
    tokens = spatial_q.shape[1]
    slot = tokens // frames
    tiled = slot % 8 == 0
    width = temporal_weight.shape[2]
    group = width // HEAD
    hbm = lambda x: pltpu.with_memory_space_constraint(x, pltpu.HBM)
    weight = hbm(jnp.transpose(temporal_weight, (1, 0, 2)))
    spatial_q, spatial_k, spatial_v = (hbm(x) for x in (spatial_q, spatial_k, spatial_v))
    gain = norm_gain.reshape(1, -1)

    staged = three_chunks(group, ways, frames, slot)
    if staged:
        sizes = MIXED if group == sum(MIXED) else (group // 3, group // 3, group - 2 * (group // 3))
    else:
        first = max(1, group * 5 // 12)
        sizes = (first, group - first) if group > 1 else (1,)
    chunks = [(sum(sizes[:i]), size) for i, size in enumerate(sizes)]
    last = len(chunks) - 1
    aligned = lambda i: group % chunks[i][1] == 0 and chunks[i][0] % chunks[i][1] == 0
    behind = [lax.rem(me + ways - k, ways) * group + c for c, _ in chunks for k in range(ways)]
    ahead = [lax.rem(me + k, ways) * group + c for c, _ in chunks for k in range(ways)]
    frame = lax.axis_index("frame").astype(jnp.int32).reshape(1)
    scalar = lambda key: behind[key[0] * ways + key[1]].reshape(1)

    def shift(x, k):
        return lax.ppermute(x, "row", [(i, (i + k) % ways) for i in range(ways)])

    received = []
    for i, (_, size) in enumerate(chunks):
        parts = []
        for k in range(1, ways):
            at = ahead[i * ways + k].reshape(1)
            packed = pack(spatial_q, spatial_k, spatial_v, at, 0, size * HEAD, aligned(i))
            parts.append(shift(packed, k))
        received.append(parts)

    pieces = {}
    for i, parts in enumerate(received):
        lines = stages(frames)[0] if staged and i != 1 else 0
        out = spatial(
            spatial_q,
            spatial_k,
            spatial_v,
            parts,
            hbm(gain),
            (scalar((i, 0)), frame),
            frames,
            lines,
        )
        if lines:
            pieces[i, 0] = spread_by_permutes(out, frame, frames)
        else:
            out = lax.all_to_all(out, "frame", split_axis=0, concat_axis=0, tiled=True)
            pieces[i, 0] = out
        for k in range(1, ways):
            pieces[i, k] = shift(pieces[i, 0], k)
    if not tiled:
        flat = lambda x: x.transpose(1, 0, 2, 3).reshape(ways, tokens, -1)
        pieces = {key: flat(x) for key, x in pieces.items()}

    others = lambda i: [[(i, k)] for k in range(1, ways)]
    if staged:
        steps = [[[(0, 0)]], [[(1, 0)]], [[(2, 0)]] + others(0) + others(1)]
    else:
        steps = [[key for i in range(last) for key in others(i)] + [[(i, 0) for i in range(last + 1)]]]
    final = [g[0] for g in others(last)]
    shared = dict(tokens=tokens, ways=ways, tiled=tiled)
    carried, given = (), ()
    for n, wanted in enumerate(steps):
        flat = [key for g in wanted for key in g]
        later = final if n == len(steps) - 1 else steps[n + 1][0] if n == len(steps) - 2 else []
        acc, ss, *brought = project(
            tuple(tuple(flat.index(key) for key in g) for g in wanted),
            [pieces[key] for key in flat],
            tuple(k for _, k in flat),
            tuple(scalar(key) for key in [g[0] for g in wanted] + later),
            [chunks[i][1] * HEAD for i, _ in later],
            carried,
            given,
            weight,
            gain,
            **shared,
        )
        carried, given = (acc, ss), brought
    carried = (*carried, *given)
    arrays, shifts = [pieces[key] for key in final], tuple(k for _, k in final)
    at = (*[scalar(key) for key in final], me.reshape(1))
    out = temporal(arrays, shifts, at, gain, carried, slot=slot, **shared)
    out = out.reshape(frames * ways, slot, width)
    out = lax.all_to_all(out, ("frame", "row"), split_axis=0, concat_axis=0, tiled=True)
    out = out.reshape(frames, ways, slot, width).transpose(0, 2, 1, 3)
    return out.reshape(1, tokens, ways * width)


MIXED = (4, 4, 4)


def three_chunks(group, ways, frames, slot):
    return group >= 3 and ways == 2 and frames & (frames - 1) == 0 and slot % 8 == 0 and frames > 2


def solution(mesh):
    return jax.shard_map(
        local,
        mesh=mesh,
        in_specs=(
            P("frame", "row", None),
            P("frame", "row", None),
            P("frame", "row", None),
            P(),
            P(None, None, "row"),
        ),
        out_specs=P("frame", "row", None),
        check_vma=False,
    )
```
